512 devices in a mesh: leaf: 32 (over y, x), col: 16 (over z, core).
Axes of the slice: x: 4, y: 8, z: 8, core: 2. Of those that a mesh axis runs over, the one named last changes fastest.
Arguments:
- points: float32 [3, 262144], P(None, ('leaf', 'col'))
- point_ids: int32 [262144], P(('leaf', 'col')), may hold values from 0 to 1048575, as said below
- signs: int32 [262144], P(('leaf', 'col')), may hold values from 0 to 1
- hadamard_sample_rows: int32 [512], replicated, may hold values from 0 to 1048575, as said below
- samples: bfloat16 [262144, 512], P(('leaf', 'col')), may hold values from -6 to 6
- skeleton: int32 [60, 128], replicated, may hold values from 0 to 8191, as said below
- ranks: int32 [60], replicated, may hold values from 64 to 128, as said below
Outputs:
- leaf_basis: bfloat16 [262144, 128], P(('leaf', 'col'))
- top_sample: float32 [512, 512], P('leaf', 'col')
- top_omega: float32 [512, 512], P('leaf', 'col')
The draws below stay inside these ranges and needn't reach their ends.
Inputs may be any that keep to these rules, and one draw needn't show every extreme that they name: `point_ids`: increasing and distinct; the first is 0 and the last 1048575. `hadamard_sample_rows`: increasing and distinct; the first is 0 and the last 1048575. `skeleton`: each row holds distinct indices; in the first 32 rows (leaves) they are below 8192, in the others below 256; entry i of a leaf row lies in [i * 64, (i + 1) * 64). `ranks`: some node has rank 128 and some other node rank 128 / 2.
All inputs are finite; a program needn't handle non-finite values.
Results may differ from the reference program's by a relative error of at most 0.0018.
Values sent between devices are 32-bit elements; how exact they have to be, the bound alone decides.
A program may use at most 64 MiB of HBM per device.

```python
import jax
import jax.numpy as jnp
from jax import lax

S = 512
R = 128
NTOTAL = 1048576
CLUSTER = 8192
NPTS = 262144
NODES = 60
NTOP = 4
N_LEAF = 32


def draw_points(key, part):
    cluster_of = jnp.arange(NPTS, dtype=jnp.int32) // CLUSTER
    centre = jnp.stack([cluster_of % 4, cluster_of // 4 % 4, cluster_of // 16]).astype(jnp.float32)
    jitter = jax.random.uniform(key, (3, NPTS), jnp.float32)
    return centre + jitter


def draw_point_ids(key, part):
    stride = NTOTAL // NPTS
    numbers = jnp.arange(NPTS, dtype=jnp.int32) * stride + jax.random.randint(key, (NPTS,), 0, stride, dtype=jnp.int32)
    return numbers.at[0].set(0).at[NPTS - 1].set(NTOTAL - 1)


def draw_hadamard_sample_rows(key, part):
    stride = NTOTAL // S
    numbers = jnp.arange(S, dtype=jnp.int32) * stride + jax.random.randint(key, (S,), 0, stride, dtype=jnp.int32)
    return numbers.at[0].set(0).at[S - 1].set(NTOTAL - 1)


def draw_skeleton(key, part):
    positions = jnp.arange(R, dtype=jnp.int32)
    leaf_step = CLUSTER // R
    leaf_rows = positions[None, :] * leaf_step + jax.random.randint(jax.random.fold_in(key, 11), (N_LEAF, R), 0, leaf_step, dtype=jnp.int32)
    upper_rows = positions[None, :] * 2 + jax.random.randint(jax.random.fold_in(key, 12), (NODES - N_LEAF, R), 0, 2, dtype=jnp.int32)
    table = jnp.concatenate([leaf_rows, upper_rows], 0)
    return table.at[0, 0].set(0).at[0, R - 1].set(CLUSTER - 1)


def draw_ranks(key, part):
    values = jax.random.randint(jax.random.fold_in(key, 21), (NODES,), R // 2, R + 1, dtype=jnp.int32)
    high_node = jax.random.randint(jax.random.fold_in(key, 22), (), 0, NODES, dtype=jnp.int32)
    low_node = (high_node + 1 + jax.random.randint(jax.random.fold_in(key, 23), (), 0, NODES - 1, dtype=jnp.int32)) % NODES
    return values.at[high_node].set(R).at[low_node].set(R // 2)


def place_ends(values, own_key, smallest, top_value):
    extent = values.shape
    place = [jax.random.randint(jax.random.fold_in(own_key, axis), (), 0, extent[axis]) for axis in range(len(extent))]
    values = values.at[tuple(place)].set(smallest)
    longest = extent.index(max(extent))
    place[longest] = (place[longest] + 1) % extent[longest]
    return values.at[tuple(place)].set(top_value)


def block_levels(rng, shape, split, least, top_value):
    factor_of, own = 1.0, jax.random.fold_in(rng, 6)
    for dim, blocks in split:
        heights = jnp.exp(jax.random.uniform(jax.random.fold_in(own, dim), (blocks,), jnp.float32, least / len(split), top_value / len(split)))
        factor_of = factor_of * jnp.repeat(heights, shape[dim] // blocks).reshape([-1 if axis == dim else 1 for axis in range(len(shape))])
    return factor_of


def noise(stream_key, shape, scale, reach, pieces=(), kind=jnp.bfloat16):
    result = jax.random.normal(stream_key, shape, jnp.float32) * scale
    if len(pieces) > 0:
        result = block_levels(stream_key, shape, pieces, -0.22, 0.18) * result
    return jnp.clip(result, min=-reach, max=reach).astype(kind)


def setup_inputs(seed: int = 0) -> dict:
    arg_keys = jax.random.split(jax.random.key(seed), 8)
    return {
        "points": draw_points(jax.random.fold_in(arg_keys[7], 71), 0),
        "point_ids": draw_point_ids(jax.random.fold_in(arg_keys[7], 71), 0),
        "signs": place_ends(jax.random.randint(arg_keys[2], (NPTS,), 0, 2), jax.random.fold_in(arg_keys[2], 1), 0, 1).astype(jnp.int32),
        "hadamard_sample_rows": draw_hadamard_sample_rows(jax.random.fold_in(arg_keys[7], 71), 0),
        "samples": noise(arg_keys[4], (NPTS, S), 1.0, 6.0, ((0, 512),)),
        "skeleton": draw_skeleton(jax.random.fold_in(arg_keys[7], 71), 0),
        "ranks": draw_ranks(jax.random.fold_in(arg_keys[7], 71), 0),
    }


KERNEL_SCALE = 1.0
OMEGA_UNIT = 0.0625
RIDGE = 0.25
HIGH = lax.Precision.HIGHEST

def omega_rows(tags, hadamard_sample_rows, bit_count):
    powers = jnp.array([1 << shift for shift in range(bit_count)], dtype=jnp.int32)
    row_bits = (tags[0][:, None] // powers[None, :] % 2).astype(jnp.float32)
    col_bits = (hadamard_sample_rows[None, :] // powers[:, None] % 2).astype(jnp.float32)
    counted = jnp.dot(row_bits, col_bits, precision=HIGH)
    parity = counted - 2.0 * jnp.floor(0.5 * counted)
    flips = (2 * tags[1] - 1).astype(jnp.float32)
    return (1.0 - 2.0 * parity) * flips[:, None] * OMEGA_UNIT

def kernel_tile(left, right):
    squared_distance = jnp.zeros((left.shape[1], right.shape[1]), jnp.float32)
    for axis_k in range(3):
        offset = left[axis_k][:, None] - right[axis_k][None, :]
        squared_distance = squared_distance + offset * offset
    return jnp.exp(-KERNEL_SCALE * squared_distance)

def ridge_fit(picked, gram, rank):
    shift = RIDGE * jnp.trace(gram) / rank.astype(jnp.float32) + 1e-06
    ident = jnp.eye(gram.shape[0], dtype=jnp.float32)
    factor = jnp.linalg.cholesky(gram + shift * ident)
    return jax.scipy.linalg.cho_solve((factor, True), picked)

def reference(points, point_ids, signs, hadamard_sample_rows, samples, skeleton, ranks):
    bit_count = NTOTAL.bit_length() - 1
    positions = jnp.arange(R, dtype=jnp.int32)
    grouped_points = points.reshape(3, N_LEAF, CLUSTER).transpose(1, 0, 2)
    grouped_tags = jnp.stack([point_ids, signs]).reshape(2, N_LEAF, CLUSTER).transpose(1, 0, 2)
    grouped_samples = samples.reshape(N_LEAF, CLUSTER, S)

    def leaf_fit(item):
        own_points, own_tags, block, skel_row, rank = item
        omega = omega_rows(own_tags, hadamard_sample_rows, bit_count)
        tile = kernel_tile(own_points, own_points).astype(jnp.bfloat16)
        near = jnp.dot(tile.astype(jnp.float32), omega.astype(jnp.bfloat16).astype(jnp.float32), preferred_element_type=jnp.float32)
        residue = block.astype(jnp.float32) - near
        keep = (positions < rank).astype(jnp.float32)
        picked = residue[skel_row] * keep[:, None]
        spots = own_points[:, skel_row]
        gram = jnp.dot(picked, picked.T, precision=HIGH)
        fitted = ridge_fit(picked, gram, rank)
        basis = jnp.dot(residue, fitted.T, precision=HIGH)
        projected = jnp.dot(basis.T, omega, precision=HIGH)
        return (basis.astype(jnp.bfloat16), picked, projected, spots)
    basis, picked, projected, spots = lax.map(leaf_fit, (grouped_points, grouped_tags, grouped_samples, skeleton[:N_LEAF], ranks[:N_LEAF]))

    def merge_pair(pair_picked, pair_proj, paired_positions, pair_ranks, node_skel, node_rank):
        cross = kernel_tile(paired_positions[0], paired_positions[1])
        left_keep = (positions < pair_ranks[0]).astype(jnp.float32)
        right_keep = (positions < pair_ranks[1]).astype(jnp.float32)
        upper = (pair_picked[0] - jnp.dot(cross, pair_proj[1], precision=HIGH)) * left_keep[:, None]
        lower = (pair_picked[1] - jnp.dot(cross.T, pair_proj[0], precision=HIGH)) * right_keep[:, None]
        candidates = jnp.concatenate([upper, lower], 0)
        stacked = jnp.concatenate([pair_proj[0], pair_proj[1]], 0)
        cand_spots = jnp.concatenate([paired_positions[0], paired_positions[1]], 1)
        keep = (positions < node_rank).astype(jnp.float32)
        new_picked = candidates[node_skel] * keep[:, None]
        new_spots = cand_spots[:, node_skel]
        gram = jnp.dot(new_picked, new_picked.T, precision=HIGH)
        fitted = ridge_fit(new_picked, gram, node_rank)
        parent_basis = jnp.dot(candidates, fitted.T, precision=HIGH)
        new_proj = jnp.dot(parent_basis.T, stacked, precision=HIGH)
        return (new_picked, new_proj, new_spots)
    child_base = 0
    count = N_LEAF
    for level in range(3):
        half = count // 2
        base = child_base + count
        picked, projected, spots = jax.vmap(merge_pair)(picked.reshape(half, 2, R, S), projected.reshape(half, 2, R, S), spots.reshape(half, 2, 3, R), ranks[child_base:child_base + count].reshape(half, 2), skeleton[base:base + half], ranks[base:base + half])
        child_base = base
        count = half
    return (basis.reshape(NPTS, R), picked.reshape(NTOP * R, S), projected.reshape(NTOP * R, S))
```

```python
import functools

import jax
import jax.numpy as jnp
from jax import lax
from jax.experimental import pallas as pl
from jax.experimental.pallas import tpu as pltpu
from jax.sharding import PartitionSpec as P

MESH = pl.DeviceIdType.MESH
HIGH = lax.Precision.HIGHEST
F32 = jnp.float32
BF16 = jnp.bfloat16
VM = pl.BlockSpec(memory_space=pltpu.VMEM)
SM = pl.BlockSpec(memory_space=pltpu.SMEM)

NTOTAL = 1048576
KERNEL_SCALE = 1.0
RIDGE = 0.25
LOG2E = 1.4426950408889634
BITS = NTOTAL.bit_length() - 1
PANEL = 16
COLS = 16
LANES = 128


def dot(a, b, ca, cb, precision=HIGH):
    return lax.dot_general(
        a, b, (((ca,), (cb,)), ((), ())), precision=precision, preferred_element_type=F32
    )


def split3(x):
    hi = x.astype(BF16)
    rest = x - hi.astype(F32)
    mid = rest.astype(BF16)
    low = (rest - mid.astype(F32)).astype(BF16)
    return hi, mid, low


def iota(shape, axis):
    return lax.broadcasted_iota(jnp.int32, shape, axis)


def kern(squared_distance):
    return jnp.exp2(squared_distance * (-KERNEL_SCALE * LOG2E))


def spd_inverse(a_ref):
    n = a_ref.shape[0]
    lane = iota((PANEL, n), 1)
    sub = iota((PANEL, n), 0)
    ident = (lane == sub).astype(F32)
    lane_n = iota((n, n), 1)

    def step(b, carry):
        start = pl.multiple_of(b * PANEL, PANEL)
        panel = a_ref[pl.ds(start, PANEL), :]
        rolled = pltpu.roll(panel, lax.rem(n - start, n), 1)
        diag = [jnp.broadcast_to(rolled[:, k : k + 1], (PANEL, n)) for k in range(PANEL)]
        rows = jnp.where(lane < PANEL, ident, rolled)
        for k in range(PANEL):
            inv = 1.0 / diag[k][k : k + 1, :]
            here = sub == k
            factor = diag[k] * inv
            for j in range(k + 1, PANEL):
                own = diag[j][k : k + 1, :]
                diag[j] = jnp.where(here, own * inv, diag[j] - factor * own)
            own = rows[k : k + 1, :]
            rows = jnp.where(here, own * inv, rows - factor * own)
        rows = pltpu.roll(rows, start, 1)
        side = jnp.where(lane < start, -panel, panel)
        side = jnp.where((lane >= start) & (lane < start + PANEL), 0.0, side)
        q1, q2, q3 = split3(side)
        r1, r2, r3 = split3(rows)
        left = jnp.concatenate([q1, q1, q1, q2, q2, q3], 0)
        right = jnp.concatenate([r1, r2, r3, r1, r2, r1], 0)
        change = dot(left, right, 0, 0, lax.Precision.DEFAULT)
        cleared = jnp.where((lane_n >= start) & (lane_n < start + PANEL), 0.0, a_ref[...])
        a_ref[...] = cleared - change
        a_ref[pl.ds(start, PANEL), :] = rows
        return carry

    lax.fori_loop(0, n // PANEL, step, 0)


def ridge_inverse(gram, rank, a_ref):
    n = gram.shape[0]
    same = iota((n, n), 0) == iota((n, n), 1)
    trace = jnp.sum(jnp.where(same, gram, 0.0), keepdims=True)
    shift = RIDGE * trace / rank.astype(F32) + 1e-06
    a_ref[...] = gram + jnp.where(same, shift, 0.0)
    spd_inverse(a_ref)


def gather_kernel(x_ref, o_ref, send, recv):
    me = lax.axis_index("col")
    barrier = pltpu.get_barrier_semaphore()
    for off in range(1, COLS):
        pl.semaphore_signal(
            barrier, inc=1, device_id={"col": lax.rem(me + off, COLS)}, device_id_type=MESH
        )
    pl.semaphore_wait(barrier, COLS - 1)
    copies = []
    for off in range(1, COLS):
        peer = lax.rem(me + off, COLS)
        copy = pltpu.make_async_remote_copy(
            src_ref=x_ref,
            dst_ref=o_ref.at[me],
            send_sem=send.at[off],
            recv_sem=recv.at[COLS - off],
            device_id={"col": peer},
            device_id_type=MESH,
        )
        copy.start()
        copies.append(copy)
    o_ref[me] = x_ref[...]
    for off in range(1, COLS):
        pltpu.make_async_remote_copy(
            src_ref=x_ref,
            dst_ref=o_ref.at[lax.rem(me + off, COLS)],
            send_sem=send.at[off],
            recv_sem=recv.at[off],
            device_id={"col": lax.rem(me + off, COLS)},
            device_id_type=MESH,
        ).wait_recv()
    for copy in copies:
        copy.wait_send()


def gather_cols(x, cid):
    return pl.pallas_call(
        gather_kernel,
        out_shape=jax.ShapeDtypeStruct((COLS, *x.shape), x.dtype),
        in_specs=[VM],
        out_specs=VM,
        scratch_shapes=[pltpu.SemaphoreType.DMA((COLS,)), pltpu.SemaphoreType.DMA((COLS,))],
        compiler_params=pltpu.CompilerParams(collective_id=cid, has_side_effects=True),
        name=f"gather_{cid}",
    )(x)


def reduce_kernel(n_ref, o_ref, half, mine, landed, s0, r0, s1, r1, s2, r2, s3, r3):
    me = lax.axis_index("col")
    core = lax.rem(me, 2)
    z = me // 2
    partner = me + 1 - 2 * core
    zs = COLS // 2
    rows = n_ref.shape[0]
    part = rows // 2
    piece = part // zs
    barrier = pltpu.get_barrier_semaphore()
    peers = [lax.rem(z + off, zs) * 2 + core for off in range(1, zs)]
    for peer in [partner, *peers]:
        pl.semaphore_signal(barrier, inc=1, device_id={"col": peer}, device_id_type=MESH)
    pl.semaphore_wait(barrier, zs)

    def copy(src, dst, send, recv, peer):
        return pltpu.make_async_remote_copy(
            src_ref=src,
            dst_ref=dst,
            send_sem=send,
            recv_sem=recv,
            device_id={"col": peer},
            device_id_type=MESH,
        )

    own0 = pl.multiple_of(core * part, part)
    other0 = pl.multiple_of((1 - core) * part, part)
    first = copy(n_ref.at[pl.ds(other0, part)], half, s0, r0, partner)
    first.start()
    first.wait_recv()
    mine[...] = n_ref[pl.ds(own0, part)] + half[...]
    waits = [first]
    for off in range(1, zs):
        peer = lax.rem(z + off, zs)
        put = copy(
            mine.at[pl.ds(pl.multiple_of(peer * piece, piece), piece)],
            landed.at[off - 1],
            s1.at[off - 1],
            r1.at[off - 1],
            peers[off - 1],
        )
        put.start()
        waits.append(put)
    here = pl.multiple_of(z * piece, piece)
    total = mine[pl.ds(here, piece)]
    for off in range(1, zs):
        waits[off].wait_recv()
        total = total + landed[off - 1]
    slot = pl.multiple_of(own0 + here, piece)
    o_ref[pl.ds(slot, piece)] = total
    spread = []
    for off in range(1, zs):
        put = copy(o_ref.at[pl.ds(slot, piece)], o_ref.at[pl.ds(slot, piece)], s2.at[off - 1], r2.at[off - 1], peers[off - 1])
        put.start()
        spread.append(put)
    put = copy(o_ref.at[pl.ds(slot, piece)], o_ref.at[pl.ds(slot, piece)], s3.at[0], r3.at[0], partner)
    put.start()
    relays = [put]
    for off in range(1, zs):
        spread[off - 1].wait_recv()
        source = lax.rem(z + zs - off, zs)
        rng = pl.ds(pl.multiple_of(own0 + source * piece, piece), piece)
        put = copy(o_ref.at[rng], o_ref.at[rng], s3.at[off], r3.at[off], partner)
        put.start()
        relays.append(put)
    for put in relays:
        put.wait_recv()
    for put in waits + spread + relays:
        put.wait_send()


def reduce_cols(x, cid):
    rows, width = x.shape
    zs = COLS // 2
    part = rows // 2
    dma = pltpu.SemaphoreType.DMA
    return pl.pallas_call(
        reduce_kernel,
        out_shape=jax.ShapeDtypeStruct(x.shape, x.dtype),
        in_specs=[VM],
        out_specs=VM,
        scratch_shapes=[
            pltpu.VMEM((part, width), F32),
            pltpu.VMEM((part, width), F32),
            pltpu.VMEM((zs - 1, part // zs, width), F32),
            dma(()),
            dma(()),
            dma((zs - 1,)),
            dma((zs - 1,)),
            dma((zs - 1,)),
            dma((zs - 1,)),
            dma((zs,)),
            dma((zs,)),
        ],
        compiler_params=pltpu.CompilerParams(collective_id=cid, has_side_effects=True),
        name=f"reduce_{cid}",
    )(x)


CHUNKS = 4


def swap_kernel(bit, *refs):
    n = 2
    ins, outs = refs[:n], refs[n : 2 * n]
    s1, r1, s2, r2 = refs[2 * n :]
    leaf = lax.axis_index("leaf")
    me = lax.axis_index("col")
    core = lax.rem(me, 2)
    partner = me + 1 - 2 * core
    side = lax.rem(leaf // bit, 2)
    sibling = leaf + bit - 2 * bit * side
    barrier = pltpu.get_barrier_semaphore()
    pl.semaphore_signal(barrier, inc=1, device_id={"leaf": sibling}, device_id_type=MESH)
    pl.semaphore_signal(barrier, inc=1, device_id={"col": partner}, device_id_type=MESH)
    pl.semaphore_wait(barrier, 2)
    rows = ins[0].shape[0]
    size = rows // 2 // CHUNKS
    first = []
    for i in range(n):
        for q in range(CHUNKS):
            rng = pl.ds(pl.multiple_of(core * (rows // 2) + q * size, size), size)
            put = pltpu.make_async_remote_copy(
                src_ref=ins[i].at[rng],
                dst_ref=outs[i].at[side, rng],
                send_sem=s1.at[i, q],
                recv_sem=r1.at[i, q],
                device_id={"leaf": sibling},
                device_id_type=MESH,
            )
            put.start()
            first.append(put)
    for i in range(n):
        outs[i][side] = ins[i][...]
    second = []
    for i in range(n):
        for q in range(CHUNKS):
            rng = pl.ds(pl.multiple_of(core * (rows // 2) + q * size, size), size)
            first[i * CHUNKS + q].wait_recv()
            put = pltpu.make_async_remote_copy(
                src_ref=outs[i].at[1 - side, rng],
                dst_ref=outs[i].at[1 - side, rng],
                send_sem=s2.at[i, q],
                recv_sem=r2.at[i, q],
                device_id={"col": partner},
                device_id_type=MESH,
            )
            put.start()
            second.append(put)
    for put in second:
        put.wait_recv()
    for put in first + second:
        put.wait_send()


def swap_siblings(xs, bit, cid):
    dma = pltpu.SemaphoreType.DMA
    n = len(xs)
    return pl.pallas_call(
        functools.partial(swap_kernel, bit),
        out_shape=[jax.ShapeDtypeStruct((2, *x.shape), x.dtype) for x in xs],
        in_specs=[VM] * n,
        out_specs=[VM] * n,
        scratch_shapes=[dma((n, CHUNKS))] * 4,
        compiler_params=pltpu.CompilerParams(collective_id=cid, has_side_effects=True),
        name=f"swap_{cid}",
    )(*xs)


def near_kernel(all_ref, own_ref, had_ref, samp_ref, skel_ref, rank_ref, res_ref, om_ref, pick_ref, acc, own_b, idx, sem):
    col = lax.axis_index("col")
    leaf = lax.axis_index("leaf")
    rows = own_ref.shape[1]
    width = samp_ref.shape[1]
    nbits = 32
    load = pltpu.make_async_copy(skel_ref.at[leaf], idx, sem)
    load.start()
    bit_row = iota((nbits, width), 0)
    had = jnp.broadcast_to(had_ref[...], (nbits, width))
    had_bits = ((had >> jnp.minimum(bit_row, BITS)) & 1).astype(F32) * 0.5
    had_bits = jnp.where(bit_row == BITS, 0.5, jnp.where(bit_row == BITS + 1, 0.25, had_bits))
    had_bits = jnp.where(bit_row > BITS + 1, 0.0, had_bits).astype(BF16)

    def omega4(block):
        shift = iota((nbits, rows), 0)
        ids = jnp.broadcast_to(block[3:4, :].astype(jnp.int32), (nbits, rows))
        bits = ((ids >> jnp.minimum(shift, BITS)) & 1).astype(F32)
        bits = jnp.where(shift == BITS, 1.0 - block[4:5, :], bits)
        bits = jnp.where(shift == BITS + 1, 1.0, bits)
        bits = jnp.where(shift > BITS + 1, 0.0, bits).astype(BF16)
        half = dot(bits, had_bits, 0, 0, lax.Precision.DEFAULT)
        return (half - jnp.round(half)).astype(BF16)

    own = own_ref[...]
    ident = (iota((8, LANES), 0) == iota((8, LANES), 1)).astype(F32)
    own_cols = dot(own, ident, 0, 0)
    for axis in range(3):
        own_b[axis] = jnp.broadcast_to(own_cols[:, axis : axis + 1], (rows, LANES))
    om_ref[...] = omega4(own)

    def step(j, carry):
        block = all_ref[j]
        om = omega4(block)
        tiles = []
        for c in range(rows // LANES):
            d2 = jnp.zeros((rows, LANES), F32)
            for axis in range(3):
                off = own_b[axis] - block[axis : axis + 1, c * LANES : (c + 1) * LANES]
                d2 = d2 + off * off
            tiles.append(kern(d2).astype(BF16))
        part = dot(jnp.concatenate(tiles, 1), om, 1, 0, lax.Precision.DEFAULT)

        @pl.when(j == 0)
        def _():
            acc[...] = part

        @pl.when(j > 0)
        def _():
            acc[...] += part

        return carry

    lax.fori_loop(0, COLS, step, 0)
    res_ref[...] = samp_ref[...].astype(F32) - 0.25 * acc[...]
    load.wait()
    count = pick_ref.shape[0]
    rank = rank_ref[leaf]
    acc[:, 0:LANES] = own_cols
    for i in range(count):
        entry = col * count + i
        where = idx[entry] - col * rows
        keep = jnp.where(entry < rank, 1.0, 0.0)
        tile = pl.ds(pl.multiple_of(where // 8 * 8, 8), 8)
        hit = iota((8, 1), 0) == lax.rem(where, 8)
        row = jnp.sum(jnp.where(hit, res_ref[tile, :], 0.0), 0, keepdims=True)
        pick_ref[i : i + 1, 0:width] = row * keep
        pick_ref[i : i + 1, width : width + LANES] = jnp.sum(
            jnp.where(hit, acc[tile, 0:LANES], 0.0), 0, keepdims=True
        )


def leaf_kernel(pick_ref, res_ref, om_ref, rank_ref, part_ref, basis_ref, inv_ref):
    leaf = lax.axis_index("leaf")
    width = res_ref.shape[1]
    picked = pick_ref[:, 0:width]
    gram = dot(picked, picked, 1, 1)
    raw = dot(res_ref[...], picked, 1, 1)
    om = om_ref[...]
    total = None
    for piece in split3(raw):
        term = dot(piece, om, 0, 0, lax.Precision.DEFAULT)
        total = term if total is None else total + term
    part_ref[...] = total * 0.25
    ridge_inverse(gram, rank_ref[leaf], inv_ref)
    basis_ref[...] = dot(raw, inv_ref[...], 1, 0).astype(BF16)


def merge_kernel(level, child_base, base, pk_ref, pr_ref, skel_ref, rank_ref, *refs):
    leaf = lax.axis_index("leaf")
    width = pr_ref.shape[2]
    r = pr_ref.shape[1]
    pair = leaf // (1 << level)
    rank_l = rank_ref[child_base + 2 * pair]
    rank_r = rank_ref[child_base + 2 * pair + 1]
    rank_p = rank_ref[base + pair]
    spots_l = pk_ref[0, :, width : width + LANES]
    spots_r = pk_ref[1, :, width : width + LANES]
    row_r = spots_r.T
    d2 = jnp.zeros((r, r), F32)
    for axis in range(3):
        off = spots_l[:, axis : axis + 1] - row_r[axis : axis + 1, :]
        d2 = d2 + off * off
    cross = kern(d2)
    proj_l, proj_r = pr_ref[0], pr_ref[1]
    sub = iota((r, 1), 0)
    upper = (pk_ref[0, :, 0:width] - dot(cross, proj_r, 1, 0)) * jnp.where(sub < rank_l, 1.0, 0.0)
    lower = (pk_ref[1, :, 0:width] - dot(cross, proj_l, 0, 0)) * jnp.where(sub < rank_r, 1.0, 0.0)
    cand = jnp.concatenate([upper, lower], 0)
    spots = jnp.concatenate([spots_l, spots_r], 0)
    row = skel_ref[pl.ds(base + pair, 1), :]
    chooser = jnp.where(jnp.broadcast_to(row, (2 * r, r)) == iota((2 * r, r), 0), 1.0, 0.0).astype(BF16)
    chosen = None
    for piece in split3(jnp.concatenate([cand, spots], 1)):
        term = dot(chooser, piece, 0, 0, lax.Precision.DEFAULT)
        chosen = term if chosen is None else chosen + term
    picked = chosen[:, 0:width] * jnp.where(sub < rank_p, 1.0, 0.0)
    gram = dot(picked, picked, 1, 1)
    raw = dot(cand, picked, 1, 1)
    back = dot(raw[0:r], proj_l, 0, 0) + dot(raw[r:], proj_r, 0, 0)
    if len(refs) == 3:
        out_pk, out_pr, inv_ref = refs
        out_pk[:, 0:width] = picked
        out_pk[:, width : width + LANES] = chosen[:, width : width + LANES]
        ridge_inverse(gram, rank_p, inv_ref)
        out_pr[...] = dot(inv_ref[...], back, 1, 0)
    else:
        top_s, top_o, inv_ref, tmp = refs
        col = lax.axis_index("col")
        share, span = top_s.shape
        ridge_inverse(gram, rank_p, inv_ref)
        tmp[...] = picked
        turn = lax.rem(width - col * span, width)
        rows = pl.ds(pl.multiple_of(lax.rem(leaf, 8) * share, share), share)
        top_s[...] = pltpu.roll(tmp[rows, :], turn, 1)[:, 0:span]
        mine = dot(inv_ref[rows, :], back, 1, 0)
        top_o[...] = pltpu.roll(mine, turn, 1)[:, 0:span]


def local(points, point_ids, signs, hadamard_sample_rows, samples, skeleton, ranks):
    rows = points.shape[1]
    width = samples.shape[1]
    r = skeleton.shape[1]
    leaf_count = lax.axis_size("leaf")
    own = jnp.concatenate(
        [
            points,
            point_ids[None].astype(F32),
            signs[None].astype(F32),
            jnp.zeros((3, rows), F32),
        ],
        0,
    )
    everyone = gather_cols(own, 0)
    shape = jax.ShapeDtypeStruct
    residue, om, picks = pl.pallas_call(
        near_kernel,
        out_shape=[shape((rows, width), F32), shape((rows, width), BF16), shape((r // COLS, width + LANES), F32)],
        in_specs=[VM, VM, VM, VM, VM, SM],
        out_specs=[VM] * 3,
        scratch_shapes=[
            pltpu.VMEM((rows, width), F32),
            pltpu.VMEM((3, rows, LANES), F32),
            pltpu.SMEM((r,), jnp.int32),
            pltpu.SemaphoreType.DMA(()),
        ],
        name="near",
    )(everyone, own, hadamard_sample_rows[None], samples, skeleton, ranks)
    picked = gather_cols(picks, 1).reshape(r, width + LANES)
    part, leaf_basis, inverse = pl.pallas_call(
        leaf_kernel,
        out_shape=[shape((r, width), F32), shape((rows, r), BF16), shape((r, r), F32)],
        in_specs=[VM, VM, VM, SM],
        out_specs=[VM] * 3,
        name="leaf",
    )(picked, residue, om, ranks)
    total = reduce_cols(part, 2)
    projected = jnp.dot(inverse, total, precision=HIGH)
    base = 0
    for level in range(1, 4):
        child_base = base
        base = base + (leaf_count >> level - 1)
        pk2, pr2 = swap_siblings([picked, projected], 1 << level - 1, 2 + level)
        last = level == 3
        share, span = r // 8, width // COLS
        out = [shape((share, span), F32)] * 2 if last else [shape((r, width + LANES), F32), shape((r, width), F32)]
        picked, projected = pl.pallas_call(
            functools.partial(merge_kernel, level, child_base, base),
            out_shape=out,
            in_specs=[VM, VM, VM, SM],
            out_specs=[VM] * 2,
            scratch_shapes=[pltpu.VMEM((r, r), F32)] + ([pltpu.VMEM((r, width), F32)] if last else []),
            name=f"merge_{level}",
        )(pk2, pr2, skeleton, ranks)
    return (leaf_basis, picked, projected)


def solution(mesh):
    placed = (
        P(None, ("leaf", "col")),
        P(("leaf", "col")),
        P(("leaf", "col")),
        P(),
        P(("leaf", "col"), None),
        P(),
        P(),
    )
    return jax.shard_map(
        local,
        mesh=mesh,
        in_specs=placed,
        out_specs=(P(("leaf", "col"), None), P("leaf", "col"), P("leaf", "col")),
        check_vma=False,
    )
```

```python
import jax
import jax.numpy as jnp
from jax import lax
from jax.experimental import pallas as pl
from jax.experimental.pallas import tpu as pltpu
from jax.sharding import PartitionSpec as P

MESH = pl.DeviceIdType.MESH
DMA = pltpu.SemaphoreType.DMA
F32 = jnp.float32
BF16 = jnp.bfloat16
VM = pl.BlockSpec(memory_space=pltpu.VMEM)
SM = pl.BlockSpec(memory_space=pltpu.SMEM)
ANY = pl.BlockSpec(memory_space=pl.ANY)

NTOTAL = 1048576
KERNEL_SCALE = 1.0
RIDGE = 0.25
LOG2E = 1.4426950408889634
BITS = NTOTAL.bit_length() - 1
NBITS = 32
PANEL = 16
COLS = 16
ZS = COLS // 2
LANES = 128
LEVELS = 3


def bdot(a, b, ca, cb):
    return lax.dot_general(a, b, (((ca,), (cb,)), ((), ())), preferred_element_type=F32)


def split(x, count):
    pieces = []
    for _ in range(count - 1):
        piece = x.astype(BF16)
        pieces.append(piece)
        x = x - piece.astype(F32)
    return [*pieces, x.astype(BF16)]


def mm(a, b, ca, cb, terms=6):
    count = 3 if terms == 6 else 2
    pa, pb = split(a, count), split(b, count)
    pairs = [(i, j) for i in range(count) for j in range(count) if i + j < count]
    left = jnp.concatenate([pa[i] for i, _ in pairs], ca)
    right = jnp.concatenate([pb[j] for _, j in pairs], cb)
    return bdot(left, right, ca, cb)


def exact(a, b, ca, cb):
    pieces = split(a, 3)
    return bdot(jnp.concatenate(pieces, ca), jnp.concatenate([b] * 3, cb), ca, cb)


def iota(shape, axis):
    return lax.broadcasted_iota(jnp.int32, shape, axis)


def kern(squared_distance):
    return jnp.exp2(squared_distance * (-KERNEL_SCALE * LOG2E))


def spd_inverse(a_ref, hook):
    n = a_ref.shape[0]
    lane = iota((PANEL, n), 1)
    sub = iota((PANEL, n), 0)
    ident = (lane == sub).astype(F32)
    lane_n = iota((n, n), 1)

    def step(b, carry):
        start = pl.multiple_of(b * PANEL, PANEL)
        panel = a_ref[pl.ds(start, PANEL), :]
        rolled = pltpu.roll(panel, lax.rem(n - start, n), 1)
        diag = [jnp.broadcast_to(rolled[:, k : k + 1], (PANEL, n)) for k in range(PANEL)]
        rows = jnp.where(lane < PANEL, ident, rolled)
        for k in range(PANEL):
            inv = 1.0 / diag[k][k : k + 1, :]
            here = sub == k
            factor = diag[k] * inv
            for j in range(k + 1, PANEL):
                own = diag[j][k : k + 1, :]
                diag[j] = jnp.where(here, own * inv, diag[j] - factor * own)
            own = rows[k : k + 1, :]
            rows = jnp.where(here, own * inv, rows - factor * own)
        rows = pltpu.roll(rows, start, 1)
        side = jnp.where(lane < start, -panel, panel)
        side = jnp.where((lane >= start) & (lane < start + PANEL), 0.0, side)
        change = mm(side, rows, 0, 0)
        cleared = jnp.where((lane_n >= start) & (lane_n < start + PANEL), 0.0, a_ref[...])
        a_ref[...] = cleared - change
        a_ref[pl.ds(start, PANEL), :] = rows
        hook(b)
        return carry

    lax.fori_loop(0, n // PANEL, step, 0)


def ridged(gram, rank):
    n = gram.shape[0]
    same = iota((n, n), 0) == iota((n, n), 1)
    trace = jnp.sum(jnp.where(same, gram, 0.0), keepdims=True)
    shift = RIDGE * trace / rank.astype(F32) + 1e-06
    return gram + jnp.where(same, shift, 0.0)


def hss_kernel(
    points_ref, ids_ref, signs_ref, had_ref, samp_hbm, skel_ref, rank_ref,
    basis_ref, top_s, top_o,
    samp, every, om_all, own_b, pick_b, res, raw_ref, part, half, mine, landed, pk, hh, ww, pp, pk3, hh3, ww3,
    samp_sem, g_s, g_r, gp_s, gp_r, p_s, p_r, pp_s, pp_r,
    pair_s, pair_r, rs_s, rs_r, ag_s, ag_r, ap_s, ap_r, ax_s, ax_r, axp_s, axp_r,
    xk_s, xk_r, xkp_s, xkp_r, xh_s, xh_r, xhp_s, xhp_r, xw_s, xw_r, xwp_s, xwp_r,
):
    leaf = lax.axis_index("leaf")
    me = lax.axis_index("col")
    leaves = lax.axis_size("leaf")
    core = lax.rem(me, 2)
    z = me // 2
    partner = me + 1 - 2 * core
    rows = points_ref.shape[1]
    width = had_ref.shape[1]
    r = skel_ref.shape[1]
    count = r // COLS
    sides = [lax.rem(leaf // (1 << lvl), 2) for lvl in range(LEVELS)]
    siblings = [leaf + (1 << lvl) - (2 << lvl) * sides[lvl] for lvl in range(LEVELS)]
    sends = []

    def put(src, dst, send, recv, keep=True, **device):
        copy = pltpu.make_async_remote_copy(
            src_ref=src, dst_ref=dst, send_sem=send, recv_sem=recv, device_id=device, device_id_type=MESH
        )
        if keep:
            sends.append(copy)
        return copy

    def zpeer(off):
        return lax.rem(z + off, ZS)

    fetch = pltpu.make_async_copy(samp_hbm, samp, samp_sem)
    fetch.start()
    barrier = pltpu.get_barrier_semaphore()
    for off in range(1, ZS):
        pl.semaphore_signal(barrier, inc=1, device_id={"col": zpeer(off) * 2 + core}, device_id_type=MESH)
    pl.semaphore_signal(barrier, inc=1, device_id={"col": partner}, device_id_type=MESH)
    for sibling in siblings:
        pl.semaphore_signal(barrier, inc=1, device_id={"leaf": sibling}, device_id_type=MESH)
    every[me, 0:3, :] = points_ref[...]
    every[me, 3:4, :] = ids_ref[...].astype(F32)
    every[me, 4:5, :] = signs_ref[...].astype(F32)
    every[me, 5:8, :] = jnp.zeros((3, rows), F32)
    pl.semaphore_wait(barrier, ZS + LEVELS)

    for off in (1, 7, 2, 6, 3, 5, 4):
        put(every.at[me], every.at[me], g_s.at[off], g_r.at[ZS - off], col=zpeer(off) * 2 + core).start()
    put(every.at[me], every.at[me], gp_s.at[0], gp_r.at[0], col=partner).start()

    bit_row = iota((NBITS, width), 0)
    had = jnp.broadcast_to(had_ref[...], (NBITS, width))
    had_bits = ((had >> jnp.minimum(bit_row, BITS)) & 1).astype(F32) * 0.5
    had_bits = jnp.where(bit_row == BITS, 0.5, jnp.where(bit_row == BITS + 1, 0.25, had_bits))
    had_bits = jnp.where(bit_row > BITS + 1, 0.0, had_bits).astype(BF16)

    def omega4(block):
        shift = iota((NBITS, rows), 0)
        ids = jnp.broadcast_to(block[3:4, :].astype(jnp.int32), (NBITS, rows))
        bits = ((ids >> jnp.minimum(shift, BITS)) & 1).astype(F32)
        bits = jnp.where(shift == BITS, 1.0 - block[4:5, :], bits)
        bits = jnp.where(shift == BITS + 1, 1.0, bits)
        bits = jnp.where(shift > BITS + 1, 0.0, bits).astype(BF16)
        halves = bdot(bits, had_bits, 0, 0)
        return (halves - jnp.round(halves)).astype(BF16)

    ident = (iota((8, LANES), 0) == iota((8, LANES), 1)).astype(BF16)
    own_cols = exact(every[me], ident, 0, 0)
    for axis in range(3):
        own_b[axis] = jnp.broadcast_to(own_cols[:, axis : axis + 1], (rows, LANES))

    my_rows = pl.ds(pl.multiple_of(me * count, count), count)
    entries = jnp.broadcast_to(skel_ref[pl.ds(leaf, 1), :] - me * rows, (rows, r))
    chooser = jnp.where(entries == iota((rows, r), 0), 1.0, 0.0).astype(BF16)
    ww3[...] = bdot(jnp.concatenate([chooser] * 3, 0), jnp.concatenate(split(own_cols, 3), 0), 0, 0)
    spot = ww3[my_rows, :]
    for axis in range(3):
        pick_b[axis] = jnp.broadcast_to(spot[:, axis : axis + 1], (count, LANES))

    def zorder(t):
        return lax.rem(jnp.where(lax.rem(t, 2) == 1, (t + 1) // 2, ZS - t // 2), ZS)

    def tile_of(columns, block):
        tiles = []
        for c in range(rows // LANES):
            d2 = None
            for axis in range(3):
                off = columns[axis] - block[axis : axis + 1, c * LANES : (c + 1) * LANES]
                d2 = off * off if d2 is None else d2 + off * off
            tiles.append(kern(d2).astype(BF16))
        return jnp.concatenate(tiles, 1)

    def scan_blocks(t, acc):
        off = zorder(t)
        there = zpeer(off)
        same = there * 2 + core
        other = there * 2 + 1 - core

        @pl.when(t > 0)
        def _():
            put(every.at[same], every.at[same], g_s.at[off], g_r.at[off], keep=False, col=partner).wait_recv()
            put(every.at[same], every.at[same], gp_s.at[t], gp_r.at[t], keep=False, col=partner).start()

        for slot in (same, other):
            if slot is other:
                put(every.at[slot], every.at[slot], gp_s.at[t], gp_r.at[t], keep=False, col=partner).wait_recv()
            block = every[slot]
            om = omega4(block)
            om_all[slot] = om
            acc = acc + bdot(tile_of([pick_b[axis] for axis in range(3)], block), om, 1, 0)
        return acc

    acc = lax.fori_loop(0, ZS, scan_blocks, jnp.zeros((count, width), F32))
    fetch.wait()
    keep = jnp.where(iota((count, 1), 0) + me * count < rank_ref[leaf], 1.0, 0.0)
    part[...] = bdot(chooser, samp[...], 0, 0)
    pk[0, sides[0], my_rows, 0:width] = (part[my_rows, :] - 0.25 * acc) * keep
    pk[0, sides[0], my_rows, width : width + LANES] = spot

    def pick_rows(slot):
        return pk.at[0, sides[0], pl.ds(pl.multiple_of(slot * count, count), count)]

    for off in (1, 7, 2, 6, 3, 5, 4):
        put(pick_rows(me), pick_rows(me), p_s.at[off], p_r.at[ZS - off], col=zpeer(off) * 2 + core).start()
    put(pick_rows(me), pick_rows(me), pp_s.at[0], pp_r.at[0], col=partner).start()

    res[...] = samp[...].astype(F32)

    def near_step(t, carry):
        off = zorder(t)
        there = zpeer(off)
        same = there * 2 + core

        @pl.when(t > 0)
        def _():
            put(pick_rows(same), pick_rows(same), p_s.at[off], p_r.at[off], keep=False, col=partner).wait_recv()
            put(pick_rows(same), pick_rows(same), pp_s.at[t], pp_r.at[t], keep=False, col=partner).start()

        columns = [own_b[axis] for axis in range(3)]
        tile = jnp.concatenate([tile_of(columns, every[there * 2 + k]) for k in range(2)], 1)
        om = om_all[pl.ds(there * 2, 2)].reshape(2 * rows, width)
        res[...] -= 0.25 * bdot(tile, om, 1, 0)
        return carry

    lax.fori_loop(0, ZS, near_step, 0)

    def finish_relays(t, carry):
        other = zpeer(zorder(t)) * 2 + 1 - core
        put(pick_rows(other), pick_rows(other), pp_s.at[t], pp_r.at[t], keep=False, col=partner).wait_recv()
        return carry

    lax.fori_loop(0, ZS, finish_relays, 0)

    def pieces(buf, level, side, chunks, half_of):
        size = r // 2 // chunks
        return [buf.at[level, side, pl.ds(pl.multiple_of(half_of * (r // 2) + q * size, size), size)] for q in range(chunks)]

    def offer(buf, level, chunks, s, rv):
        for q, piece in enumerate(pieces(buf, level, sides[level], chunks, core)):
            put(piece, piece, s.at[level, q], rv.at[level, q], leaf=siblings[level]).start()

    def relay(buf, level, chunks, s, rv, s2, rv2):
        for q, piece in enumerate(pieces(buf, level, 1 - sides[level], chunks, core)):
            put(piece, piece, s.at[level, q], rv.at[level, q], keep=False, leaf=siblings[level]).wait_recv()
            put(piece, piece, s2.at[level, q], rv2.at[level, q], keep=False, col=partner).start()

    def settle(buf, level, chunks, s2, rv2):
        for q, piece in enumerate(pieces(buf, level, 1 - sides[level], chunks, 1 - core)):
            put(piece, piece, s2.at[level, q], rv2.at[level, q], keep=False, col=partner).wait_recv()

    def drain_relay(buf, level, chunks, s2, rv2):
        for q, piece in enumerate(pieces(buf, level, 1 - sides[level], chunks, core)):
            put(piece, piece, s2.at[level, q], rv2.at[level, q], keep=False, col=partner).wait_send()

    offer(pk, 0, 2, xk_s, xk_r)

    side0 = sides[0]
    picked = pk[0, side0, :, 0:width]
    raw = mm(res[...], picked, 1, 1)
    raw_ref[...] = raw
    om_own = om_all[me]
    part[...] = 0.25 * exact(raw, om_own, 0, 0)
    r2 = r // 2
    own0 = pl.multiple_of(core * r2, r2)
    other0 = pl.multiple_of((1 - core) * r2, r2)
    pair = put(part.at[pl.ds(other0, r2)], half, pair_s, pair_r, col=partner)
    pair.start()
    ww[0, side0] = ridged(mm(picked, picked, 1, 1), rank_ref[leaf])
    scatter = []
    for off in range(1, ZS):
        piece = pl.ds(pl.multiple_of(zpeer(off) * count, count), count)
        scatter.append(put(mine.at[piece], landed.at[off - 1], rs_s.at[off], rs_r.at[off], col=zpeer(off) * 2 + core))

    def leaf_hook(b):
        @pl.when(b == 2)
        def _():
            pair.wait_recv()
            mine[...] = part[pl.ds(own0, r2)] + half[...]
            for copy in scatter:
                copy.start()

        @pl.when(b == 6)
        def _():
            relay(pk, 0, 2, xk_s, xk_r, xkp_s, xkp_r)

    spd_inverse(ww.at[0, side0], leaf_hook)
    offer(ww, 0, 1, xw_s, xw_r)
    basis_ref[...] = mm(raw_ref[...], ww[0, side0], 1, 0).astype(BF16)

    def n_rows(side, half_of, chip):
        return hh.at[0, side, pl.ds(pl.multiple_of(half_of * r2 + chip * count, count), count)]

    total = mine[pl.ds(pl.multiple_of(z * count, count), count)]
    for off in range(1, ZS):
        scatter[off - 1].wait_recv()
        total = total + landed[off - 1]
    hh[0, side0, pl.ds(pl.multiple_of(own0 + z * count, count), count)] = total
    here = n_rows(side0, core, z)
    for off in (1, 7, 2, 6, 3, 5, 4):
        put(here, here, ag_s.at[off], ag_r.at[ZS - off], col=zpeer(off) * 2 + core).start()
    put(here, here, ap_s.at[0], ap_r.at[0], col=partner).start()
    put(here, here, ax_s.at[0], ax_r.at[0], leaf=siblings[0]).start()
    for off in (1, 7, 2, 6, 3, 5, 4):
        got = n_rows(side0, core, zpeer(off))
        put(got, got, ag_s.at[off], ag_r.at[off], keep=False, col=partner).wait_recv()
        put(got, got, ap_s.at[off], ap_r.at[off], col=partner).start()
        put(got, got, ax_s.at[off], ax_r.at[off], leaf=siblings[0]).start()
    relay(ww, 0, 1, xw_s, xw_r, xwp_s, xwp_r)
    for off in (0, 1, 7, 2, 6, 3, 5, 4):
        got = n_rows(1 - side0, core, zpeer(off))
        put(got, got, ax_s.at[off], ax_r.at[off], keep=False, leaf=siblings[0]).wait_recv()
        put(got, got, axp_s.at[off], axp_r.at[off], col=partner).start()
    for off in range(ZS):
        got = n_rows(side0, 1 - core, zpeer(off))
        put(got, got, ap_s.at[off], ap_r.at[off], keep=False, col=partner).wait_recv()
    pp[side0] = mm(ww[0, side0], hh[0, side0], 1, 0)
    settle(pk, 0, 2, xkp_s, xkp_r)
    settle(ww, 0, 1, xwp_s, xwp_r)
    for off in range(ZS):
        got = n_rows(1 - side0, 1 - core, zpeer(off))
        put(got, got, axp_s.at[off], axp_r.at[off], keep=False, col=partner).wait_recv()
    pp[1 - side0] = mm(ww[0, 1 - side0], hh[0, 1 - side0], 1, 0)

    child_base = 0
    base = 0
    sub = iota((r, 1), 0)
    for level in range(1, LEVELS + 1):
        child_base, base = base, base + leaves // (1 << (level - 1))
        node = leaf // (1 << level)
        rank_l = rank_ref[child_base + 2 * node]
        rank_r = rank_ref[child_base + 2 * node + 1]
        rank_p = rank_ref[base + node]
        spots_l = pk[level - 1, 0, :, width : width + LANES]
        spots_r = pk[level - 1, 1, :, width : width + LANES]
        row_r = spots_r.T
        d2 = None
        for axis in range(3):
            off = spots_l[:, axis : axis + 1] - row_r[axis : axis + 1, :]
            d2 = off * off if d2 is None else d2 + off * off
        cross = kern(d2)
        proj_l, proj_r = pp[0], pp[1]
        upper = (pk[level - 1, 0, :, 0:width] - mm(cross, proj_r, 1, 0, 3)) * jnp.where(sub < rank_l, 1.0, 0.0)
        lower = (pk[level - 1, 1, :, 0:width] - mm(cross, proj_l, 0, 0, 3)) * jnp.where(sub < rank_r, 1.0, 0.0)
        cand = jnp.concatenate([upper, lower], 0)
        spots = jnp.concatenate([spots_l, spots_r], 0)
        row = skel_ref[pl.ds(base + node, 1), :]
        chooser = jnp.where(jnp.broadcast_to(row, (2 * r, r)) == iota((2 * r, r), 0), 1.0, 0.0).astype(BF16)
        three = split(jnp.concatenate([cand, spots], 1), 3)
        chosen = bdot(jnp.concatenate([chooser] * 3, 0), jnp.concatenate(three, 0), 0, 0)
        picked = chosen[:, 0:width] * jnp.where(sub < rank_p, 1.0, 0.0)
        last = level == LEVELS
        if not last:
            side = sides[level]
            pk[level, side, :, 0:width] = picked
            pk[level, side, :, width : width + LANES] = chosen[:, width : width + LANES]
            offer(pk, level, 2, xk_s, xk_r)
        else:
            pk3[...] = picked
        raw = mm(cand, picked, 1, 1, 3)
        back = mm(raw, jnp.concatenate([proj_l, proj_r], 0), 0, 0)
        if not last:
            hh[level, side] = back
            offer(hh, level, 2, xh_s, xh_r)
        else:
            hh3[...] = back
        gram = ridged(mm(picked, picked, 1, 1, 3), rank_p)
        if not last:
            ww[level, side] = gram

            def hook(b, level=level):
                @pl.when(b == 4)
                def _():
                    relay(pk, level, 2, xk_s, xk_r, xkp_s, xkp_r)

            spd_inverse(ww.at[level, side], hook)
            offer(ww, level, 1, xw_s, xw_r)
            pp[side] = mm(ww[level, side], hh[level, side], 1, 0)
            relay(hh, level, 2, xh_s, xh_r, xhp_s, xhp_r)
            relay(ww, level, 1, xw_s, xw_r, xwp_s, xwp_r)
            settle(pk, level, 2, xkp_s, xkp_r)
            settle(hh, level, 2, xhp_s, xhp_r)
            settle(ww, level, 1, xwp_s, xwp_r)
            pp[1 - side] = mm(ww[level, 1 - side], hh[level, 1 - side], 1, 0)
        else:
            ww3[...] = gram
            spd_inverse(ww3, lambda b: None)
            share, span = top_s.shape
            turn = lax.rem(width - me * span, width)
            mine_rows = pl.ds(pl.multiple_of(lax.rem(leaf, 8) * share, share), share)
            top_s[...] = pltpu.roll(pk3[mine_rows, :], turn, 1)[:, 0:span]
            top_o[...] = pltpu.roll(mm(ww3[mine_rows, :], hh3[...], 1, 0), turn, 1)[:, 0:span]

    for copy in sends:
        copy.wait_send()
    for level in range(LEVELS):
        drain_relay(pk, level, 2, xkp_s, xkp_r)
        drain_relay(ww, level, 1, xwp_s, xwp_r)
        if level > 0:
            drain_relay(hh, level, 2, xhp_s, xhp_r)

    def drain(t, carry):
        same = zpeer(zorder(t)) * 2 + core
        put(every.at[same], every.at[same], gp_s.at[t], gp_r.at[t], keep=False, col=partner).wait_send()
        put(pick_rows(same), pick_rows(same), pp_s.at[t], pp_r.at[t], keep=False, col=partner).wait_send()
        return carry

    lax.fori_loop(1, ZS, drain, 0)


def local(points, point_ids, signs, hadamard_sample_rows, samples, skeleton, ranks):
    rows = points.shape[1]
    width = samples.shape[1]
    r = skeleton.shape[1]
    count = r // COLS
    shape = jax.ShapeDtypeStruct
    fetched = pltpu.VMEM
    sems = [DMA(()), *[DMA((ZS,))] * 8, DMA(()), DMA(()), *[DMA((ZS,))] * 10, *[DMA((LEVELS, 2))] * 12]
    return pl.pallas_call(
        hss_kernel,
        out_shape=[
            shape((rows, r), BF16),
            shape((r // 8, width // COLS), F32),
            shape((r // 8, width // COLS), F32),
        ],
        in_specs=[VM, VM, VM, VM, ANY, VM, SM],
        out_specs=[VM] * 3,
        scratch_shapes=[
            fetched((rows, width), BF16),
            fetched((COLS, 8, rows), F32),
            fetched((COLS, rows, width), BF16),
            fetched((3, rows, LANES), F32),
            fetched((3, count, LANES), F32),
            fetched((rows, width), F32),
            fetched((rows, r), F32),
            fetched((r, width), F32),
            fetched((r // 2, width), F32),
            fetched((r // 2, width), F32),
            fetched((ZS - 1, count, width), F32),
            fetched((LEVELS, 2, r, width + LANES), F32),
            fetched((LEVELS, 2, r, width), F32),
            fetched((LEVELS, 2, r, r), F32),
            fetched((2, r, width), F32),
            fetched((r, width), F32),
            fetched((r, width), F32),
            fetched((r, r), F32),
            *sems,
        ],
        compiler_params=pltpu.CompilerParams(collective_id=0, has_side_effects=True),
        name="hss",
    )(points, point_ids[None], signs[None], hadamard_sample_rows[None], samples, skeleton, ranks)


def solution(mesh):
    placed = (
        P(None, ("leaf", "col")),
        P(("leaf", "col")),
        P(("leaf", "col")),
        P(),
        P(("leaf", "col"), None),
        P(),
        P(),
    )
    return jax.shard_map(
        local,
        mesh=mesh,
        in_specs=placed,
        out_specs=(P(("leaf", "col"), None), P("leaf", "col"), P("leaf", "col")),
        check_vma=False,
    )
```

```python
import jax
import jax.numpy as jnp
from jax import lax
from jax.experimental import pallas as pl
from jax.experimental.pallas import tpu as pltpu
from jax.sharding import PartitionSpec as P

MESH = pl.DeviceIdType.MESH
DMA = pltpu.SemaphoreType.DMA
F32 = jnp.float32
BF16 = jnp.bfloat16
VM = pl.BlockSpec(memory_space=pltpu.VMEM)
SM = pl.BlockSpec(memory_space=pltpu.SMEM)
ANY = pl.BlockSpec(memory_space=pl.ANY)

NTOTAL = 1048576
KERNEL_SCALE = 1.0
RIDGE = 0.25
LOG2E = 1.4426950408889634
BITS = NTOTAL.bit_length() - 1
NBITS = 32
PANEL = 16
COLS = 16
ZS = COLS // 2
LANES = 128
LEVELS = 3


def bdot(a, b, ca, cb):
    return lax.dot_general(a, b, (((ca,), (cb,)), ((), ())), preferred_element_type=F32)


def split(x, count):
    pieces = []
    for _ in range(count - 1):
        piece = x.astype(BF16)
        pieces.append(piece)
        x = x - piece.astype(F32)
    return [*pieces, x.astype(BF16)]


def mm(a, b, ca, cb, terms=6):
    count = 3 if terms == 6 else 2
    pa, pb = split(a, count), split(b, count)
    pairs = [(i, j) for i in range(count) for j in range(count) if i + j < count]
    left = jnp.concatenate([pa[i] for i, _ in pairs], ca)
    right = jnp.concatenate([pb[j] for _, j in pairs], cb)
    return bdot(left, right, ca, cb)


def exact(a, b, ca, cb):
    pieces = split(a, 3)
    return bdot(jnp.concatenate(pieces, ca), jnp.concatenate([b] * 3, cb), ca, cb)


def iota(shape, axis):
    return lax.broadcasted_iota(jnp.int32, shape, axis)


def kern(squared_distance):
    return jnp.exp2(squared_distance * (-KERNEL_SCALE * LOG2E))


def spd_inverse(a_ref, hook):
    n = a_ref.shape[0]
    lane = iota((PANEL, n), 1)
    sub = iota((PANEL, n), 0)
    ident = (lane == sub).astype(F32)
    lane_n = iota((n, n), 1)

    def step(b, carry):
        start = pl.multiple_of(b * PANEL, PANEL)
        panel = a_ref[pl.ds(start, PANEL), :]
        rolled = pltpu.roll(panel, lax.rem(n - start, n), 1)
        diag = [jnp.broadcast_to(rolled[:, k : k + 1], (PANEL, n)) for k in range(PANEL)]
        rows = jnp.where(lane < PANEL, ident, rolled)
        for k in range(PANEL):
            inv = 1.0 / diag[k][k : k + 1, :]
            here = sub == k
            factor = diag[k] * inv
            for j in range(k + 1, PANEL):
                own = diag[j][k : k + 1, :]
                diag[j] = jnp.where(here, own * inv, diag[j] - factor * own)
            own = rows[k : k + 1, :]
            rows = jnp.where(here, own * inv, rows - factor * own)
        rows = pltpu.roll(rows, start, 1)
        side = jnp.where(lane < start, -panel, panel)
        side = jnp.where((lane >= start) & (lane < start + PANEL), 0.0, side)
        change = mm(side, rows, 0, 0)
        cleared = jnp.where((lane_n >= start) & (lane_n < start + PANEL), 0.0, a_ref[...])
        a_ref[...] = cleared - change
        a_ref[pl.ds(start, PANEL), :] = rows
        hook(b)
        return carry

    lax.fori_loop(0, n // PANEL, step, 0)


def ridged(gram, rank):
    n = gram.shape[0]
    same = iota((n, n), 0) == iota((n, n), 1)
    trace = jnp.sum(jnp.where(same, gram, 0.0), keepdims=True)
    shift = RIDGE * trace / rank.astype(F32) + 1e-06
    return gram + jnp.where(same, shift, 0.0)


def hss_kernel(
    points_ref, ids_ref, signs_ref, had_ref, samp_hbm, skel_ref, rank_ref,
    basis_ref, top_s, top_o,
    samp, every, om_all, own_b, pick_b, res, raw_ref, part, half, mine, landed, spk, pk, sp, hh, ww, pp, pk3, hh3, ww3,
    samp_sem, g_s, g_r, gp_s, gp_r, p_s, p_r, pp_s, pp_r,
    pair_s, pair_r, rs_s, rs_r, ag_s, ag_r, ap_s, ap_r, ax_s, ax_r, axp_s, axp_r,
    xs_s, xs_r, xk_s, xk_r, xkp_s, xkp_r, xh_s, xh_r, xhp_s, xhp_r, xw_s, xw_r, xwp_s, xwp_r,
):
    leaf = lax.axis_index("leaf")
    me = lax.axis_index("col")
    leaves = lax.axis_size("leaf")
    core = lax.rem(me, 2)
    z = me // 2
    partner = me + 1 - 2 * core
    rows = points_ref.shape[1]
    width = had_ref.shape[1]
    r = skel_ref.shape[1]
    count = r // COLS
    sides = [lax.rem(leaf // (1 << lvl), 2) for lvl in range(LEVELS)]
    siblings = [leaf + (1 << lvl) - (2 << lvl) * sides[lvl] for lvl in range(LEVELS)]
    sends = []

    def put(src, dst, send, recv, keep=True, **device):
        copy = pltpu.make_async_remote_copy(
            src_ref=src, dst_ref=dst, send_sem=send, recv_sem=recv, device_id=device, device_id_type=MESH
        )
        if keep:
            sends.append(copy)
        return copy

    def zpeer(off):
        return lax.rem(z + off, ZS)

    fetch = pltpu.make_async_copy(samp_hbm, samp, samp_sem)
    fetch.start()
    barrier = pltpu.get_barrier_semaphore()
    for off in range(1, ZS):
        pl.semaphore_signal(barrier, inc=1, device_id={"col": zpeer(off) * 2 + core}, device_id_type=MESH)
    pl.semaphore_signal(barrier, inc=1, device_id={"col": partner}, device_id_type=MESH)
    for sibling in siblings:
        pl.semaphore_signal(barrier, inc=1, device_id={"leaf": sibling}, device_id_type=MESH)
    every[me, 0:3, :] = points_ref[...]
    every[me, 3:4, :] = ids_ref[...].astype(F32)
    every[me, 4:5, :] = signs_ref[...].astype(F32)
    every[me, 5:8, :] = jnp.zeros((3, rows), F32)

    my_rows = pl.ds(pl.multiple_of(me * count, count), count)
    entry = skel_ref[pl.ds(leaf, 1), :]

    def chooser_of(slot):
        return jnp.where(
            jnp.broadcast_to(entry - slot * rows, (rows, r)) == iota((rows, r), 0), 1.0, 0.0
        ).astype(BF16)

    fetch.wait()
    part[...] = bdot(chooser_of(me), samp[...], 0, 0)
    spk[my_rows, :] = part[my_rows, :]

    ident = (iota((8, LANES), 0) == iota((8, LANES), 1)).astype(BF16)
    own_cols = exact(every[me], ident, 0, 0)
    for axis in range(3):
        own_b[axis] = jnp.broadcast_to(own_cols[:, axis : axis + 1], (rows, LANES))
    bit_row = iota((NBITS, width), 0)
    had = jnp.broadcast_to(had_ref[...], (NBITS, width))
    had_bits = ((had >> jnp.minimum(bit_row, BITS)) & 1).astype(F32) * 0.5
    had_bits = jnp.where(bit_row == BITS, 0.5, jnp.where(bit_row == BITS + 1, 0.25, had_bits))
    had_bits = jnp.where(bit_row > BITS + 1, 0.0, had_bits).astype(BF16)
    res[...] = samp[...].astype(F32)
    pl.semaphore_wait(barrier, ZS + LEVELS)

    def pick_rows(slot):
        return spk.at[pl.ds(pl.multiple_of(slot * count, count), count)]

    order = (1, 7, 2, 6, 3, 5, 4)
    for off in order:
        put(every.at[me], every.at[me], g_s.at[off], g_r.at[ZS - off], col=zpeer(off) * 2 + core).start()
    put(every.at[me], every.at[me], gp_s.at[0], gp_r.at[0], col=partner).start()
    for off in order:
        put(pick_rows(me), pick_rows(me), p_s.at[off], p_r.at[ZS - off], col=zpeer(off) * 2 + core).start()
    put(pick_rows(me), pick_rows(me), pp_s.at[0], pp_r.at[0], col=partner).start()

    def omega4(block):
        shift = iota((NBITS, rows), 0)
        ids = jnp.broadcast_to(block[3:4, :].astype(jnp.int32), (NBITS, rows))
        bits = ((ids >> jnp.minimum(shift, BITS)) & 1).astype(F32)
        bits = jnp.where(shift == BITS, 1.0 - block[4:5, :], bits)
        bits = jnp.where(shift == BITS + 1, 1.0, bits)
        bits = jnp.where(shift > BITS + 1, 0.0, bits).astype(BF16)
        halves = bdot(bits, had_bits, 0, 0)
        return (halves - jnp.round(halves)).astype(BF16)

    def zorder(t):
        return lax.rem(jnp.where(lax.rem(t, 2) == 1, (t + 1) // 2, ZS - t // 2), ZS)

    def tile_of(columns, block):
        tiles = []
        for c in range(rows // LANES):
            d2 = None
            for axis in range(3):
                off = columns[axis] - block[axis : axis + 1, c * LANES : (c + 1) * LANES]
                d2 = off * off if d2 is None else d2 + off * off
            tiles.append(kern(d2).astype(BF16))
        return jnp.concatenate(tiles, 1)

    def near_step(t, spots):
        off = zorder(t)
        there = zpeer(off)
        same = there * 2 + core
        other = there * 2 + 1 - core

        @pl.when(t > 0)
        def _():
            put(every.at[same], every.at[same], g_s.at[off], g_r.at[off], keep=False, col=partner).wait_recv()
            put(every.at[same], every.at[same], gp_s.at[t], gp_r.at[t], keep=False, col=partner).start()

        put(every.at[other], every.at[other], gp_s.at[t], gp_r.at[t], keep=False, col=partner).wait_recv()
        columns = [own_b[axis] for axis in range(3)]
        tiles, omegas = [], []
        for k in range(2):
            block = every[there * 2 + k]
            spots = spots + exact(block, chooser_of(there * 2 + k), 1, 0)
            om = omega4(block)
            om_all[there * 2 + k] = om
            omegas.append(om)
            tiles.append(tile_of(columns, block))
        res[...] -= 0.25 * bdot(jnp.concatenate(tiles, 1), jnp.concatenate(omegas, 0), 1, 0)

        @pl.when(t > 0)
        def _():
            put(pick_rows(same), pick_rows(same), p_s.at[off], p_r.at[off], keep=False, col=partner).wait_recv()
            put(pick_rows(same), pick_rows(same), pp_s.at[t], pp_r.at[t], keep=False, col=partner).start()

        return spots

    spots = lax.fori_loop(0, ZS, near_step, jnp.zeros((8, r), F32))
    sp[0, sides[0]] = spots
    put(sp.at[0, sides[0]], sp.at[0, sides[0]], xs_s.at[0], xs_r.at[0], leaf=siblings[0]).start()

    spot_cols = exact(spots, ident, 0, 0)
    for axis in range(3):
        pick_b[axis] = jnp.broadcast_to(spot_cols[:, axis : axis + 1], (r, LANES))
    part[...] = jnp.zeros((r, width), F32)

    def pick_step(t, carry):
        there = zpeer(zorder(t))
        other = there * 2 + 1 - core
        columns = [pick_b[axis] for axis in range(3)]
        tile = jnp.concatenate([tile_of(columns, every[there * 2 + k]) for k in range(2)], 1)
        part[...] += bdot(tile, om_all[pl.ds(there * 2, 2)].reshape(2 * rows, width), 1, 0)
        put(pick_rows(other), pick_rows(other), pp_s.at[t], pp_r.at[t], keep=False, col=partner).wait_recv()
        return carry

    lax.fori_loop(0, ZS, pick_step, 0)
    sub = iota((r, 1), 0)
    pk[0, sides[0]] = (spk[...] - 0.25 * part[...]) * jnp.where(sub < rank_ref[leaf], 1.0, 0.0)

    def pieces(buf, level, side, chunks, half_of):
        size = r // 2 // chunks
        return [buf.at[level, side, pl.ds(pl.multiple_of(half_of * (r // 2) + q * size, size), size)] for q in range(chunks)]

    def offer(buf, level, chunks, s, rv):
        for q, piece in enumerate(pieces(buf, level, sides[level], chunks, core)):
            put(piece, piece, s.at[level, q], rv.at[level, q], leaf=siblings[level]).start()

    def relay(buf, level, chunks, s, rv, s2, rv2):
        for q, piece in enumerate(pieces(buf, level, 1 - sides[level], chunks, core)):
            put(piece, piece, s.at[level, q], rv.at[level, q], keep=False, leaf=siblings[level]).wait_recv()
            put(piece, piece, s2.at[level, q], rv2.at[level, q], keep=False, col=partner).start()

    def settle(buf, level, chunks, s2, rv2):
        for q, piece in enumerate(pieces(buf, level, 1 - sides[level], chunks, 1 - core)):
            put(piece, piece, s2.at[level, q], rv2.at[level, q], keep=False, col=partner).wait_recv()

    def hear(level):
        got = sp.at[level, 1 - sides[level]]
        put(got, got, xs_s.at[level], xs_r.at[level], keep=False, leaf=siblings[level]).wait_recv()

    def drain_relay(buf, level, chunks, s2, rv2):
        for q, piece in enumerate(pieces(buf, level, 1 - sides[level], chunks, core)):
            put(piece, piece, s2.at[level, q], rv2.at[level, q], keep=False, col=partner).wait_send()

    offer(pk, 0, 2, xk_s, xk_r)

    side0 = sides[0]
    picked = pk[0, side0]
    raw = mm(res[...], picked, 1, 1)
    raw_ref[...] = raw
    om_own = om_all[me]
    part[...] = 0.25 * exact(raw, om_own, 0, 0)
    r2 = r // 2
    own0 = pl.multiple_of(core * r2, r2)
    other0 = pl.multiple_of((1 - core) * r2, r2)
    pair = put(part.at[pl.ds(other0, r2)], half, pair_s, pair_r, col=partner)
    pair.start()
    ww[0, side0] = ridged(mm(picked, picked, 1, 1), rank_ref[leaf])
    scatter = []
    for off in range(1, ZS):
        piece = pl.ds(pl.multiple_of(zpeer(off) * count, count), count)
        scatter.append(put(mine.at[piece], landed.at[off - 1], rs_s.at[off], rs_r.at[off], col=zpeer(off) * 2 + core))

    def leaf_hook(b):
        @pl.when(b == 2)
        def _():
            pair.wait_recv()
            mine[...] = part[pl.ds(own0, r2)] + half[...]
            for copy in scatter:
                copy.start()

        @pl.when(b == 6)
        def _():
            relay(pk, 0, 2, xk_s, xk_r, xkp_s, xkp_r)

    spd_inverse(ww.at[0, side0], leaf_hook)
    offer(ww, 0, 1, xw_s, xw_r)
    basis_ref[...] = mm(raw_ref[...], ww[0, side0], 1, 0).astype(BF16)

    def n_rows(side, half_of, chip):
        return hh.at[0, side, pl.ds(pl.multiple_of(half_of * r2 + chip * count, count), count)]

    total = mine[pl.ds(pl.multiple_of(z * count, count), count)]
    for off in range(1, ZS):
        scatter[off - 1].wait_recv()
        total = total + landed[off - 1]
    hh[0, side0, pl.ds(pl.multiple_of(own0 + z * count, count), count)] = total
    here = n_rows(side0, core, z)
    for off in (1, 7, 2, 6, 3, 5, 4):
        put(here, here, ag_s.at[off], ag_r.at[ZS - off], col=zpeer(off) * 2 + core).start()
    put(here, here, ap_s.at[0], ap_r.at[0], col=partner).start()
    put(here, here, ax_s.at[0], ax_r.at[0], leaf=siblings[0]).start()
    for off in (1, 7, 2, 6, 3, 5, 4):
        got = n_rows(side0, core, zpeer(off))
        put(got, got, ag_s.at[off], ag_r.at[off], keep=False, col=partner).wait_recv()
        put(got, got, ap_s.at[off], ap_r.at[off], col=partner).start()
        put(got, got, ax_s.at[off], ax_r.at[off], leaf=siblings[0]).start()
    relay(ww, 0, 1, xw_s, xw_r, xwp_s, xwp_r)
    for off in (0, 1, 7, 2, 6, 3, 5, 4):
        got = n_rows(1 - side0, core, zpeer(off))
        put(got, got, ax_s.at[off], ax_r.at[off], keep=False, leaf=siblings[0]).wait_recv()
        put(got, got, axp_s.at[off], axp_r.at[off], col=partner).start()
    for off in range(ZS):
        got = n_rows(side0, 1 - core, zpeer(off))
        put(got, got, ap_s.at[off], ap_r.at[off], keep=False, col=partner).wait_recv()
    pp[side0] = mm(ww[0, side0], hh[0, side0], 1, 0)
    settle(pk, 0, 2, xkp_s, xkp_r)
    hear(0)
    settle(ww, 0, 1, xwp_s, xwp_r)
    for off in range(ZS):
        got = n_rows(1 - side0, 1 - core, zpeer(off))
        put(got, got, axp_s.at[off], axp_r.at[off], keep=False, col=partner).wait_recv()
    pp[1 - side0] = mm(ww[0, 1 - side0], hh[0, 1 - side0], 1, 0)

    child_base = 0
    base = 0
    for level in range(1, LEVELS + 1):
        child_base, base = base, base + leaves // (1 << (level - 1))
        node = leaf // (1 << level)
        rank_l = rank_ref[child_base + 2 * node]
        rank_r = rank_ref[child_base + 2 * node + 1]
        rank_p = rank_ref[base + node]
        spots_l = exact(sp[level - 1, 0], ident, 0, 0)
        row_r = sp[level - 1, 1]
        d2 = None
        for axis in range(3):
            off = spots_l[:, axis : axis + 1] - row_r[axis : axis + 1, :]
            d2 = off * off if d2 is None else d2 + off * off
        cross = kern(d2)
        proj_l, proj_r = pp[0], pp[1]
        upper = (pk[level - 1, 0] - mm(cross, proj_r, 1, 0, 3)) * jnp.where(sub < rank_l, 1.0, 0.0)
        lower = (pk[level - 1, 1] - mm(cross, proj_l, 0, 0, 3)) * jnp.where(sub < rank_r, 1.0, 0.0)
        cand = jnp.concatenate([upper, lower], 0)
        spots = jnp.concatenate([sp[level - 1, 0], row_r], 1)
        row = skel_ref[pl.ds(base + node, 1), :]
        chooser = jnp.where(jnp.broadcast_to(row, (2 * r, r)) == iota((2 * r, r), 0), 1.0, 0.0).astype(BF16)
        three = split(cand, 3)
        chosen = bdot(jnp.concatenate([chooser] * 3, 0), jnp.concatenate(three, 0), 0, 0)
        picked = chosen * jnp.where(sub < rank_p, 1.0, 0.0)
        last = level == LEVELS
        if not last:
            side = sides[level]
            pk[level, side] = picked
            sp[level, side] = exact(spots, chooser, 1, 0)
            offer(pk, level, 2, xk_s, xk_r)
            put(sp.at[level, side], sp.at[level, side], xs_s.at[level], xs_r.at[level], leaf=siblings[level]).start()
        else:
            pk3[...] = picked
        raw = mm(cand, picked, 1, 1, 3)
        back = mm(raw, jnp.concatenate([proj_l, proj_r], 0), 0, 0)
        if not last:
            hh[level, side] = back
            offer(hh, level, 2, xh_s, xh_r)
        else:
            hh3[...] = back
        gram = ridged(mm(picked, picked, 1, 1, 3), rank_p)
        if not last:
            ww[level, side] = gram

            def hook(b, level=level):
                @pl.when(b == 4)
                def _():
                    relay(pk, level, 2, xk_s, xk_r, xkp_s, xkp_r)

            spd_inverse(ww.at[level, side], hook)
            offer(ww, level, 1, xw_s, xw_r)
            pp[side] = mm(ww[level, side], hh[level, side], 1, 0)
            relay(hh, level, 2, xh_s, xh_r, xhp_s, xhp_r)
            relay(ww, level, 1, xw_s, xw_r, xwp_s, xwp_r)
            settle(pk, level, 2, xkp_s, xkp_r)
            hear(level)
            settle(hh, level, 2, xhp_s, xhp_r)
            settle(ww, level, 1, xwp_s, xwp_r)
            pp[1 - side] = mm(ww[level, 1 - side], hh[level, 1 - side], 1, 0)
        else:
            ww3[...] = gram
            spd_inverse(ww3, lambda b: None)
            share, span = top_s.shape
            turn = lax.rem(width - me * span, width)
            mine_rows = pl.ds(pl.multiple_of(lax.rem(leaf, 8) * share, share), share)
            top_s[...] = pltpu.roll(pk3[mine_rows, :], turn, 1)[:, 0:span]
            top_o[...] = pltpu.roll(mm(ww3[mine_rows, :], hh3[...], 1, 0), turn, 1)[:, 0:span]

    for copy in sends:
        copy.wait_send()
    for level in range(LEVELS):
        drain_relay(pk, level, 2, xkp_s, xkp_r)
        drain_relay(ww, level, 1, xwp_s, xwp_r)
        if level > 0:
            drain_relay(hh, level, 2, xhp_s, xhp_r)

    def drain(t, carry):
        same = zpeer(zorder(t)) * 2 + core
        put(every.at[same], every.at[same], gp_s.at[t], gp_r.at[t], keep=False, col=partner).wait_send()
        put(pick_rows(same), pick_rows(same), pp_s.at[t], pp_r.at[t], keep=False, col=partner).wait_send()
        return carry

    lax.fori_loop(1, ZS, drain, 0)


def local(points, point_ids, signs, hadamard_sample_rows, samples, skeleton, ranks):
    rows = points.shape[1]
    width = samples.shape[1]
    r = skeleton.shape[1]
    count = r // COLS
    shape = jax.ShapeDtypeStruct
    fetched = pltpu.VMEM
    sems = [DMA(()), *[DMA((ZS,))] * 8, DMA(()), DMA(()), *[DMA((ZS,))] * 10, *[DMA((LEVELS,))] * 2, *[DMA((LEVELS, 2))] * 12]
    return pl.pallas_call(
        hss_kernel,
        out_shape=[
            shape((rows, r), BF16),
            shape((r // 8, width // COLS), F32),
            shape((r // 8, width // COLS), F32),
        ],
        in_specs=[VM, VM, VM, VM, ANY, VM, SM],
        out_specs=[VM] * 3,
        scratch_shapes=[
            fetched((rows, width), BF16),
            fetched((COLS, 8, rows), F32),
            fetched((COLS, rows, width), BF16),
            fetched((3, rows, LANES), F32),
            fetched((3, r, LANES), F32),
            fetched((rows, width), F32),
            fetched((rows, r), F32),
            fetched((r, width), F32),
            fetched((r // 2, width), F32),
            fetched((r // 2, width), F32),
            fetched((ZS - 1, count, width), F32),
            fetched((r, width), F32),
            fetched((LEVELS, 2, r, width), F32),
            fetched((LEVELS, 2, 8, r), F32),
            fetched((LEVELS, 2, r, width), F32),
            fetched((LEVELS, 2, r, r), F32),
            fetched((2, r, width), F32),
            fetched((r, width), F32),
            fetched((r, width), F32),
            fetched((r, r), F32),
            *sems,
        ],
        compiler_params=pltpu.CompilerParams(collective_id=0, has_side_effects=True),
        name="hss",
    )(points, point_ids[None], signs[None], hadamard_sample_rows[None], samples, skeleton, ranks)


def solution(mesh):
    placed = (
        P(None, ("leaf", "col")),
        P(("leaf", "col")),
        P(("leaf", "col")),
        P(),
        P(("leaf", "col"), None),
        P(),
        P(),
    )
    return jax.shard_map(
        local,
        mesh=mesh,
        in_specs=placed,
        out_specs=(P(("leaf", "col"), None), P("leaf", "col"), P("leaf", "col")),
        check_vma=False,
    )
```

```python
import jax
import jax.numpy as jnp
from jax import lax
from jax.experimental import pallas as pl
from jax.experimental.pallas import tpu as pltpu
from jax.sharding import PartitionSpec as P

MESH = pl.DeviceIdType.MESH
DMA = pltpu.SemaphoreType.DMA
F32 = jnp.float32
BF16 = jnp.bfloat16
VM = pl.BlockSpec(memory_space=pltpu.VMEM)
SM = pl.BlockSpec(memory_space=pltpu.SMEM)
ANY = pl.BlockSpec(memory_space=pl.ANY)

NTOTAL = 1048576
KERNEL_SCALE = 1.0
RIDGE = 0.25
LOG2E = 1.4426950408889634
BITS = NTOTAL.bit_length() - 1
NBITS = 32
PANEL = 16
COLS = 16
ZS = COLS // 2
LANES = 128
LEVELS = 3


def bdot(a, b, ca, cb):
    return lax.dot_general(a, b, (((ca,), (cb,)), ((), ())), preferred_element_type=F32)


def split(x, count):
    pieces = []
    for _ in range(count - 1):
        piece = x.astype(BF16)
        pieces.append(piece)
        x = x - piece.astype(F32)
    return [*pieces, x.astype(BF16)]


def mm(a, b, ca, cb, terms=6):
    count = 3 if terms == 6 else 2
    pa, pb = split(a, count), split(b, count)
    pairs = [(i, j) for i in range(count) for j in range(count) if i + j < count]
    left = jnp.concatenate([pa[i] for i, _ in pairs], ca)
    right = jnp.concatenate([pb[j] for _, j in pairs], cb)
    return bdot(left, right, ca, cb)


def exact(a, b, ca, cb):
    pieces = split(a, 3)
    return bdot(jnp.concatenate(pieces, ca), jnp.concatenate([b] * 3, cb), ca, cb)


def iota(shape, axis):
    return lax.broadcasted_iota(jnp.int32, shape, axis)


def kern(squared_distance):
    return jnp.exp2(squared_distance * (-KERNEL_SCALE * LOG2E))


def spd_inverse(a_ref, hook):
    n = a_ref.shape[0]
    lane = iota((PANEL, n), 1)
    sub = iota((PANEL, n), 0)
    ident = (lane == sub).astype(F32)
    lane_n = iota((n, n), 1)

    def step(b, carry):
        start = pl.multiple_of(b * PANEL, PANEL)
        panel = a_ref[pl.ds(start, PANEL), :]
        rolled = pltpu.roll(panel, lax.rem(n - start, n), 1)
        diag = [jnp.broadcast_to(rolled[:, k : k + 1], (PANEL, n)) for k in range(PANEL)]
        rows = jnp.where(lane < PANEL, ident, rolled)
        for k in range(PANEL):
            inv = 1.0 / diag[k][k : k + 1, :]
            here = sub == k
            factor = diag[k] * inv
            for j in range(k + 1, PANEL):
                own = diag[j][k : k + 1, :]
                diag[j] = jnp.where(here, own * inv, diag[j] - factor * own)
            own = rows[k : k + 1, :]
            rows = jnp.where(here, own * inv, rows - factor * own)
        rows = pltpu.roll(rows, start, 1)
        side = jnp.where(lane < start, -panel, panel)
        side = jnp.where((lane >= start) & (lane < start + PANEL), 0.0, side)
        change = mm(side, rows, 0, 0)
        cleared = jnp.where((lane_n >= start) & (lane_n < start + PANEL), 0.0, a_ref[...])
        a_ref[...] = cleared - change
        a_ref[pl.ds(start, PANEL), :] = rows
        hook(b)
        return carry

    lax.fori_loop(0, n // PANEL, step, 0)


def ridged(gram, rank):
    n = gram.shape[0]
    same = iota((n, n), 0) == iota((n, n), 1)
    trace = jnp.sum(jnp.where(same, gram, 0.0), keepdims=True)
    shift = RIDGE * trace / rank.astype(F32) + 1e-06
    return gram + jnp.where(same, shift, 0.0)


def hss_kernel(
    points_ref, ids_ref, signs_ref, had_ref, samp_hbm, skel_ref, rank_ref,
    basis_ref, top_s, top_o,
    samp, every, om_all, own_b, pick_b, res, raw_ref, part, half, mine, landed, spk, pk, sp, hh, ww, pp, pk3, hh3, ww3,
    samp_sem, g_s, g_r, gp_s, gp_r, p_s, p_r, pp_s, pp_r,
    pair_s, pair_r, rs_s, rs_r, ag_s, ag_r, ap_s, ap_r, ax_s, ax_r, axp_s, axp_r,
    xs_s, xs_r, xk_s, xk_r, xkp_s, xkp_r, xh_s, xh_r, xhp_s, xhp_r, xw_s, xw_r, xwp_s, xwp_r,
):
    leaf = lax.axis_index("leaf")
    me = lax.axis_index("col")
    leaves = lax.axis_size("leaf")
    core = lax.rem(me, 2)
    z = me // 2
    partner = me + 1 - 2 * core
    rows = points_ref.shape[1]
    width = had_ref.shape[1]
    r = skel_ref.shape[1]
    count = r // COLS
    sides = [lax.rem(leaf // (1 << lvl), 2) for lvl in range(LEVELS)]
    siblings = [leaf + (1 << lvl) - (2 << lvl) * sides[lvl] for lvl in range(LEVELS)]
    sends = []

    def put(src, dst, send, recv, keep=True, **device):
        copy = pltpu.make_async_remote_copy(
            src_ref=src, dst_ref=dst, send_sem=send, recv_sem=recv, device_id=device, device_id_type=MESH
        )
        if keep:
            sends.append(copy)
        return copy

    def zpeer(off):
        return lax.rem(z + off, ZS)

    fetch = pltpu.make_async_copy(samp_hbm, samp, samp_sem)
    fetch.start()
    barrier = pltpu.get_barrier_semaphore()
    for off in range(1, ZS):
        pl.semaphore_signal(barrier, inc=1, device_id={"col": zpeer(off) * 2 + core}, device_id_type=MESH)
    pl.semaphore_signal(barrier, inc=1, device_id={"col": partner}, device_id_type=MESH)
    for sibling in siblings:
        pl.semaphore_signal(barrier, inc=1, device_id={"leaf": sibling}, device_id_type=MESH)
    every[me, 0:3, :] = points_ref[...]
    every[me, 3:4, :] = ids_ref[...].astype(F32)
    every[me, 4:5, :] = signs_ref[...].astype(F32)
    every[:, 5:8, :] = jnp.zeros((COLS, 3, rows), F32)

    my_rows = pl.ds(pl.multiple_of(me * count, count), count)
    entry = skel_ref[pl.ds(leaf, 1), :]

    def chooser_of(slot):
        return jnp.where(
            jnp.broadcast_to(entry - slot * rows, (rows, r)) == iota((rows, r), 0), 1.0, 0.0
        ).astype(BF16)

    fetch.wait()
    part[...] = bdot(chooser_of(me), samp[...], 0, 0)
    spk[my_rows, :] = part[my_rows, :]

    ident = (iota((8, LANES), 0) == iota((8, LANES), 1)).astype(BF16)
    own_cols = exact(every[me], ident, 0, 0)
    for axis in range(3):
        own_b[axis] = jnp.broadcast_to(own_cols[:, axis : axis + 1], (rows, LANES))
    bit_row = iota((NBITS, width), 0)
    had = jnp.broadcast_to(had_ref[...], (NBITS, width))
    had_bits = ((had >> jnp.minimum(bit_row, BITS)) & 1).astype(F32) * 0.5
    had_bits = jnp.where(bit_row == BITS, 0.5, jnp.where(bit_row == BITS + 1, 0.25, had_bits))
    had_bits = jnp.where(bit_row > BITS + 1, 0.0, had_bits).astype(BF16)
    res[...] = samp[...].astype(F32)
    pl.semaphore_wait(barrier, ZS + LEVELS)

    def pick_rows(slot):
        return spk.at[pl.ds(pl.multiple_of(slot * count, count), count)]

    def block_of(slot):
        return every.at[slot, pl.ds(0, 5)]

    order = (1, 7, 2, 6, 3, 5, 4)
    for off in order:
        put(block_of(me), block_of(me), g_s.at[off], g_r.at[ZS - off], col=zpeer(off) * 2 + core).start()
    put(block_of(me), block_of(me), gp_s.at[0], gp_r.at[0], col=partner).start()
    for off in order:
        put(pick_rows(me), pick_rows(me), p_s.at[off], p_r.at[ZS - off], col=zpeer(off) * 2 + core).start()
    put(pick_rows(me), pick_rows(me), pp_s.at[0], pp_r.at[0], col=partner).start()

    def omega4(block):
        shift = iota((NBITS, rows), 0)
        ids = jnp.broadcast_to(block[3:4, :].astype(jnp.int32), (NBITS, rows))
        bits = ((ids >> jnp.minimum(shift, BITS)) & 1).astype(F32)
        bits = jnp.where(shift == BITS, 1.0 - block[4:5, :], bits)
        bits = jnp.where(shift == BITS + 1, 1.0, bits)
        bits = jnp.where(shift > BITS + 1, 0.0, bits).astype(BF16)
        halves = bdot(bits, had_bits, 0, 0)
        return (halves - jnp.round(halves)).astype(BF16)

    def zorder(t):
        return lax.rem(jnp.where(lax.rem(t, 2) == 1, (t + 1) // 2, ZS - t // 2), ZS)

    def tile_of(columns, block):
        tiles = []
        for c in range(rows // LANES):
            d2 = None
            for axis in range(3):
                off = columns[axis] - block[axis : axis + 1, c * LANES : (c + 1) * LANES]
                d2 = off * off if d2 is None else d2 + off * off
            tiles.append(kern(d2).astype(BF16))
        return jnp.concatenate(tiles, 1)

    def near_step(t, spots):
        off = zorder(t)
        there = zpeer(off)
        same = there * 2 + core
        other = there * 2 + 1 - core

        @pl.when(t > 0)
        def _():
            put(block_of(same), block_of(same), g_s.at[off], g_r.at[off], keep=False, col=partner).wait_recv()
            put(block_of(same), block_of(same), gp_s.at[t], gp_r.at[t], keep=False, col=partner).start()

        put(block_of(other), block_of(other), gp_s.at[t], gp_r.at[t], keep=False, col=partner).wait_recv()
        columns = [own_b[axis] for axis in range(3)]
        tiles, omegas = [], []
        for k in range(2):
            block = every[there * 2 + k]
            spots = spots + exact(block, chooser_of(there * 2 + k), 1, 0)
            om = omega4(block)
            om_all[there * 2 + k] = om
            omegas.append(om)
            tiles.append(tile_of(columns, block))
        res[...] -= 0.25 * bdot(jnp.concatenate(tiles, 1), jnp.concatenate(omegas, 0), 1, 0)

        return spots

    spots = lax.fori_loop(0, ZS, near_step, jnp.zeros((8, r), F32))
    sp[0, sides[0]] = spots
    put(sp.at[0, sides[0]], sp.at[0, sides[0]], xs_s.at[0], xs_r.at[0], leaf=siblings[0]).start()

    spot_cols = exact(spots, ident, 0, 0)
    for axis in range(3):
        pick_b[axis] = jnp.broadcast_to(spot_cols[:, axis : axis + 1], (r, LANES))
    part[...] = jnp.zeros((r, width), F32)

    def pick_relay(t, carry):
        off = zorder(t)
        same = zpeer(off) * 2 + core
        put(pick_rows(same), pick_rows(same), p_s.at[off], p_r.at[off], keep=False, col=partner).wait_recv()
        put(pick_rows(same), pick_rows(same), pp_s.at[t], pp_r.at[t], keep=False, col=partner).start()
        return carry

    lax.fori_loop(1, ZS, pick_relay, 0)

    def pick_step(t, carry):
        there = zpeer(zorder(t))
        columns = [pick_b[axis] for axis in range(3)]
        tile = jnp.concatenate([tile_of(columns, every[there * 2 + k]) for k in range(2)], 1)
        part[...] += bdot(tile, om_all[pl.ds(there * 2, 2)].reshape(2 * rows, width), 1, 0)
        return carry

    lax.fori_loop(0, ZS, pick_step, 0)

    def pick_settle(t, carry):
        other = zpeer(zorder(t)) * 2 + 1 - core
        put(pick_rows(other), pick_rows(other), pp_s.at[t], pp_r.at[t], keep=False, col=partner).wait_recv()
        return carry

    lax.fori_loop(0, ZS, pick_settle, 0)
    sub = iota((r, 1), 0)
    pk[0, sides[0]] = (spk[...] - 0.25 * part[...]) * jnp.where(sub < rank_ref[leaf], 1.0, 0.0)

    def pieces(buf, level, side, chunks, half_of):
        size = r // 2 // chunks
        return [buf.at[level, side, pl.ds(pl.multiple_of(half_of * (r // 2) + q * size, size), size)] for q in range(chunks)]

    def offer(buf, level, chunks, s, rv):
        for q, piece in enumerate(pieces(buf, level, sides[level], chunks, core)):
            put(piece, piece, s.at[level, q], rv.at[level, q], leaf=siblings[level]).start()

    def relay(buf, level, chunks, s, rv, s2, rv2):
        for q, piece in enumerate(pieces(buf, level, 1 - sides[level], chunks, core)):
            put(piece, piece, s.at[level, q], rv.at[level, q], keep=False, leaf=siblings[level]).wait_recv()
            put(piece, piece, s2.at[level, q], rv2.at[level, q], keep=False, col=partner).start()

    def settle(buf, level, chunks, s2, rv2):
        for q, piece in enumerate(pieces(buf, level, 1 - sides[level], chunks, 1 - core)):
            put(piece, piece, s2.at[level, q], rv2.at[level, q], keep=False, col=partner).wait_recv()

    def hear(level):
        got = sp.at[level, 1 - sides[level]]
        put(got, got, xs_s.at[level], xs_r.at[level], keep=False, leaf=siblings[level]).wait_recv()

    def drain_relay(buf, level, chunks, s2, rv2):
        for q, piece in enumerate(pieces(buf, level, 1 - sides[level], chunks, core)):
            put(piece, piece, s2.at[level, q], rv2.at[level, q], keep=False, col=partner).wait_send()

    offer(pk, 0, 2, xk_s, xk_r)

    side0 = sides[0]
    picked = pk[0, side0]
    raw = mm(res[...], picked, 1, 1)
    raw_ref[...] = raw
    om_own = om_all[me]
    part[...] = 0.25 * exact(raw, om_own, 0, 0)
    r2 = r // 2
    own0 = pl.multiple_of(core * r2, r2)
    other0 = pl.multiple_of((1 - core) * r2, r2)
    pair = put(part.at[pl.ds(other0, r2)], half, pair_s, pair_r, col=partner)
    pair.start()
    ww[0, side0] = ridged(mm(picked, picked, 1, 1), rank_ref[leaf])
    scatter = []
    for off in range(1, ZS):
        piece = pl.ds(pl.multiple_of(zpeer(off) * count, count), count)
        scatter.append(put(mine.at[piece], landed.at[off - 1], rs_s.at[off], rs_r.at[off], col=zpeer(off) * 2 + core))

    def leaf_hook(b):
        @pl.when(b == 2)
        def _():
            pair.wait_recv()
            mine[...] = part[pl.ds(own0, r2)] + half[...]
            for copy in scatter:
                copy.start()

        @pl.when(b == 6)
        def _():
            relay(pk, 0, 2, xk_s, xk_r, xkp_s, xkp_r)

    spd_inverse(ww.at[0, side0], leaf_hook)
    offer(ww, 0, 1, xw_s, xw_r)
    basis_ref[...] = mm(raw_ref[...], ww[0, side0], 1, 0).astype(BF16)

    def n_rows(side, half_of, chip):
        return hh.at[0, side, pl.ds(pl.multiple_of(half_of * r2 + chip * count, count), count)]

    total = mine[pl.ds(pl.multiple_of(z * count, count), count)]
    for off in range(1, ZS):
        scatter[off - 1].wait_recv()
        total = total + landed[off - 1]
    hh[0, side0, pl.ds(pl.multiple_of(own0 + z * count, count), count)] = total
    here = n_rows(side0, core, z)
    for off in (1, 7, 2, 6, 3, 5, 4):
        put(here, here, ag_s.at[off], ag_r.at[ZS - off], col=zpeer(off) * 2 + core).start()
    put(here, here, ap_s.at[0], ap_r.at[0], col=partner).start()
    put(here, here, ax_s.at[0], ax_r.at[0], leaf=siblings[0]).start()
    for off in (1, 7, 2, 6, 3, 5, 4):
        got = n_rows(side0, core, zpeer(off))
        put(got, got, ag_s.at[off], ag_r.at[off], keep=False, col=partner).wait_recv()
        put(got, got, ap_s.at[off], ap_r.at[off], col=partner).start()
        put(got, got, ax_s.at[off], ax_r.at[off], leaf=siblings[0]).start()
    relay(ww, 0, 1, xw_s, xw_r, xwp_s, xwp_r)
    for off in (0, 1, 7, 2, 6, 3, 5, 4):
        got = n_rows(1 - side0, core, zpeer(off))
        put(got, got, ax_s.at[off], ax_r.at[off], keep=False, leaf=siblings[0]).wait_recv()
        put(got, got, axp_s.at[off], axp_r.at[off], col=partner).start()
    for off in range(ZS):
        got = n_rows(side0, 1 - core, zpeer(off))
        put(got, got, ap_s.at[off], ap_r.at[off], keep=False, col=partner).wait_recv()
    pp[side0] = mm(ww[0, side0], hh[0, side0], 1, 0)
    settle(pk, 0, 2, xkp_s, xkp_r)
    hear(0)
    settle(ww, 0, 1, xwp_s, xwp_r)
    for off in range(ZS):
        got = n_rows(1 - side0, 1 - core, zpeer(off))
        put(got, got, axp_s.at[off], axp_r.at[off], keep=False, col=partner).wait_recv()
    pp[1 - side0] = mm(ww[0, 1 - side0], hh[0, 1 - side0], 1, 0)

    child_base = 0
    base = 0
    for level in range(1, LEVELS + 1):
        child_base, base = base, base + leaves // (1 << (level - 1))
        node = leaf // (1 << level)
        rank_l = rank_ref[child_base + 2 * node]
        rank_r = rank_ref[child_base + 2 * node + 1]
        rank_p = rank_ref[base + node]
        spots_l = exact(sp[level - 1, 0], ident, 0, 0)
        row_r = sp[level - 1, 1]
        d2 = None
        for axis in range(3):
            off = spots_l[:, axis : axis + 1] - row_r[axis : axis + 1, :]
            d2 = off * off if d2 is None else d2 + off * off
        cross = kern(d2)
        proj_l, proj_r = pp[0], pp[1]
        upper = (pk[level - 1, 0] - mm(cross, proj_r, 1, 0, 3)) * jnp.where(sub < rank_l, 1.0, 0.0)
        lower = (pk[level - 1, 1] - mm(cross, proj_l, 0, 0, 3)) * jnp.where(sub < rank_r, 1.0, 0.0)
        cand = jnp.concatenate([upper, lower], 0)
        spots = jnp.concatenate([sp[level - 1, 0], row_r], 1)
        row = skel_ref[pl.ds(base + node, 1), :]
        chooser = jnp.where(jnp.broadcast_to(row, (2 * r, r)) == iota((2 * r, r), 0), 1.0, 0.0).astype(BF16)
        three = split(cand, 3)
        chosen = bdot(jnp.concatenate([chooser] * 3, 0), jnp.concatenate(three, 0), 0, 0)
        picked = chosen * jnp.where(sub < rank_p, 1.0, 0.0)
        last = level == LEVELS
        if not last:
            side = sides[level]
            pk[level, side] = picked
            sp[level, side] = exact(spots, chooser, 1, 0)
            offer(pk, level, 2, xk_s, xk_r)
            put(sp.at[level, side], sp.at[level, side], xs_s.at[level], xs_r.at[level], leaf=siblings[level]).start()
        else:
            pk3[...] = picked
        raw = mm(cand, picked, 1, 1, 3)
        back = mm(raw, jnp.concatenate([proj_l, proj_r], 0), 0, 0)
        if not last:
            hh[level, side] = back
            offer(hh, level, 2, xh_s, xh_r)
        else:
            hh3[...] = back
        gram = ridged(mm(picked, picked, 1, 1, 3), rank_p)
        if not last:
            ww[level, side] = gram

            def hook(b, level=level):
                @pl.when(b == 4)
                def _():
                    relay(pk, level, 2, xk_s, xk_r, xkp_s, xkp_r)

            spd_inverse(ww.at[level, side], hook)
            offer(ww, level, 1, xw_s, xw_r)
            pp[side] = mm(ww[level, side], hh[level, side], 1, 0)
            relay(hh, level, 2, xh_s, xh_r, xhp_s, xhp_r)
            relay(ww, level, 1, xw_s, xw_r, xwp_s, xwp_r)
            settle(pk, level, 2, xkp_s, xkp_r)
            hear(level)
            settle(hh, level, 2, xhp_s, xhp_r)
            settle(ww, level, 1, xwp_s, xwp_r)
            pp[1 - side] = mm(ww[level, 1 - side], hh[level, 1 - side], 1, 0)
        else:
            ww3[...] = gram
            spd_inverse(ww3, lambda b: None)
            share, span = top_s.shape
            turn = lax.rem(width - me * span, width)
            mine_rows = pl.ds(pl.multiple_of(lax.rem(leaf, 8) * share, share), share)
            top_s[...] = pltpu.roll(pk3[mine_rows, :], turn, 1)[:, 0:span]
            top_o[...] = pltpu.roll(mm(ww3[mine_rows, :], hh3[...], 1, 0), turn, 1)[:, 0:span]

    for copy in sends:
        copy.wait_send()
    for level in range(LEVELS):
        drain_relay(pk, level, 2, xkp_s, xkp_r)
        drain_relay(ww, level, 1, xwp_s, xwp_r)
        if level > 0:
            drain_relay(hh, level, 2, xhp_s, xhp_r)

    def drain(t, carry):
        same = zpeer(zorder(t)) * 2 + core
        put(block_of(same), block_of(same), gp_s.at[t], gp_r.at[t], keep=False, col=partner).wait_send()
        put(pick_rows(same), pick_rows(same), pp_s.at[t], pp_r.at[t], keep=False, col=partner).wait_send()
        return carry

    lax.fori_loop(1, ZS, drain, 0)


def local(points, point_ids, signs, hadamard_sample_rows, samples, skeleton, ranks):
    rows = points.shape[1]
    width = samples.shape[1]
    r = skeleton.shape[1]
    count = r // COLS
    shape = jax.ShapeDtypeStruct
    fetched = pltpu.VMEM
    sems = [DMA(()), *[DMA((ZS,))] * 8, DMA(()), DMA(()), *[DMA((ZS,))] * 10, *[DMA((LEVELS,))] * 2, *[DMA((LEVELS, 2))] * 12]
    return pl.pallas_call(
        hss_kernel,
        out_shape=[
            shape((rows, r), BF16),
            shape((r // 8, width // COLS), F32),
            shape((r // 8, width // COLS), F32),
        ],
        in_specs=[VM, VM, VM, VM, ANY, VM, SM],
        out_specs=[VM] * 3,
        scratch_shapes=[
            fetched((rows, width), BF16),
            fetched((COLS, 8, rows), F32),
            fetched((COLS, rows, width), BF16),
            fetched((3, rows, LANES), F32),
            fetched((3, r, LANES), F32),
            fetched((rows, width), F32),
            fetched((rows, r), F32),
            fetched((r, width), F32),
            fetched((r // 2, width), F32),
            fetched((r // 2, width), F32),
            fetched((ZS - 1, count, width), F32),
            fetched((r, width), F32),
            fetched((LEVELS, 2, r, width), F32),
            fetched((LEVELS, 2, 8, r), F32),
            fetched((LEVELS, 2, r, width), F32),
            fetched((LEVELS, 2, r, r), F32),
            fetched((2, r, width), F32),
            fetched((r, width), F32),
            fetched((r, width), F32),
            fetched((r, r), F32),
            *sems,
        ],
        compiler_params=pltpu.CompilerParams(collective_id=0, has_side_effects=True),
        name="hss",
    )(points, point_ids[None], signs[None], hadamard_sample_rows[None], samples, skeleton, ranks)


def solution(mesh):
    placed = (
        P(None, ("leaf", "col")),
        P(("leaf", "col")),
        P(("leaf", "col")),
        P(),
        P(("leaf", "col"), None),
        P(),
        P(),
    )
    return jax.shard_map(
        local,
        mesh=mesh,
        in_specs=placed,
        out_specs=(P(("leaf", "col"), None), P("leaf", "col"), P("leaf", "col")),
        check_vma=False,
    )
```

```python
import jax
import jax.numpy as jnp
from jax import lax
from jax.experimental import pallas as pl
from jax.experimental.pallas import tpu as pltpu
from jax.sharding import PartitionSpec as P

MESH = pl.DeviceIdType.MESH
DMA = pltpu.SemaphoreType.DMA
F32 = jnp.float32
BF16 = jnp.bfloat16
VM = pl.BlockSpec(memory_space=pltpu.VMEM)
SM = pl.BlockSpec(memory_space=pltpu.SMEM)
ANY = pl.BlockSpec(memory_space=pl.ANY)
HBM = pl.BlockSpec(memory_space=pltpu.HBM)

NTOTAL = 1048576
KERNEL_SCALE = 1.0
RIDGE = 0.25
LOG2E = 1.4426950408889634
BITS = NTOTAL.bit_length() - 1
NBITS = 32
PANEL = 16
COLS = 16
ZS = COLS // 2
LANES = 128
LEVELS = 3


def bdot(a, b, ca, cb):
    return lax.dot_general(a, b, (((ca,), (cb,)), ((), ())), preferred_element_type=F32)


def split(x, count):
    pieces = []
    for _ in range(count - 1):
        piece = x.astype(BF16)
        pieces.append(piece)
        x = x - piece.astype(F32)
    return [*pieces, x.astype(BF16)]


def mm(a, b, ca, cb, terms=6):
    count = 3 if terms == 6 else 2
    pa, pb = split(a, count), split(b, count)
    pairs = [(i, j) for i in range(count) for j in range(count) if i + j < count]
    left = jnp.concatenate([pa[i] for i, _ in pairs], ca)
    right = jnp.concatenate([pb[j] for _, j in pairs], cb)
    return bdot(left, right, ca, cb)


def exact(a, b, ca, cb):
    pieces = split(a, 3)
    return bdot(jnp.concatenate(pieces, ca), jnp.concatenate([b] * 3, cb), ca, cb)


def iota(shape, axis):
    return lax.broadcasted_iota(jnp.int32, shape, axis)


def kern(squared_distance):
    return jnp.exp2(squared_distance * (-KERNEL_SCALE * LOG2E))


def spd_inverse(a_ref, hook):
    n = a_ref.shape[0]
    lane = iota((PANEL, n), 1)
    sub = iota((PANEL, n), 0)
    ident = (lane == sub).astype(F32)
    lane_n = iota((n, n), 1)

    def step(b, carry):
        start = pl.multiple_of(b * PANEL, PANEL)
        panel = a_ref[pl.ds(start, PANEL), :]
        rolled = pltpu.roll(panel, lax.rem(n - start, n), 1)
        diag = [jnp.broadcast_to(rolled[:, k : k + 1], (PANEL, n)) for k in range(PANEL)]
        rows = jnp.where(lane < PANEL, ident, rolled)
        for k in range(PANEL):
            inv = 1.0 / diag[k][k : k + 1, :]
            here = sub == k
            factor = diag[k] * inv
            for j in range(k + 1, PANEL):
                own = diag[j][k : k + 1, :]
                diag[j] = jnp.where(here, own * inv, diag[j] - factor * own)
            own = rows[k : k + 1, :]
            rows = jnp.where(here, own * inv, rows - factor * own)
        rows = pltpu.roll(rows, start, 1)
        side = jnp.where(lane < start, -panel, panel)
        side = jnp.where((lane >= start) & (lane < start + PANEL), 0.0, side)
        change = mm(side, rows, 0, 0)
        cleared = jnp.where((lane_n >= start) & (lane_n < start + PANEL), 0.0, a_ref[...])
        a_ref[...] = cleared - change
        a_ref[pl.ds(start, PANEL), :] = rows
        hook(b)
        return carry

    lax.fori_loop(0, n // PANEL, step, 0)


def ridged(gram, rank):
    n = gram.shape[0]
    same = iota((n, n), 0) == iota((n, n), 1)
    trace = jnp.sum(jnp.where(same, gram, 0.0), keepdims=True)
    shift = RIDGE * trace / rank.astype(F32) + 1e-06
    return gram + jnp.where(same, shift, 0.0)


def unit8():
    return (iota((8, LANES), 0) == iota((8, LANES), 1)).astype(BF16)


def merge(level, leaf, pk, pp, sp, skel_ref, rank_ref):
    leaves = lax.axis_size("leaf")
    r = skel_ref.shape[1]
    child_base = sum(leaves >> k for k in range(level - 1))
    base = child_base + (leaves >> (level - 1))
    sub = iota((r, 1), 0)
    node = leaf // (1 << level)
    rank_l = rank_ref[child_base + 2 * node]
    rank_r = rank_ref[child_base + 2 * node + 1]
    rank_p = rank_ref[base + node]
    spots_l = exact(sp[0], unit8(), 0, 0)
    row_r = sp[1]
    d2 = None
    for axis in range(3):
        off = spots_l[:, axis : axis + 1] - row_r[axis : axis + 1, :]
        d2 = off * off if d2 is None else d2 + off * off
    cross = kern(d2)
    upper = (pk[0] - mm(cross, pp[1], 1, 0, 3)) * jnp.where(sub < rank_l, 1.0, 0.0)
    lower = (pk[1] - mm(cross, pp[0], 0, 0, 3)) * jnp.where(sub < rank_r, 1.0, 0.0)
    cand = jnp.concatenate([upper, lower], 0)
    spots = jnp.concatenate([sp[0], row_r], 1)
    row = skel_ref[pl.ds(base + node, 1), :]
    chooser = jnp.where(jnp.broadcast_to(row, (2 * r, r)) == iota((2 * r, r), 0), 1.0, 0.0).astype(BF16)
    chosen = bdot(jnp.concatenate([chooser] * 3, 0), jnp.concatenate(split(cand, 3), 0), 0, 0)
    return cand, spots, chooser, chosen * jnp.where(sub < rank_p, 1.0, 0.0), rank_p


def top_kernel(basis_ref, pk, pp, sp, skel_ref, rank_ref, basis_out, top_s, top_o, pk3, ww3, sem):
    save = pltpu.make_async_copy(basis_ref, basis_out, sem)
    save.start()
    leaf = lax.axis_index("leaf")
    me = lax.axis_index("col")
    width = pk.shape[2]
    share, span = top_s.shape
    cand, _, _, picked, rank = merge(LEVELS, leaf, pk, pp, sp, skel_ref, rank_ref)
    pk3[...] = picked
    raw = mm(cand, picked, 1, 1, 3)
    back = mm(raw, jnp.concatenate([pp[0], pp[1]], 0), 0, 0)
    ww3[...] = ridged(mm(picked, picked, 1, 1, 3), rank)
    spd_inverse(ww3, lambda b: None)
    turn = lax.rem(width - me * span, width)
    rows = pl.ds(pl.multiple_of(lax.rem(leaf, 8) * share, share), share)
    top_s[...] = pltpu.roll(pk3[rows, :], turn, 1)[:, 0:span]
    top_o[...] = pltpu.roll(mm(ww3[rows, :], back, 1, 0), turn, 1)[:, 0:span]
    save.wait()


def hss_kernel(
    points_ref, ids_ref, signs_ref, had_ref, samp_hbm, skel_ref, rank_ref,
    basis_ref, pk_out, sp_out, pp,
    samp, every, om_all, own_b, pick_b, res, raw_ref, part, half, mine, landed, spk, pk_low, sp_low, hh, ww,
    samp_sem, g_s, g_r, gp_s, gp_r, p_s, p_r, pp_s, pp_r,
    pair_s, pair_r, rs_s, rs_r, ag_s, ag_r, ap_s, ap_r, ax_s, ax_r, axp_s, axp_r,
    xs_s, xs_r, xk_s, xk_r, xkp_s, xkp_r, xh_s, xh_r, xhp_s, xhp_r, xw_s, xw_r, xwp_s, xwp_r,
):
    leaf = lax.axis_index("leaf")
    me = lax.axis_index("col")
    leaves = lax.axis_size("leaf")
    core = lax.rem(me, 2)
    z = me // 2
    partner = me + 1 - 2 * core
    rows = points_ref.shape[1]
    width = had_ref.shape[1]
    r = skel_ref.shape[1]
    count = r // COLS
    pk = [pk_low.at[0], pk_low.at[1], pk_out]
    sp = [sp_low.at[0], sp_low.at[1], sp_out]
    zhalf = lax.rem(z, 2)
    zmate = (z + 1 - 2 * zhalf) * 2 + core
    sides = [lax.rem(leaf // (1 << lvl), 2) for lvl in range(LEVELS)]
    siblings = [leaf + (1 << lvl) - (2 << lvl) * sides[lvl] for lvl in range(LEVELS)]
    sends = []

    def put(src, dst, send, recv, keep=True, **device):
        copy = pltpu.make_async_remote_copy(
            src_ref=src, dst_ref=dst, send_sem=send, recv_sem=recv, device_id=device, device_id_type=MESH
        )
        if keep:
            sends.append(copy)
        return copy

    def zpeer(off):
        return lax.rem(z + off, ZS)

    fetch = pltpu.make_async_copy(samp_hbm, samp, samp_sem)
    fetch.start()
    barrier = pltpu.get_barrier_semaphore()
    for off in range(1, ZS):
        pl.semaphore_signal(barrier, inc=1, device_id={"col": zpeer(off) * 2 + core}, device_id_type=MESH)
    pl.semaphore_signal(barrier, inc=1, device_id={"col": partner}, device_id_type=MESH)
    for sibling in siblings:
        pl.semaphore_signal(barrier, inc=1, device_id={"leaf": sibling}, device_id_type=MESH)
    every[me, 0:3, :] = points_ref[...]
    every[me, 3:4, :] = ids_ref[...].astype(F32)
    every[me, 4:5, :] = signs_ref[...].astype(F32)
    every[:, 5:8, :] = jnp.zeros((COLS, 3, rows), F32)

    my_rows = pl.ds(pl.multiple_of(me * count, count), count)
    entry = skel_ref[pl.ds(leaf, 1), :]

    def chooser_of(slot):
        return jnp.where(
            jnp.broadcast_to(entry - slot * rows, (rows, r)) == iota((rows, r), 0), 1.0, 0.0
        ).astype(BF16)

    fetch.wait()
    part[...] = bdot(chooser_of(me), samp[...], 0, 0)
    spk[my_rows, :] = part[my_rows, :]

    ident = unit8()
    own_cols = exact(every[me], ident, 0, 0)
    for axis in range(3):
        own_b[axis] = jnp.broadcast_to(own_cols[:, axis : axis + 1], (rows, LANES))
    bit_row = iota((NBITS, width), 0)
    had = jnp.broadcast_to(had_ref[...], (NBITS, width))
    had_bits = ((had >> jnp.minimum(bit_row, BITS)) & 1).astype(F32) * 0.5
    had_bits = jnp.where(bit_row == BITS, 0.5, jnp.where(bit_row == BITS + 1, 0.25, had_bits))
    had_bits = jnp.where(bit_row > BITS + 1, 0.0, had_bits).astype(BF16)
    res[...] = samp[...].astype(F32)
    pl.semaphore_wait(barrier, ZS + LEVELS)

    def pick_rows(slot):
        return spk.at[pl.ds(pl.multiple_of(slot * count, count), count)]

    def block_of(slot):
        return every.at[slot, pl.ds(0, 5)]

    order = (1, 7, 2, 6, 3, 5, 4)
    for off in order:
        put(block_of(me), block_of(me), g_s.at[off], g_r.at[ZS - off], col=zpeer(off) * 2 + core).start()
    put(block_of(me), block_of(me), gp_s.at[0], gp_r.at[0], col=partner).start()
    for off in order:
        put(pick_rows(me), pick_rows(me), p_s.at[off], p_r.at[ZS - off], col=zpeer(off) * 2 + core).start()
    put(pick_rows(me), pick_rows(me), pp_s.at[0], pp_r.at[0], col=partner).start()

    def omega4(block):
        shift = iota((NBITS, rows), 0)
        ids = jnp.broadcast_to(block[3:4, :].astype(jnp.int32), (NBITS, rows))
        bits = ((ids >> jnp.minimum(shift, BITS)) & 1).astype(F32)
        bits = jnp.where(shift == BITS, 1.0 - block[4:5, :], bits)
        bits = jnp.where(shift == BITS + 1, 1.0, bits)
        bits = jnp.where(shift > BITS + 1, 0.0, bits).astype(BF16)
        halves = bdot(bits, had_bits, 0, 0)
        return (halves - jnp.round(halves)).astype(BF16)

    def zorder(t):
        return lax.rem(jnp.where(lax.rem(t, 2) == 1, (t + 1) // 2, ZS - t // 2), ZS)

    def tile_of(columns, block):
        tiles = []
        for c in range(rows // LANES):
            d2 = None
            for axis in range(3):
                off = columns[axis] - block[axis : axis + 1, c * LANES : (c + 1) * LANES]
                d2 = off * off if d2 is None else d2 + off * off
            tiles.append(kern(d2).astype(BF16))
        return jnp.concatenate(tiles, 1)

    def near_step(t, spots):
        off = zorder(t)
        there = zpeer(off)
        same = there * 2 + core
        other = there * 2 + 1 - core

        @pl.when(t > 0)
        def _():
            put(block_of(same), block_of(same), g_s.at[off], g_r.at[off], keep=False, col=partner).wait_recv()
            put(block_of(same), block_of(same), gp_s.at[t], gp_r.at[t], keep=False, col=partner).start()

        put(block_of(other), block_of(other), gp_s.at[t], gp_r.at[t], keep=False, col=partner).wait_recv()
        columns = [own_b[axis] for axis in range(3)]
        tiles, omegas = [], []
        for k in range(2):
            block = every[there * 2 + k]
            spots = spots + exact(block, chooser_of(there * 2 + k), 1, 0)
            om = omega4(block)
            om_all[there * 2 + k] = om
            omegas.append(om)
            tiles.append(tile_of(columns, block))
        res[...] -= 0.25 * bdot(jnp.concatenate(tiles, 1), jnp.concatenate(omegas, 0), 1, 0)

        return spots

    spots = lax.fori_loop(0, ZS, near_step, jnp.zeros((8, r), F32))
    sp[0][sides[0]] = spots
    put(sp[0].at[sides[0]], sp[0].at[sides[0]], xs_s.at[0], xs_r.at[0], leaf=siblings[0]).start()

    spot_cols = exact(spots, ident, 0, 0)
    for axis in range(3):
        pick_b[axis] = jnp.broadcast_to(spot_cols[:, axis : axis + 1], (r, LANES))
    part[...] = jnp.zeros((r, width), F32)

    def pick_relay(t, carry):
        off = zorder(t)
        same = zpeer(off) * 2 + core
        put(pick_rows(same), pick_rows(same), p_s.at[off], p_r.at[off], keep=False, col=partner).wait_recv()
        put(pick_rows(same), pick_rows(same), pp_s.at[t], pp_r.at[t], keep=False, col=partner).start()
        return carry

    lax.fori_loop(1, ZS, pick_relay, 0)

    def pick_step(t, carry):
        there = zpeer(zorder(t))
        columns = [pick_b[axis] for axis in range(3)]
        tile = jnp.concatenate([tile_of(columns, every[there * 2 + k]) for k in range(2)], 1)
        part[...] += bdot(tile, om_all[pl.ds(there * 2, 2)].reshape(2 * rows, width), 1, 0)
        return carry

    lax.fori_loop(0, ZS, pick_step, 0)

    def pick_settle(t, carry):
        other = zpeer(zorder(t)) * 2 + 1 - core
        put(pick_rows(other), pick_rows(other), pp_s.at[t], pp_r.at[t], keep=False, col=partner).wait_recv()
        return carry

    lax.fori_loop(0, ZS, pick_settle, 0)
    sub = iota((r, 1), 0)
    pk[0][sides[0]] = (spk[...] - 0.25 * part[...]) * jnp.where(sub < rank_ref[leaf], 1.0, 0.0)

    def pieces(buf, level, side, chunks, half_of):
        size = r // 2 // chunks
        return [buf.at[level, side, pl.ds(pl.multiple_of(half_of * (r // 2) + q * size, size), size)] for q in range(chunks)]

    def offer(buf, level, chunks, s, rv):
        for q, piece in enumerate(pieces(buf, level, sides[level], chunks, core)):
            put(piece, piece, s.at[level, q], rv.at[level, q], leaf=siblings[level]).start()

    def relay(buf, level, chunks, s, rv, s2, rv2):
        for q, piece in enumerate(pieces(buf, level, 1 - sides[level], chunks, core)):
            put(piece, piece, s.at[level, q], rv.at[level, q], keep=False, leaf=siblings[level]).wait_recv()
            put(piece, piece, s2.at[level, q], rv2.at[level, q], keep=False, col=partner).start()

    def settle(buf, level, chunks, s2, rv2):
        for q, piece in enumerate(pieces(buf, level, 1 - sides[level], chunks, 1 - core)):
            put(piece, piece, s2.at[level, q], rv2.at[level, q], keep=False, col=partner).wait_recv()

    def quarter(level, side, half_of, chip):
        size = r // 4
        return pk[level].at[side, pl.ds(pl.multiple_of((half_of * 2 + chip) * size, size), size)]

    def offer_picked(level):
        piece = quarter(level, sides[level], core, zhalf)
        put(piece, piece, xk_s.at[level, 0], xk_r.at[level, 0], leaf=siblings[level]).start()

    def relay_picked(level):
        got = quarter(level, 1 - sides[level], core, zhalf)
        put(got, got, xk_s.at[level, 0], xk_r.at[level, 0], keep=False, leaf=siblings[level]).wait_recv()
        put(got, got, xk_s.at[level, 1], xk_r.at[level, 1], keep=False, col=zmate).start()
        put(got, got, xkp_s.at[level, 0], xkp_r.at[level, 0], keep=False, col=partner).start()

    def relay_picked_mate(level):
        got = quarter(level, 1 - sides[level], core, 1 - zhalf)
        put(got, got, xk_s.at[level, 1], xk_r.at[level, 1], keep=False, col=zmate).wait_recv()
        put(got, got, xkp_s.at[level, 1], xkp_r.at[level, 1], keep=False, col=partner).start()

    def settle_picked(level):
        for q, chip in enumerate((zhalf, 1 - zhalf)):
            got = quarter(level, 1 - sides[level], 1 - core, chip)
            put(got, got, xkp_s.at[level, q], xkp_r.at[level, q], keep=False, col=partner).wait_recv()

    def drain_picked(level):
        got = quarter(level, 1 - sides[level], core, zhalf)
        put(got, got, xk_s.at[level, 1], xk_r.at[level, 1], keep=False, col=zmate).wait_send()
        for q in range(2):
            put(got, got, xkp_s.at[level, q], xkp_r.at[level, q], keep=False, col=partner).wait_send()

    def hear(level):
        got = sp[level].at[1 - sides[level]]
        put(got, got, xs_s.at[level], xs_r.at[level], keep=False, leaf=siblings[level]).wait_recv()

    def drain_relay(buf, level, chunks, s2, rv2):
        for q, piece in enumerate(pieces(buf, level, 1 - sides[level], chunks, core)):
            put(piece, piece, s2.at[level, q], rv2.at[level, q], keep=False, col=partner).wait_send()

    offer_picked(0)

    side0 = sides[0]
    picked = pk[0][side0]
    raw = mm(res[...], picked, 1, 1)
    raw_ref[...] = raw
    om_own = om_all[me]
    part[...] = 0.25 * exact(raw, om_own, 0, 0)
    r2 = r // 2
    own0 = pl.multiple_of(core * r2, r2)
    other0 = pl.multiple_of((1 - core) * r2, r2)
    pair = put(part.at[pl.ds(other0, r2)], half, pair_s, pair_r, col=partner)
    pair.start()
    ww[0, side0] = ridged(mm(picked, picked, 1, 1), rank_ref[leaf])
    scatter = []
    for off in range(1, ZS):
        piece = pl.ds(pl.multiple_of(zpeer(off) * count, count), count)
        scatter.append(put(mine.at[piece], landed.at[off - 1], rs_s.at[off], rs_r.at[off], col=zpeer(off) * 2 + core))

    def leaf_hook(b):
        @pl.when(b == 2)
        def _():
            pair.wait_recv()
            mine[...] = part[pl.ds(own0, r2)] + half[...]
            for copy in scatter:
                copy.start()

        @pl.when(b == 6)
        def _():
            relay_picked(0)

    spd_inverse(ww.at[0, side0], leaf_hook)
    offer(ww, 0, 1, xw_s, xw_r)
    basis_ref[...] = mm(raw_ref[...], ww[0, side0], 1, 0).astype(BF16)

    def n_rows(side, half_of, chip):
        return hh.at[0, side, pl.ds(pl.multiple_of(half_of * r2 + chip * count, count), count)]

    total = mine[pl.ds(pl.multiple_of(z * count, count), count)]
    for off in range(1, ZS):
        scatter[off - 1].wait_recv()
        total = total + landed[off - 1]
    hh[0, side0, pl.ds(pl.multiple_of(own0 + z * count, count), count)] = total
    here = n_rows(side0, core, z)
    for off in (1, 7, 2, 6, 3, 5, 4):
        put(here, here, ag_s.at[off], ag_r.at[ZS - off], col=zpeer(off) * 2 + core).start()
    put(here, here, ap_s.at[0], ap_r.at[0], col=partner).start()
    put(here, here, ax_s.at[0], ax_r.at[0], leaf=siblings[0]).start()
    for off in (1, 7, 2, 6, 3, 5, 4):
        got = n_rows(side0, core, zpeer(off))
        put(got, got, ag_s.at[off], ag_r.at[off], keep=False, col=partner).wait_recv()
        put(got, got, ap_s.at[off], ap_r.at[off], col=partner).start()
        put(got, got, ax_s.at[off], ax_r.at[off], leaf=siblings[0]).start()
    relay_picked_mate(0)
    relay(ww, 0, 1, xw_s, xw_r, xwp_s, xwp_r)
    for off in (0, 1, 7, 2, 6, 3, 5, 4):
        got = n_rows(1 - side0, core, zpeer(off))
        put(got, got, ax_s.at[off], ax_r.at[off], keep=False, leaf=siblings[0]).wait_recv()
        put(got, got, axp_s.at[off], axp_r.at[off], col=partner).start()
    for off in range(ZS):
        got = n_rows(side0, 1 - core, zpeer(off))
        put(got, got, ap_s.at[off], ap_r.at[off], keep=False, col=partner).wait_recv()
    pp[side0] = mm(ww[0, side0], hh[0, side0], 1, 0)
    settle_picked(0)
    hear(0)
    settle(ww, 0, 1, xwp_s, xwp_r)
    for off in range(ZS):
        got = n_rows(1 - side0, 1 - core, zpeer(off))
        put(got, got, axp_s.at[off], axp_r.at[off], keep=False, col=partner).wait_recv()
    pp[1 - side0] = mm(ww[0, 1 - side0], hh[0, 1 - side0], 1, 0)

    for level in range(1, LEVELS):
        side = sides[level]
        cand, spots, chooser, picked, rank = merge(level, leaf, pk[level - 1], pp, sp[level - 1], skel_ref, rank_ref)
        pk[level][side] = picked
        offer_picked(level)
        sp[level][side] = exact(spots, chooser, 1, 0)
        put(sp[level].at[side], sp[level].at[side], xs_s.at[level], xs_r.at[level], leaf=siblings[level]).start()
        raw = mm(cand, picked, 1, 1, 3)
        hh[level, side] = mm(raw, jnp.concatenate([pp[0], pp[1]], 0), 0, 0)
        offer(hh, level, 4, xh_s, xh_r)
        ww[level, side] = ridged(mm(picked, picked, 1, 1, 3), rank)

        def hook(b, level=level):
            @pl.when(b == 5)
            def _():
                relay_picked(level)

        spd_inverse(ww.at[level, side], hook)
        offer(ww, level, 1, xw_s, xw_r)
        pp[side] = mm(ww[level, side], hh[level, side], 1, 0)
        relay_picked_mate(level)
        relay(hh, level, 4, xh_s, xh_r, xhp_s, xhp_r)
        relay(ww, level, 1, xw_s, xw_r, xwp_s, xwp_r)
        settle_picked(level)
        hear(level)
        settle(hh, level, 4, xhp_s, xhp_r)
        settle(ww, level, 1, xwp_s, xwp_r)
        pp[1 - side] = mm(ww[level, 1 - side], hh[level, 1 - side], 1, 0)

    for copy in sends:
        copy.wait_send()
    for level in range(LEVELS):
        drain_picked(level)
        drain_relay(ww, level, 1, xwp_s, xwp_r)
        if level > 0:
            drain_relay(hh, level, 4, xhp_s, xhp_r)

    def drain(t, carry):
        same = zpeer(zorder(t)) * 2 + core
        put(block_of(same), block_of(same), gp_s.at[t], gp_r.at[t], keep=False, col=partner).wait_send()
        put(pick_rows(same), pick_rows(same), pp_s.at[t], pp_r.at[t], keep=False, col=partner).wait_send()
        return carry

    lax.fori_loop(1, ZS, drain, 0)


def local(points, point_ids, signs, hadamard_sample_rows, samples, skeleton, ranks):
    rows = points.shape[1]
    width = samples.shape[1]
    r = skeleton.shape[1]
    count = r // COLS
    shape = jax.ShapeDtypeStruct
    fetched = pltpu.VMEM
    pair_of = [DMA((LEVELS, 2))] * 4
    sems = [
        DMA(()), *[DMA((ZS,))] * 8, DMA(()), DMA(()), *[DMA((ZS,))] * 10, *[DMA((LEVELS,))] * 2,
        *pair_of, *[DMA((LEVELS, 4))] * 4, *pair_of,
    ]
    basis, pk, sp, pp = pl.pallas_call(
        hss_kernel,
        out_shape=[
            shape((rows, r), BF16),
            shape((2, r, width), F32),
            shape((2, 8, r), F32),
            shape((2, r, width), F32),
        ],
        in_specs=[VM, VM, VM, VM, HBM, VM, SM],
        out_specs=[VM] * 4,
        scratch_shapes=[
            fetched((rows, width), BF16),
            fetched((COLS, 8, rows), F32),
            fetched((COLS, rows, width), BF16),
            fetched((3, rows, LANES), F32),
            fetched((3, r, LANES), F32),
            fetched((rows, width), F32),
            fetched((rows, r), F32),
            fetched((r, width), F32),
            fetched((r // 2, width), F32),
            fetched((r // 2, width), F32),
            fetched((ZS - 1, count, width), F32),
            fetched((r, width), F32),
            fetched((2, 2, r, width), F32),
            fetched((2, 2, 8, r), F32),
            fetched((LEVELS, 2, r, width), F32),
            fetched((LEVELS, 2, r, r), F32),
            *sems,
        ],
        compiler_params=pltpu.CompilerParams(
            collective_id=0, has_side_effects=True, vmem_limit_bytes=32 * 1024 * 1024
        ),
        name="hss",
    )(points, point_ids[None], signs[None], hadamard_sample_rows[None], samples, skeleton, ranks)
    top = shape((r // 8, width // COLS), F32)
    return pl.pallas_call(
        top_kernel,
        out_shape=[shape((rows, r), BF16), top, top],
        in_specs=[VM, VM, VM, VM, VM, SM],
        out_specs=[ANY, VM, VM],
        scratch_shapes=[fetched((r, width), F32), fetched((r, r), F32), DMA(())],
        compiler_params=pltpu.CompilerParams(vmem_limit_bytes=32 * 1024 * 1024),
        name="top",
    )(basis, pk, pp, sp, skeleton, ranks)


def solution(mesh):
    placed = (
        P(None, ("leaf", "col")),
        P(("leaf", "col")),
        P(("leaf", "col")),
        P(),
        P(("leaf", "col"), None),
        P(),
        P(),
    )
    return jax.shard_map(
        local,
        mesh=mesh,
        in_specs=placed,
        out_specs=(P(("leaf", "col"), None), P("leaf", "col"), P("leaf", "col")),
        check_vma=False,
    )
```

```python
import jax
import jax.numpy as jnp
from jax import lax
from jax.experimental import pallas as pl
from jax.experimental.pallas import tpu as pltpu
from jax.sharding import PartitionSpec as P

MESH = pl.DeviceIdType.MESH
DMA = pltpu.SemaphoreType.DMA
F32 = jnp.float32
BF16 = jnp.bfloat16
VM = pl.BlockSpec(memory_space=pltpu.VMEM)
SM = pl.BlockSpec(memory_space=pltpu.SMEM)
ANY = pl.BlockSpec(memory_space=pl.ANY)
HBM = pl.BlockSpec(memory_space=pltpu.HBM)

NTOTAL = 1048576
KERNEL_SCALE = 1.0
RIDGE = 0.25
LOG2E = 1.4426950408889634
BITS = NTOTAL.bit_length() - 1
NBITS = 32
PANEL = 16
COLS = 16
ZS = COLS // 2
LANES = 128
LEVELS = 3


def bdot(a, b, ca, cb):
    return lax.dot_general(a, b, (((ca,), (cb,)), ((), ())), preferred_element_type=F32)


def split(x, count):
    pieces = []
    for _ in range(count - 1):
        piece = x.astype(BF16)
        pieces.append(piece)
        x = x - piece.astype(F32)
    return [*pieces, x.astype(BF16)]


def mm(a, b, ca, cb, terms=6):
    count = 3 if terms == 6 else 2
    pa, pb = split(a, count), split(b, count)
    pairs = [(i, j) for i in range(count) for j in range(count) if i + j < count]
    left = jnp.concatenate([pa[i] for i, _ in pairs], ca)
    right = jnp.concatenate([pb[j] for _, j in pairs], cb)
    return bdot(left, right, ca, cb)


def exact(a, b, ca, cb):
    pieces = split(a, 3)
    return bdot(jnp.concatenate(pieces, ca), jnp.concatenate([b] * 3, cb), ca, cb)


def iota(shape, axis):
    return lax.broadcasted_iota(jnp.int32, shape, axis)


def kern(squared_distance):
    return jnp.exp2(squared_distance * (-KERNEL_SCALE * LOG2E))


def spd_inverse(a_ref, hook):
    n = a_ref.shape[0]
    lane = iota((PANEL, n), 1)
    sub = iota((PANEL, n), 0)
    ident = (lane == sub).astype(F32)
    lane_n = iota((n, n), 1)

    def step(b, carry):
        start = pl.multiple_of(b * PANEL, PANEL)
        panel = a_ref[pl.ds(start, PANEL), :]
        rolled = pltpu.roll(panel, lax.rem(n - start, n), 1)
        diag = [jnp.broadcast_to(rolled[:, k : k + 1], (PANEL, n)) for k in range(PANEL)]
        rows = jnp.where(lane < PANEL, ident, rolled)
        for k in range(PANEL):
            inv = 1.0 / diag[k][k : k + 1, :]
            here = sub == k
            factor = diag[k] * inv
            for j in range(k + 1, PANEL):
                own = diag[j][k : k + 1, :]
                diag[j] = jnp.where(here, own * inv, diag[j] - factor * own)
            own = rows[k : k + 1, :]
            rows = jnp.where(here, own * inv, rows - factor * own)
        rows = pltpu.roll(rows, start, 1)
        side = jnp.where(lane < start, -panel, panel)
        side = jnp.where((lane >= start) & (lane < start + PANEL), 0.0, side)
        change = mm(side, rows, 0, 0)
        cleared = jnp.where((lane_n >= start) & (lane_n < start + PANEL), 0.0, a_ref[...])
        a_ref[...] = cleared - change
        a_ref[pl.ds(start, PANEL), :] = rows
        hook(b)
        return carry

    lax.fori_loop(0, n // PANEL, step, 0)


def ridged(gram, rank):
    n = gram.shape[0]
    same = iota((n, n), 0) == iota((n, n), 1)
    trace = jnp.sum(jnp.where(same, gram, 0.0), keepdims=True)
    shift = RIDGE * trace / rank.astype(F32) + 1e-06
    return gram + jnp.where(same, shift, 0.0)


def unit8():
    return (iota((8, LANES), 0) == iota((8, LANES), 1)).astype(BF16)


def merge(level, leaf, pk, pp, sp, skel_ref, rank_ref):
    leaves = lax.axis_size("leaf")
    r = skel_ref.shape[1]
    child_base = sum(leaves >> k for k in range(level - 1))
    base = child_base + (leaves >> (level - 1))
    sub = iota((r, 1), 0)
    node = leaf // (1 << level)
    rank_l = rank_ref[child_base + 2 * node]
    rank_r = rank_ref[child_base + 2 * node + 1]
    rank_p = rank_ref[base + node]
    spots_l = exact(sp[0], unit8(), 0, 0)
    row_r = sp[1]
    d2 = None
    for axis in range(3):
        off = spots_l[:, axis : axis + 1] - row_r[axis : axis + 1, :]
        d2 = off * off if d2 is None else d2 + off * off
    cross = kern(d2)
    upper = (pk[0] - mm(cross, pp[1], 1, 0, 3)) * jnp.where(sub < rank_l, 1.0, 0.0)
    lower = (pk[1] - mm(cross, pp[0], 0, 0, 3)) * jnp.where(sub < rank_r, 1.0, 0.0)
    cand = jnp.concatenate([upper, lower], 0)
    spots = jnp.concatenate([sp[0], row_r], 1)
    row = skel_ref[pl.ds(base + node, 1), :]
    chooser = jnp.where(jnp.broadcast_to(row, (2 * r, r)) == iota((2 * r, r), 0), 1.0, 0.0).astype(BF16)
    chosen = bdot(jnp.concatenate([chooser] * 3, 0), jnp.concatenate(split(cand, 3), 0), 0, 0)
    return cand, spots, chooser, chosen * jnp.where(sub < rank_p, 1.0, 0.0), rank_p


def top_kernel(basis_ref, pk, pp, sp, skel_ref, rank_ref, basis_out, top_s, top_o, pk3, ww3, sem):
    save = pltpu.make_async_copy(basis_ref, basis_out, sem)
    save.start()
    leaf = lax.axis_index("leaf")
    me = lax.axis_index("col")
    width = pk.shape[2]
    share, span = top_s.shape
    cand, _, _, picked, rank = merge(LEVELS, leaf, pk, pp, sp, skel_ref, rank_ref)
    pk3[...] = picked
    raw = mm(cand, picked, 1, 1, 3)
    back = mm(raw, jnp.concatenate([pp[0], pp[1]], 0), 0, 0)
    ww3[...] = ridged(mm(picked, picked, 1, 1, 3), rank)
    spd_inverse(ww3, lambda b: None)
    turn = lax.rem(width - me * span, width)
    rows = pl.ds(pl.multiple_of(lax.rem(leaf, 8) * share, share), share)
    top_s[...] = pltpu.roll(pk3[rows, :], turn, 1)[:, 0:span]
    top_o[...] = pltpu.roll(mm(ww3[rows, :], back, 1, 0), turn, 1)[:, 0:span]
    save.wait()


def hss_kernel(
    points_hbm, ids_hbm, signs_hbm, had_hbm, samp_hbm, skel_hbm, rank_hbm,
    basis_ref, pk_out, sp_out, pp,
    points_ref, ids_ref, signs_ref, had_ref, skel_ref, rank_ref, samp, every, om_all, own_b, pick_b, res, raw_ref, part, half, mine, landed, spk, pk_low, sp_low, hh, ww,
    samp_sem, g_s, g_r, gp_s, gp_r, p_s, p_r, pp_s, pp_r,
    pair_s, pair_r, rs_s, rs_r, ag_s, ag_r, ap_s, ap_r, ax_s, ax_r, axp_s, axp_r,
    xs_s, xs_r, xk_s, xk_r, xkp_s, xkp_r, xh_s, xh_r, xhp_s, xhp_r, xw_s, xw_r, xwp_s, xwp_r,
):
    leaf = lax.axis_index("leaf")
    me = lax.axis_index("col")
    leaves = lax.axis_size("leaf")
    core = lax.rem(me, 2)
    z = me // 2
    partner = me + 1 - 2 * core
    rows = points_ref.shape[1]
    width = had_ref.shape[1]
    r = skel_ref.shape[1]
    count = r // COLS
    pk = [pk_low.at[0], pk_low.at[1], pk_out]
    sp = [sp_low.at[0], sp_low.at[1], sp_out]
    zhalf = lax.rem(z, 2)
    zmate = (z + 1 - 2 * zhalf) * 2 + core
    sides = [lax.rem(leaf // (1 << lvl), 2) for lvl in range(LEVELS)]
    siblings = [leaf + (1 << lvl) - (2 << lvl) * sides[lvl] for lvl in range(LEVELS)]
    sends = []

    def put(src, dst, send, recv, keep=True, **device):
        copy = pltpu.make_async_remote_copy(
            src_ref=src, dst_ref=dst, send_sem=send, recv_sem=recv, device_id=device, device_id_type=MESH
        )
        if keep:
            sends.append(copy)
        return copy

    def zpeer(off):
        return lax.rem(z + off, ZS)

    fetches = [
        pltpu.make_async_copy(source, target, samp_sem.at[i])
        for i, (source, target) in enumerate(
            (
                (points_hbm, points_ref),
                (ids_hbm, ids_ref),
                (signs_hbm, signs_ref),
                (skel_hbm, skel_ref),
                (rank_hbm, rank_ref),
                (had_hbm, had_ref),
                (samp_hbm, samp),
            )
        )
    ]
    for fetch in fetches:
        fetch.start()
    barrier = pltpu.get_barrier_semaphore()
    for off in range(1, ZS):
        pl.semaphore_signal(barrier, inc=1, device_id={"col": zpeer(off) * 2 + core}, device_id_type=MESH)
    pl.semaphore_signal(barrier, inc=1, device_id={"col": partner}, device_id_type=MESH)
    for sibling in siblings:
        pl.semaphore_signal(barrier, inc=1, device_id={"leaf": sibling}, device_id_type=MESH)
    for fetch in fetches:
        fetch.wait()
    every[me, 0:3, :] = points_ref[...]
    every[me, 3:4, :] = ids_ref[...].astype(F32)
    every[me, 4:5, :] = signs_ref[...].astype(F32)
    every[:, 5:8, :] = jnp.zeros((COLS, 3, rows), F32)

    my_rows = pl.ds(pl.multiple_of(me * count, count), count)
    entry = skel_ref[pl.ds(leaf, 1), :]

    def chooser_of(slot):
        return jnp.where(
            jnp.broadcast_to(entry - slot * rows, (rows, r)) == iota((rows, r), 0), 1.0, 0.0
        ).astype(BF16)

    part[...] = bdot(chooser_of(me), samp[...], 0, 0)
    spk[my_rows, :] = part[my_rows, :]

    ident = unit8()
    own_cols = exact(every[me], ident, 0, 0)
    for axis in range(3):
        own_b[axis] = jnp.broadcast_to(own_cols[:, axis : axis + 1], (rows, LANES))
    bit_row = iota((NBITS, width), 0)
    had = jnp.broadcast_to(had_ref[...], (NBITS, width))
    had_bits = ((had >> jnp.minimum(bit_row, BITS)) & 1).astype(F32) * 0.5
    had_bits = jnp.where(bit_row == BITS, 0.5, jnp.where(bit_row == BITS + 1, 0.25, had_bits))
    had_bits = jnp.where(bit_row > BITS + 1, 0.0, had_bits).astype(BF16)
    res[...] = samp[...].astype(F32)
    pl.semaphore_wait(barrier, ZS + LEVELS)

    def pick_rows(slot):
        return spk.at[pl.ds(pl.multiple_of(slot * count, count), count)]

    def block_of(slot):
        return every.at[slot, pl.ds(0, 5)]

    order = (1, 7, 2, 6, 3, 5, 4)
    for off in order:
        put(block_of(me), block_of(me), g_s.at[off], g_r.at[ZS - off], col=zpeer(off) * 2 + core).start()
    put(block_of(me), block_of(me), gp_s.at[0], gp_r.at[0], col=partner).start()
    for off in order:
        put(pick_rows(me), pick_rows(me), p_s.at[off], p_r.at[ZS - off], col=zpeer(off) * 2 + core).start()
    put(pick_rows(me), pick_rows(me), pp_s.at[0], pp_r.at[0], col=partner).start()

    def omega4(block):
        shift = iota((NBITS, rows), 0)
        ids = jnp.broadcast_to(block[3:4, :].astype(jnp.int32), (NBITS, rows))
        bits = ((ids >> jnp.minimum(shift, BITS)) & 1).astype(F32)
        bits = jnp.where(shift == BITS, 1.0 - block[4:5, :], bits)
        bits = jnp.where(shift == BITS + 1, 1.0, bits)
        bits = jnp.where(shift > BITS + 1, 0.0, bits).astype(BF16)
        halves = bdot(bits, had_bits, 0, 0)
        return (halves - jnp.round(halves)).astype(BF16)

    def zorder(t):
        return lax.rem(jnp.where(lax.rem(t, 2) == 1, (t + 1) // 2, ZS - t // 2), ZS)

    def tile_of(columns, block):
        tiles = []
        for c in range(rows // LANES):
            d2 = None
            for axis in range(3):
                off = columns[axis] - block[axis : axis + 1, c * LANES : (c + 1) * LANES]
                d2 = off * off if d2 is None else d2 + off * off
            tiles.append(kern(d2).astype(BF16))
        return jnp.concatenate(tiles, 1)

    def near_step(t, spots):
        off = zorder(t)
        there = zpeer(off)
        same = there * 2 + core
        other = there * 2 + 1 - core

        @pl.when(t > 0)
        def _():
            put(block_of(same), block_of(same), g_s.at[off], g_r.at[off], keep=False, col=partner).wait_recv()
            put(block_of(same), block_of(same), gp_s.at[t], gp_r.at[t], keep=False, col=partner).start()

        put(block_of(other), block_of(other), gp_s.at[t], gp_r.at[t], keep=False, col=partner).wait_recv()
        columns = [own_b[axis] for axis in range(3)]
        tiles, omegas = [], []
        for k in range(2):
            block = every[there * 2 + k]
            spots = spots + exact(block, chooser_of(there * 2 + k), 1, 0)
            om = omega4(block)
            om_all[there * 2 + k] = om
            omegas.append(om)
            tiles.append(tile_of(columns, block))
        res[...] -= 0.25 * bdot(jnp.concatenate(tiles, 1), jnp.concatenate(omegas, 0), 1, 0)

        return spots

    spots = lax.fori_loop(0, ZS, near_step, jnp.zeros((8, r), F32))
    sp[0][sides[0]] = spots
    put(sp[0].at[sides[0]], sp[0].at[sides[0]], xs_s.at[0], xs_r.at[0], leaf=siblings[0]).start()

    spot_cols = exact(spots, ident, 0, 0)
    for axis in range(3):
        pick_b[axis] = jnp.broadcast_to(spot_cols[:, axis : axis + 1], (r, LANES))
    part[...] = jnp.zeros((r, width), F32)

    def pick_relay(t, carry):
        off = zorder(t)
        same = zpeer(off) * 2 + core
        put(pick_rows(same), pick_rows(same), p_s.at[off], p_r.at[off], keep=False, col=partner).wait_recv()
        put(pick_rows(same), pick_rows(same), pp_s.at[t], pp_r.at[t], keep=False, col=partner).start()
        return carry

    lax.fori_loop(1, ZS, pick_relay, 0)

    def pick_step(t, carry):
        there = zpeer(zorder(t))
        columns = [pick_b[axis] for axis in range(3)]
        tile = jnp.concatenate([tile_of(columns, every[there * 2 + k]) for k in range(2)], 1)
        part[...] += bdot(tile, om_all[pl.ds(there * 2, 2)].reshape(2 * rows, width), 1, 0)
        return carry

    lax.fori_loop(0, ZS, pick_step, 0)

    def pick_settle(t, carry):
        other = zpeer(zorder(t)) * 2 + 1 - core
        put(pick_rows(other), pick_rows(other), pp_s.at[t], pp_r.at[t], keep=False, col=partner).wait_recv()
        return carry

    lax.fori_loop(0, ZS, pick_settle, 0)
    sub = iota((r, 1), 0)
    pk[0][sides[0]] = (spk[...] - 0.25 * part[...]) * jnp.where(sub < rank_ref[leaf], 1.0, 0.0)

    def pieces(buf, level, side, chunks, half_of):
        size = r // 2 // chunks
        return [buf.at[level, side, pl.ds(pl.multiple_of(half_of * (r // 2) + q * size, size), size)] for q in range(chunks)]

    def offer(buf, level, chunks, s, rv):
        for q, piece in enumerate(pieces(buf, level, sides[level], chunks, core)):
            put(piece, piece, s.at[level, q], rv.at[level, q], leaf=siblings[level]).start()

    def relay(buf, level, chunks, s, rv, s2, rv2):
        for q, piece in enumerate(pieces(buf, level, 1 - sides[level], chunks, core)):
            put(piece, piece, s.at[level, q], rv.at[level, q], keep=False, leaf=siblings[level]).wait_recv()
            put(piece, piece, s2.at[level, q], rv2.at[level, q], keep=False, col=partner).start()

    def settle(buf, level, chunks, s2, rv2):
        for q, piece in enumerate(pieces(buf, level, 1 - sides[level], chunks, 1 - core)):
            put(piece, piece, s2.at[level, q], rv2.at[level, q], keep=False, col=partner).wait_recv()

    def quarter(level, side, half_of, chip):
        size = r // 4
        return pk[level].at[side, pl.ds(pl.multiple_of((half_of * 2 + chip) * size, size), size)]

    def offer_picked(level):
        piece = quarter(level, sides[level], core, zhalf)
        put(piece, piece, xk_s.at[level, 0], xk_r.at[level, 0], leaf=siblings[level]).start()

    def relay_picked(level):
        got = quarter(level, 1 - sides[level], core, zhalf)
        put(got, got, xk_s.at[level, 0], xk_r.at[level, 0], keep=False, leaf=siblings[level]).wait_recv()
        put(got, got, xk_s.at[level, 1], xk_r.at[level, 1], keep=False, col=zmate).start()
        put(got, got, xkp_s.at[level, 0], xkp_r.at[level, 0], keep=False, col=partner).start()

    def relay_picked_mate(level):
        got = quarter(level, 1 - sides[level], core, 1 - zhalf)
        put(got, got, xk_s.at[level, 1], xk_r.at[level, 1], keep=False, col=zmate).wait_recv()
        put(got, got, xkp_s.at[level, 1], xkp_r.at[level, 1], keep=False, col=partner).start()

    def settle_picked(level):
        for q, chip in enumerate((zhalf, 1 - zhalf)):
            got = quarter(level, 1 - sides[level], 1 - core, chip)
            put(got, got, xkp_s.at[level, q], xkp_r.at[level, q], keep=False, col=partner).wait_recv()

    def drain_picked(level):
        got = quarter(level, 1 - sides[level], core, zhalf)
        put(got, got, xk_s.at[level, 1], xk_r.at[level, 1], keep=False, col=zmate).wait_send()
        for q in range(2):
            put(got, got, xkp_s.at[level, q], xkp_r.at[level, q], keep=False, col=partner).wait_send()

    def hear(level):
        got = sp[level].at[1 - sides[level]]
        put(got, got, xs_s.at[level], xs_r.at[level], keep=False, leaf=siblings[level]).wait_recv()

    def drain_relay(buf, level, chunks, s2, rv2):
        for q, piece in enumerate(pieces(buf, level, 1 - sides[level], chunks, core)):
            put(piece, piece, s2.at[level, q], rv2.at[level, q], keep=False, col=partner).wait_send()

    offer_picked(0)

    side0 = sides[0]
    picked = pk[0][side0]
    raw = mm(res[...], picked, 1, 1)
    raw_ref[...] = raw
    om_own = om_all[me]
    part[...] = 0.25 * exact(raw, om_own, 0, 0)
    r2 = r // 2
    own0 = pl.multiple_of(core * r2, r2)
    other0 = pl.multiple_of((1 - core) * r2, r2)
    pair = put(part.at[pl.ds(other0, r2)], half, pair_s, pair_r, col=partner)
    pair.start()
    ww[0, side0] = ridged(mm(picked, picked, 1, 1), rank_ref[leaf])
    scatter = []
    for off in range(1, ZS):
        piece = pl.ds(pl.multiple_of(zpeer(off) * count, count), count)
        scatter.append(put(mine.at[piece], landed.at[off - 1], rs_s.at[off], rs_r.at[off], col=zpeer(off) * 2 + core))

    def leaf_hook(b):
        @pl.when(b == 2)
        def _():
            pair.wait_recv()
            mine[...] = part[pl.ds(own0, r2)] + half[...]
            for copy in scatter:
                copy.start()

        @pl.when(b == 6)
        def _():
            relay_picked(0)

    spd_inverse(ww.at[0, side0], leaf_hook)
    offer(ww, 0, 1, xw_s, xw_r)
    basis_ref[...] = mm(raw_ref[...], ww[0, side0], 1, 0).astype(BF16)

    def n_rows(side, half_of, chip):
        return hh.at[0, side, pl.ds(pl.multiple_of(half_of * r2 + chip * count, count), count)]

    total = mine[pl.ds(pl.multiple_of(z * count, count), count)]
    for off in range(1, ZS):
        scatter[off - 1].wait_recv()
        total = total + landed[off - 1]
    hh[0, side0, pl.ds(pl.multiple_of(own0 + z * count, count), count)] = total
    here = n_rows(side0, core, z)
    for off in (1, 7, 2, 6, 3, 5, 4):
        put(here, here, ag_s.at[off], ag_r.at[ZS - off], col=zpeer(off) * 2 + core).start()
    put(here, here, ap_s.at[0], ap_r.at[0], col=partner).start()
    put(here, here, ax_s.at[0], ax_r.at[0], leaf=siblings[0]).start()
    for off in (1, 7, 2, 6, 3, 5, 4):
        got = n_rows(side0, core, zpeer(off))
        put(got, got, ag_s.at[off], ag_r.at[off], keep=False, col=partner).wait_recv()
        put(got, got, ap_s.at[off], ap_r.at[off], col=partner).start()
        put(got, got, ax_s.at[off], ax_r.at[off], leaf=siblings[0]).start()
    relay_picked_mate(0)
    relay(ww, 0, 1, xw_s, xw_r, xwp_s, xwp_r)
    for off in (0, 1, 7, 2, 6, 3, 5, 4):
        got = n_rows(1 - side0, core, zpeer(off))
        put(got, got, ax_s.at[off], ax_r.at[off], keep=False, leaf=siblings[0]).wait_recv()
        put(got, got, axp_s.at[off], axp_r.at[off], col=partner).start()
    for off in range(ZS):
        got = n_rows(side0, 1 - core, zpeer(off))
        put(got, got, ap_s.at[off], ap_r.at[off], keep=False, col=partner).wait_recv()
    pp[side0] = mm(ww[0, side0], hh[0, side0], 1, 0)
    settle_picked(0)
    hear(0)
    settle(ww, 0, 1, xwp_s, xwp_r)
    for off in range(ZS):
        got = n_rows(1 - side0, 1 - core, zpeer(off))
        put(got, got, axp_s.at[off], axp_r.at[off], keep=False, col=partner).wait_recv()
    pp[1 - side0] = mm(ww[0, 1 - side0], hh[0, 1 - side0], 1, 0)

    for level in range(1, LEVELS):
        side = sides[level]
        cand, spots, chooser, picked, rank = merge(level, leaf, pk[level - 1], pp, sp[level - 1], skel_ref, rank_ref)
        pk[level][side] = picked
        offer_picked(level)
        sp[level][side] = exact(spots, chooser, 1, 0)
        put(sp[level].at[side], sp[level].at[side], xs_s.at[level], xs_r.at[level], leaf=siblings[level]).start()
        raw = mm(cand, picked, 1, 1, 3)
        hh[level, side] = mm(raw, jnp.concatenate([pp[0], pp[1]], 0), 0, 0)
        offer(hh, level, 4, xh_s, xh_r)
        ww[level, side] = ridged(mm(picked, picked, 1, 1, 3), rank)

        def hook(b, level=level):
            @pl.when(b == 5)
            def _():
                relay_picked(level)

        spd_inverse(ww.at[level, side], hook)
        offer(ww, level, 1, xw_s, xw_r)
        pp[side] = mm(ww[level, side], hh[level, side], 1, 0)
        relay_picked_mate(level)
        relay(hh, level, 4, xh_s, xh_r, xhp_s, xhp_r)
        relay(ww, level, 1, xw_s, xw_r, xwp_s, xwp_r)
        settle_picked(level)
        hear(level)
        settle(hh, level, 4, xhp_s, xhp_r)
        settle(ww, level, 1, xwp_s, xwp_r)
        pp[1 - side] = mm(ww[level, 1 - side], hh[level, 1 - side], 1, 0)

    for copy in sends:
        copy.wait_send()
    for level in range(LEVELS):
        drain_picked(level)
        drain_relay(ww, level, 1, xwp_s, xwp_r)
        if level > 0:
            drain_relay(hh, level, 4, xhp_s, xhp_r)

    def drain(t, carry):
        same = zpeer(zorder(t)) * 2 + core
        put(block_of(same), block_of(same), gp_s.at[t], gp_r.at[t], keep=False, col=partner).wait_send()
        put(pick_rows(same), pick_rows(same), pp_s.at[t], pp_r.at[t], keep=False, col=partner).wait_send()
        return carry

    lax.fori_loop(1, ZS, drain, 0)


def local(points, point_ids, signs, hadamard_sample_rows, samples, skeleton, ranks):
    rows = points.shape[1]
    width = samples.shape[1]
    r = skeleton.shape[1]
    count = r // COLS
    shape = jax.ShapeDtypeStruct
    fetched = pltpu.VMEM
    inputs = [points, point_ids[None], signs[None], hadamard_sample_rows[None], samples, skeleton, ranks]
    pair_of = [DMA((LEVELS, 2))] * 4
    sems = [
        DMA((7,)), *[DMA((ZS,))] * 8, DMA(()), DMA(()), *[DMA((ZS,))] * 10, *[DMA((LEVELS,))] * 2,
        *pair_of, *[DMA((LEVELS, 4))] * 4, *pair_of,
    ]
    basis, pk, sp, pp = pl.pallas_call(
        hss_kernel,
        out_shape=[
            shape((rows, r), BF16),
            shape((2, r, width), F32),
            shape((2, 8, r), F32),
            shape((2, r, width), F32),
        ],
        in_specs=[HBM] * 7,
        out_specs=[VM] * 4,
        scratch_shapes=[
            fetched((3, rows), F32),
            fetched((1, rows), jnp.int32),
            fetched((1, rows), jnp.int32),
            fetched((1, width), jnp.int32),
            fetched(skeleton.shape, jnp.int32),
            pltpu.SMEM(ranks.shape, jnp.int32),
            fetched((rows, width), BF16),
            fetched((COLS, 8, rows), F32),
            fetched((COLS, rows, width), BF16),
            fetched((3, rows, LANES), F32),
            fetched((3, r, LANES), F32),
            fetched((rows, width), F32),
            fetched((rows, r), F32),
            fetched((r, width), F32),
            fetched((r // 2, width), F32),
            fetched((r // 2, width), F32),
            fetched((ZS - 1, count, width), F32),
            fetched((r, width), F32),
            fetched((2, 2, r, width), F32),
            fetched((2, 2, 8, r), F32),
            fetched((LEVELS, 2, r, width), F32),
            fetched((LEVELS, 2, r, r), F32),
            *sems,
        ],
        compiler_params=pltpu.CompilerParams(
            collective_id=0, has_side_effects=True, vmem_limit_bytes=32 * 1024 * 1024
        ),
        name="hss",
    )(*[pltpu.with_memory_space_constraint(x, pltpu.HBM) for x in inputs])
    top = shape((r // 8, width // COLS), F32)
    return pl.pallas_call(
        top_kernel,
        out_shape=[shape((rows, r), BF16), top, top],
        in_specs=[VM, VM, VM, VM, VM, SM],
        out_specs=[ANY, VM, VM],
        scratch_shapes=[fetched((r, width), F32), fetched((r, r), F32), DMA(())],
        compiler_params=pltpu.CompilerParams(vmem_limit_bytes=32 * 1024 * 1024),
        name="top",
    )(basis, pk, pp, sp, skeleton, ranks)


def solution(mesh):
    placed = (
        P(None, ("leaf", "col")),
        P(("leaf", "col")),
        P(("leaf", "col")),
        P(),
        P(("leaf", "col"), None),
        P(),
        P(),
    )
    return jax.shard_map(
        local,
        mesh=mesh,
        in_specs=placed,
        out_specs=(P(("leaf", "col"), None), P("leaf", "col"), P("leaf", "col")),
        check_vma=False,
    )
```

```python
import jax
import jax.numpy as jnp
from jax import lax
from jax.experimental import pallas as pl
from jax.experimental.pallas import tpu as pltpu
from jax.sharding import PartitionSpec as P

MESH = pl.DeviceIdType.MESH
DMA = pltpu.SemaphoreType.DMA
F32 = jnp.float32
BF16 = jnp.bfloat16
VM = pl.BlockSpec(memory_space=pltpu.VMEM)
SM = pl.BlockSpec(memory_space=pltpu.SMEM)
ANY = pl.BlockSpec(memory_space=pl.ANY)
HBM = pl.BlockSpec(memory_space=pltpu.HBM)

NTOTAL = 1048576
KERNEL_SCALE = 1.0
RIDGE = 0.25
LOG2E = 1.4426950408889634
BITS = NTOTAL.bit_length() - 1
NBITS = 32
PANEL = 16
COLS = 16
ZS = COLS // 2
LANES = 128
LEVELS = 3


def bdot(a, b, ca, cb):
    return lax.dot_general(a, b, (((ca,), (cb,)), ((), ())), preferred_element_type=F32)


def split(x, count):
    pieces = []
    for _ in range(count - 1):
        piece = x.astype(BF16)
        pieces.append(piece)
        x = x - piece.astype(F32)
    return [*pieces, x.astype(BF16)]


def mm(a, b, ca, cb, terms=6):
    count = 3 if terms == 6 else 2
    pa, pb = split(a, count), split(b, count)
    pairs = [(i, j) for i in range(count) for j in range(count) if i + j < count]
    left = jnp.concatenate([pa[i] for i, _ in pairs], ca)
    right = jnp.concatenate([pb[j] for _, j in pairs], cb)
    return bdot(left, right, ca, cb)


def exact(a, b, ca, cb):
    pieces = split(a, 3)
    return bdot(jnp.concatenate(pieces, ca), jnp.concatenate([b] * 3, cb), ca, cb)


def iota(shape, axis):
    return lax.broadcasted_iota(jnp.int32, shape, axis)


def kern(squared_distance):
    return jnp.exp2(squared_distance * (-KERNEL_SCALE * LOG2E))


def spd_inverse(a_ref, scale, hook):
    n = a_ref.shape[0]
    lane = iota((PANEL, n), 1)
    sub = iota((PANEL, n), 0)
    ident = (lane == sub).astype(F32)
    lane_n = iota((n, n), 1)

    def step(b, carry):
        start = pl.multiple_of(b * PANEL, PANEL)
        panel = a_ref[pl.ds(start, PANEL), :]
        rolled = pltpu.roll(panel, lax.rem(n - start, n), 1)
        diag = [jnp.broadcast_to(rolled[:, k : k + 1], (PANEL, n)) for k in range(PANEL)]
        rows = jnp.where(lane < PANEL, ident, rolled)
        for k in range(0, PANEL, 2):
            one, two = diag[k], diag[k + 1]
            a, c = one[k : k + 1, :], two[k + 1 : k + 2, :]
            low, up = one[k + 1 : k + 2, :], two[k : k + 1, :]
            inv = 1.0 / (a * c - low * up)
            first, second = sub == k, sub == k + 1
            g0 = jnp.where(first, -c, jnp.where(second, low, one * c - two * low))
            g1 = jnp.where(first, up, jnp.where(second, -a, two * a - one * up))

            def sweep(x):
                base = jnp.where(first | second, 0.0, x)
                return base - (g0 * x[k : k + 1, :] + g1 * x[k + 1 : k + 2, :]) * inv

            for j in range(k + 2, PANEL):
                diag[j] = sweep(diag[j])
            rows = sweep(rows)
        rows = pltpu.roll(rows, start, 1)
        side = jnp.where(lane < start, -panel, panel)
        side = jnp.where((lane >= start) & (lane < start + PANEL), 0.0, side)
        change = mm(side, rows, 0, 0)
        cleared = jnp.where((lane_n >= start) & (lane_n < start + PANEL), 0.0, a_ref[...])
        a_ref[...] = cleared - change
        a_ref[pl.ds(start, PANEL), :] = rows
        hook(b)
        return carry

    lax.fori_loop(0, n // PANEL, step, 0)
    a_ref[...] = a_ref[...] * scale


def ridged(gram, rank):
    n = gram.shape[0]
    same = iota((n, n), 0) == iota((n, n), 1)
    trace = jnp.sum(jnp.where(same, gram, 0.0), keepdims=True)
    shift = RIDGE * trace / rank.astype(F32) + 1e-06
    scale = 1.0 / shift
    return gram * scale + jnp.where(same, 1.0, 0.0), scale


def unit8():
    return (iota((8, LANES), 0) == iota((8, LANES), 1)).astype(BF16)


def merge(level, leaf, pk, pp, sp, skel_ref, rank_ref):
    leaves = lax.axis_size("leaf")
    r = skel_ref.shape[1]
    child_base = sum(leaves >> k for k in range(level - 1))
    base = child_base + (leaves >> (level - 1))
    sub = iota((r, 1), 0)
    node = leaf // (1 << level)
    rank_l = rank_ref[child_base + 2 * node]
    rank_r = rank_ref[child_base + 2 * node + 1]
    rank_p = rank_ref[base + node]
    spots_l = exact(sp[0], unit8(), 0, 0)
    row_r = sp[1]
    d2 = None
    for axis in range(3):
        off = spots_l[:, axis : axis + 1] - row_r[axis : axis + 1, :]
        d2 = off * off if d2 is None else d2 + off * off
    cross = kern(d2)
    upper = (pk[0] - mm(cross, pp[1], 1, 0, 3)) * jnp.where(sub < rank_l, 1.0, 0.0)
    lower = (pk[1] - mm(cross, pp[0], 0, 0, 3)) * jnp.where(sub < rank_r, 1.0, 0.0)
    cand = jnp.concatenate([upper, lower], 0)
    spots = jnp.concatenate([sp[0], row_r], 1)
    row = skel_ref[pl.ds(base + node, 1), :]
    chooser = jnp.where(jnp.broadcast_to(row, (2 * r, r)) == iota((2 * r, r), 0), 1.0, 0.0).astype(BF16)
    chosen = bdot(jnp.concatenate([chooser] * 3, 0), jnp.concatenate(split(cand, 3), 0), 0, 0)
    return cand, spots, chooser, chosen * jnp.where(sub < rank_p, 1.0, 0.0), rank_p


def top_kernel(basis_ref, pk, pp, sp, skel_hbm, rank_hbm, basis_out, top_s, top_o, skel_ref, rank_ref, pk3, ww3, sem):
    fetches = [
        pltpu.make_async_copy(rank_hbm, rank_ref, sem.at[1]),
        pltpu.make_async_copy(skel_hbm, skel_ref, sem.at[2]),
    ]
    for fetch in fetches:
        fetch.start()
    save = pltpu.make_async_copy(basis_ref, basis_out, sem.at[0])
    save.start()
    for fetch in fetches:
        fetch.wait()
    leaf = lax.axis_index("leaf")
    me = lax.axis_index("col")
    width = pk.shape[2]
    share, span = top_s.shape
    cand, _, _, picked, rank = merge(LEVELS, leaf, pk, pp, sp, skel_ref, rank_ref)
    pk3[...] = picked
    raw = mm(cand, picked, 1, 1, 3)
    back = mm(raw, jnp.concatenate([pp[0], pp[1]], 0), 0, 0)
    ww3[...], scale = ridged(mm(picked, picked, 1, 1, 3), rank)
    spd_inverse(ww3, scale, lambda b: None)
    turn = lax.rem(width - me * span, width)
    rows = pl.ds(pl.multiple_of(lax.rem(leaf, 8) * share, share), share)
    top_s[...] = pltpu.roll(pk3[rows, :], turn, 1)[:, 0:span]
    top_o[...] = pltpu.roll(mm(ww3[rows, :], back, 1, 0), turn, 1)[:, 0:span]
    save.wait()


def hss_kernel(
    points_hbm, ids_hbm, signs_hbm, had_hbm, samp_hbm, skel_hbm, rank_hbm,
    basis_ref, pk_out, sp_out, pp,
    points_ref, ids_ref, signs_ref, had_ref, skel_ref, rank_ref, samp, every, om_all, own_b, pick_b, res, raw_ref, part, half, mine, landed, spk, pk_low, sp_low, hh, ww,
    samp_sem, g_s, g_r, gp_s, gp_r, p_s, p_r, pp_s, pp_r,
    pair_s, pair_r, rs_s, rs_r, ag_s, ag_r, ap_s, ap_r, ax_s, ax_r, axp_s, axp_r,
    xs_s, xs_r, xk_s, xk_r, xkp_s, xkp_r, xh_s, xh_r, xhp_s, xhp_r, xw_s, xw_r, xwp_s, xwp_r,
):
    leaf = lax.axis_index("leaf")
    me = lax.axis_index("col")
    leaves = lax.axis_size("leaf")
    core = lax.rem(me, 2)
    z = me // 2
    partner = me + 1 - 2 * core
    rows = points_ref.shape[1]
    width = had_ref.shape[1]
    r = skel_ref.shape[1]
    count = r // COLS
    pk = [pk_low.at[0], pk_low.at[1], pk_out]
    sp = [sp_low.at[0], sp_low.at[1], sp_out]
    zhalf = lax.rem(z, 2)
    zmate = (z + 1 - 2 * zhalf) * 2 + core
    sides = [lax.rem(leaf // (1 << lvl), 2) for lvl in range(LEVELS)]
    siblings = [leaf + (1 << lvl) - (2 << lvl) * sides[lvl] for lvl in range(LEVELS)]
    sends = []

    def put(src, dst, send, recv, keep=True, **device):
        copy = pltpu.make_async_remote_copy(
            src_ref=src, dst_ref=dst, send_sem=send, recv_sem=recv, device_id=device, device_id_type=MESH
        )
        if keep:
            sends.append(copy)
        return copy

    def zpeer(off):
        return lax.rem(z + off, ZS)

    fetches = [
        pltpu.make_async_copy(source, target, samp_sem.at[i])
        for i, (source, target) in enumerate(
            (
                (points_hbm, points_ref),
                (ids_hbm, ids_ref),
                (signs_hbm, signs_ref),
                (skel_hbm, skel_ref),
                (rank_hbm, rank_ref),
                (had_hbm, had_ref),
                (samp_hbm, samp),
            )
        )
    ]
    for fetch in fetches:
        fetch.start()
    barrier = pltpu.get_barrier_semaphore()
    for off in range(1, ZS):
        pl.semaphore_signal(barrier, inc=1, device_id={"col": zpeer(off) * 2 + core}, device_id_type=MESH)
    pl.semaphore_signal(barrier, inc=1, device_id={"col": partner}, device_id_type=MESH)
    for sibling in siblings:
        pl.semaphore_signal(barrier, inc=1, device_id={"leaf": sibling}, device_id_type=MESH)
    for fetch in fetches:
        fetch.wait()
    every[me, 0:3, :] = points_ref[...]
    every[me, 3:4, :] = ids_ref[...].astype(F32)
    every[me, 4:5, :] = signs_ref[...].astype(F32)
    every[:, 5:8, :] = jnp.zeros((COLS, 3, rows), F32)

    my_rows = pl.ds(pl.multiple_of(me * count, count), count)
    entry = skel_ref[pl.ds(leaf, 1), :]

    def chooser_of(slot):
        return jnp.where(
            jnp.broadcast_to(entry - slot * rows, (rows, r)) == iota((rows, r), 0), 1.0, 0.0
        ).astype(BF16)

    part[...] = bdot(chooser_of(me), samp[...], 0, 0)
    spk[my_rows, :] = part[my_rows, :]

    ident = unit8()
    own_cols = exact(every[me], ident, 0, 0)
    for axis in range(3):
        own_b[axis] = jnp.broadcast_to(own_cols[:, axis : axis + 1], (rows, LANES))
    bit_row = iota((NBITS, width), 0)
    had = jnp.broadcast_to(had_ref[...], (NBITS, width))
    had_bits = ((had >> jnp.minimum(bit_row, BITS)) & 1).astype(F32) * 0.5
    had_bits = jnp.where(bit_row == BITS, 0.5, jnp.where(bit_row == BITS + 1, 0.25, had_bits))
    had_bits = jnp.where(bit_row > BITS + 1, 0.0, had_bits).astype(BF16)
    res[...] = samp[...].astype(F32)
    pl.semaphore_wait(barrier, ZS + LEVELS)

    def pick_rows(slot):
        return spk.at[pl.ds(pl.multiple_of(slot * count, count), count)]

    def block_of(slot):
        return every.at[slot, pl.ds(0, 5)]

    order = (1, 7, 2, 6, 3, 5, 4)
    for off in order:
        put(block_of(me), block_of(me), g_s.at[off], g_r.at[ZS - off], col=zpeer(off) * 2 + core).start()
    put(block_of(me), block_of(me), gp_s.at[0], gp_r.at[0], col=partner).start()
    for off in order:
        put(pick_rows(me), pick_rows(me), p_s.at[off], p_r.at[ZS - off], col=zpeer(off) * 2 + core).start()
    put(pick_rows(me), pick_rows(me), pp_s.at[0], pp_r.at[0], col=partner).start()

    def omega4(block):
        shift = iota((NBITS, rows), 0)
        ids = jnp.broadcast_to(block[3:4, :].astype(jnp.int32), (NBITS, rows))
        bits = ((ids >> jnp.minimum(shift, BITS)) & 1).astype(F32)
        bits = jnp.where(shift == BITS, 1.0 - block[4:5, :], bits)
        bits = jnp.where(shift == BITS + 1, 1.0, bits)
        bits = jnp.where(shift > BITS + 1, 0.0, bits).astype(BF16)
        halves = bdot(bits, had_bits, 0, 0)
        return (halves - jnp.round(halves)).astype(BF16)

    def zorder(t):
        return lax.rem(jnp.where(lax.rem(t, 2) == 1, (t + 1) // 2, ZS - t // 2), ZS)

    def tile_of(columns, block):
        tiles = []
        for c in range(rows // LANES):
            d2 = None
            for axis in range(3):
                off = columns[axis] - block[axis : axis + 1, c * LANES : (c + 1) * LANES]
                d2 = off * off if d2 is None else d2 + off * off
            tiles.append(kern(d2).astype(BF16))
        return jnp.concatenate(tiles, 1)

    def near_step(t, spots):
        off = zorder(t)
        there = zpeer(off)
        same = there * 2 + core
        other = there * 2 + 1 - core

        @pl.when(t > 0)
        def _():
            put(block_of(same), block_of(same), g_s.at[off], g_r.at[off], keep=False, col=partner).wait_recv()
            put(block_of(same), block_of(same), gp_s.at[t], gp_r.at[t], keep=False, col=partner).start()

        put(block_of(other), block_of(other), gp_s.at[t], gp_r.at[t], keep=False, col=partner).wait_recv()
        columns = [own_b[axis] for axis in range(3)]
        tiles, omegas = [], []
        for k in range(2):
            block = every[there * 2 + k]
            spots = spots + exact(block, chooser_of(there * 2 + k), 1, 0)
            om = omega4(block)
            om_all[there * 2 + k] = om
            omegas.append(om)
            tiles.append(tile_of(columns, block))
        res[...] -= 0.25 * bdot(jnp.concatenate(tiles, 1), jnp.concatenate(omegas, 0), 1, 0)

        return spots

    spots = lax.fori_loop(0, ZS, near_step, jnp.zeros((8, r), F32))
    sp[0][sides[0]] = spots
    put(sp[0].at[sides[0]], sp[0].at[sides[0]], xs_s.at[0], xs_r.at[0], leaf=siblings[0]).start()

    spot_cols = exact(spots, ident, 0, 0)
    for axis in range(3):
        pick_b[axis] = jnp.broadcast_to(spot_cols[:, axis : axis + 1], (r, LANES))
    part[...] = jnp.zeros((r, width), F32)

    def pick_relay(t, carry):
        off = zorder(t)
        same = zpeer(off) * 2 + core
        put(pick_rows(same), pick_rows(same), p_s.at[off], p_r.at[off], keep=False, col=partner).wait_recv()
        put(pick_rows(same), pick_rows(same), pp_s.at[t], pp_r.at[t], keep=False, col=partner).start()
        return carry

    lax.fori_loop(1, ZS, pick_relay, 0)

    def pick_step(t, carry):
        there = zpeer(zorder(t))
        columns = [pick_b[axis] for axis in range(3)]
        tile = jnp.concatenate([tile_of(columns, every[there * 2 + k]) for k in range(2)], 1)
        part[...] += bdot(tile, om_all[pl.ds(there * 2, 2)].reshape(2 * rows, width), 1, 0)
        return carry

    lax.fori_loop(0, ZS, pick_step, 0)

    def pick_settle(t, carry):
        other = zpeer(zorder(t)) * 2 + 1 - core
        put(pick_rows(other), pick_rows(other), pp_s.at[t], pp_r.at[t], keep=False, col=partner).wait_recv()
        return carry

    lax.fori_loop(0, ZS, pick_settle, 0)
    sub = iota((r, 1), 0)
    pk[0][sides[0]] = (spk[...] - 0.25 * part[...]) * jnp.where(sub < rank_ref[leaf], 1.0, 0.0)

    def pieces(buf, level, side, chunks, half_of):
        size = r // 2 // chunks
        return [buf.at[level, side, pl.ds(pl.multiple_of(half_of * (r // 2) + q * size, size), size)] for q in range(chunks)]

    def offer(buf, level, chunks, s, rv):
        for q, piece in enumerate(pieces(buf, level, sides[level], chunks, core)):
            put(piece, piece, s.at[level, q], rv.at[level, q], leaf=siblings[level]).start()

    def relay(buf, level, chunks, s, rv, s2, rv2):
        for q, piece in enumerate(pieces(buf, level, 1 - sides[level], chunks, core)):
            put(piece, piece, s.at[level, q], rv.at[level, q], keep=False, leaf=siblings[level]).wait_recv()
            put(piece, piece, s2.at[level, q], rv2.at[level, q], keep=False, col=partner).start()

    def settle(buf, level, chunks, s2, rv2):
        for q, piece in enumerate(pieces(buf, level, 1 - sides[level], chunks, 1 - core)):
            put(piece, piece, s2.at[level, q], rv2.at[level, q], keep=False, col=partner).wait_recv()

    def quarter(level, side, half_of, chip):
        size = r // 4
        return pk[level].at[side, pl.ds(pl.multiple_of((half_of * 2 + chip) * size, size), size)]

    def offer_picked(level):
        piece = quarter(level, sides[level], core, zhalf)
        put(piece, piece, xk_s.at[level, 0], xk_r.at[level, 0], leaf=siblings[level]).start()

    def relay_picked(level):
        got = quarter(level, 1 - sides[level], core, zhalf)
        put(got, got, xk_s.at[level, 0], xk_r.at[level, 0], keep=False, leaf=siblings[level]).wait_recv()
        put(got, got, xk_s.at[level, 1], xk_r.at[level, 1], keep=False, col=zmate).start()
        put(got, got, xkp_s.at[level, 0], xkp_r.at[level, 0], keep=False, col=partner).start()

    def relay_picked_mate(level):
        got = quarter(level, 1 - sides[level], core, 1 - zhalf)
        put(got, got, xk_s.at[level, 1], xk_r.at[level, 1], keep=False, col=zmate).wait_recv()
        put(got, got, xkp_s.at[level, 1], xkp_r.at[level, 1], keep=False, col=partner).start()

    def settle_picked(level):
        for q, chip in enumerate((zhalf, 1 - zhalf)):
            got = quarter(level, 1 - sides[level], 1 - core, chip)
            put(got, got, xkp_s.at[level, q], xkp_r.at[level, q], keep=False, col=partner).wait_recv()

    def drain_picked(level):
        got = quarter(level, 1 - sides[level], core, zhalf)
        put(got, got, xk_s.at[level, 1], xk_r.at[level, 1], keep=False, col=zmate).wait_send()
        for q in range(2):
            put(got, got, xkp_s.at[level, q], xkp_r.at[level, q], keep=False, col=partner).wait_send()

    def hear(level):
        got = sp[level].at[1 - sides[level]]
        put(got, got, xs_s.at[level], xs_r.at[level], keep=False, leaf=siblings[level]).wait_recv()

    def drain_relay(buf, level, chunks, s2, rv2):
        for q, piece in enumerate(pieces(buf, level, 1 - sides[level], chunks, core)):
            put(piece, piece, s2.at[level, q], rv2.at[level, q], keep=False, col=partner).wait_send()

    offer_picked(0)

    side0 = sides[0]
    picked = pk[0][side0]
    raw = mm(res[...], picked, 1, 1)
    raw_ref[...] = raw
    om_own = om_all[me]
    part[...] = 0.25 * exact(raw, om_own, 0, 0)
    r2 = r // 2
    own0 = pl.multiple_of(core * r2, r2)
    other0 = pl.multiple_of((1 - core) * r2, r2)
    pair = put(part.at[pl.ds(other0, r2)], half, pair_s, pair_r, col=partner)
    pair.start()
    ww[0, side0], scale = ridged(mm(picked, picked, 1, 1), rank_ref[leaf])
    scatter = []
    for off in range(1, ZS):
        piece = pl.ds(pl.multiple_of(zpeer(off) * count, count), count)
        scatter.append(put(mine.at[piece], landed.at[off - 1], rs_s.at[off], rs_r.at[off], col=zpeer(off) * 2 + core))

    def leaf_hook(b):
        @pl.when(b == 2)
        def _():
            pair.wait_recv()
            mine[...] = part[pl.ds(own0, r2)] + half[...]
            for copy in scatter:
                copy.start()

        @pl.when(b == 6)
        def _():
            relay_picked(0)

    spd_inverse(ww.at[0, side0], scale, leaf_hook)
    offer(ww, 0, 1, xw_s, xw_r)
    basis_ref[...] = mm(raw_ref[...], ww[0, side0], 1, 0).astype(BF16)

    def n_rows(side, half_of, chip):
        return hh.at[0, side, pl.ds(pl.multiple_of(half_of * r2 + chip * count, count), count)]

    total = mine[pl.ds(pl.multiple_of(z * count, count), count)]
    for off in range(1, ZS):
        scatter[off - 1].wait_recv()
        total = total + landed[off - 1]
    hh[0, side0, pl.ds(pl.multiple_of(own0 + z * count, count), count)] = total
    here = n_rows(side0, core, z)
    for off in (1, 7, 2, 6, 3, 5, 4):
        put(here, here, ag_s.at[off], ag_r.at[ZS - off], col=zpeer(off) * 2 + core).start()
    put(here, here, ap_s.at[0], ap_r.at[0], col=partner).start()
    put(here, here, ax_s.at[0], ax_r.at[0], leaf=siblings[0]).start()
    for off in (1, 7, 2, 6, 3, 5, 4):
        got = n_rows(side0, core, zpeer(off))
        put(got, got, ag_s.at[off], ag_r.at[off], keep=False, col=partner).wait_recv()
        put(got, got, ap_s.at[off], ap_r.at[off], col=partner).start()
        put(got, got, ax_s.at[off], ax_r.at[off], leaf=siblings[0]).start()
    relay_picked_mate(0)
    relay(ww, 0, 1, xw_s, xw_r, xwp_s, xwp_r)
    for off in (0, 1, 7, 2, 6, 3, 5, 4):
        got = n_rows(1 - side0, core, zpeer(off))
        put(got, got, ax_s.at[off], ax_r.at[off], keep=False, leaf=siblings[0]).wait_recv()
        put(got, got, axp_s.at[off], axp_r.at[off], col=partner).start()
    for off in range(ZS):
        got = n_rows(side0, 1 - core, zpeer(off))
        put(got, got, ap_s.at[off], ap_r.at[off], keep=False, col=partner).wait_recv()
    pp[side0] = mm(ww[0, side0], hh[0, side0], 1, 0)
    settle_picked(0)
    hear(0)
    settle(ww, 0, 1, xwp_s, xwp_r)
    for off in range(ZS):
        got = n_rows(1 - side0, 1 - core, zpeer(off))
        put(got, got, axp_s.at[off], axp_r.at[off], keep=False, col=partner).wait_recv()
    pp[1 - side0] = mm(ww[0, 1 - side0], hh[0, 1 - side0], 1, 0)

    for level in range(1, LEVELS):
        side = sides[level]
        cand, spots, chooser, picked, rank = merge(level, leaf, pk[level - 1], pp, sp[level - 1], skel_ref, rank_ref)
        pk[level][side] = picked
        offer_picked(level)
        sp[level][side] = exact(spots, chooser, 1, 0)
        put(sp[level].at[side], sp[level].at[side], xs_s.at[level], xs_r.at[level], leaf=siblings[level]).start()
        raw = mm(cand, picked, 1, 1, 3)
        hh[level, side] = mm(raw, jnp.concatenate([pp[0], pp[1]], 0), 0, 0)
        offer(hh, level, 4, xh_s, xh_r)
        ww[level, side], scale = ridged(mm(picked, picked, 1, 1, 3), rank)

        def hook(b, level=level):
            @pl.when(b == 5)
            def _():
                relay_picked(level)

        spd_inverse(ww.at[level, side], scale, hook)
        offer(ww, level, 1, xw_s, xw_r)
        pp[side] = mm(ww[level, side], hh[level, side], 1, 0)
        relay_picked_mate(level)
        relay(hh, level, 4, xh_s, xh_r, xhp_s, xhp_r)
        relay(ww, level, 1, xw_s, xw_r, xwp_s, xwp_r)
        settle_picked(level)
        hear(level)
        settle(hh, level, 4, xhp_s, xhp_r)
        settle(ww, level, 1, xwp_s, xwp_r)
        pp[1 - side] = mm(ww[level, 1 - side], hh[level, 1 - side], 1, 0)

    for copy in sends:
        copy.wait_send()
    for level in range(LEVELS):
        drain_picked(level)
        drain_relay(ww, level, 1, xwp_s, xwp_r)
        if level > 0:
            drain_relay(hh, level, 4, xhp_s, xhp_r)

    def drain(t, carry):
        same = zpeer(zorder(t)) * 2 + core
        put(block_of(same), block_of(same), gp_s.at[t], gp_r.at[t], keep=False, col=partner).wait_send()
        put(pick_rows(same), pick_rows(same), pp_s.at[t], pp_r.at[t], keep=False, col=partner).wait_send()
        return carry

    lax.fori_loop(1, ZS, drain, 0)


def local(points, point_ids, signs, hadamard_sample_rows, samples, skeleton, ranks):
    rows = points.shape[1]
    width = samples.shape[1]
    r = skeleton.shape[1]
    count = r // COLS
    shape = jax.ShapeDtypeStruct
    fetched = pltpu.VMEM
    inputs = [points, point_ids[None], signs[None], hadamard_sample_rows[None], samples, skeleton, ranks]
    pair_of = [DMA((LEVELS, 2))] * 4
    sems = [
        DMA((7,)), *[DMA((ZS,))] * 8, DMA(()), DMA(()), *[DMA((ZS,))] * 10, *[DMA((LEVELS,))] * 2,
        *pair_of, *[DMA((LEVELS, 4))] * 4, *pair_of,
    ]
    basis, pk, sp, pp = pl.pallas_call(
        hss_kernel,
        out_shape=[
            shape((rows, r), BF16),
            shape((2, r, width), F32),
            shape((2, 8, r), F32),
            shape((2, r, width), F32),
        ],
        in_specs=[HBM] * 7,
        out_specs=[VM] * 4,
        scratch_shapes=[
            fetched((3, rows), F32),
            fetched((1, rows), jnp.int32),
            fetched((1, rows), jnp.int32),
            fetched((1, width), jnp.int32),
            fetched(skeleton.shape, jnp.int32),
            pltpu.SMEM(ranks.shape, jnp.int32),
            fetched((rows, width), BF16),
            fetched((COLS, 8, rows), F32),
            fetched((COLS, rows, width), BF16),
            fetched((3, rows, LANES), F32),
            fetched((3, r, LANES), F32),
            fetched((rows, width), F32),
            fetched((rows, r), F32),
            fetched((r, width), F32),
            fetched((r // 2, width), F32),
            fetched((r // 2, width), F32),
            fetched((ZS - 1, count, width), F32),
            fetched((r, width), F32),
            fetched((2, 2, r, width), F32),
            fetched((2, 2, 8, r), F32),
            fetched((LEVELS, 2, r, width), F32),
            fetched((LEVELS, 2, r, r), F32),
            *sems,
        ],
        compiler_params=pltpu.CompilerParams(
            collective_id=0, has_side_effects=True, vmem_limit_bytes=32 * 1024 * 1024
        ),
        name="hss",
    )(*[pltpu.with_memory_space_constraint(x, pltpu.HBM) for x in inputs])
    top = shape((r // 8, width // COLS), F32)
    return pl.pallas_call(
        top_kernel,
        out_shape=[shape((rows, r), BF16), top, top],
        in_specs=[VM, VM, VM, VM, HBM, HBM],
        out_specs=[ANY, VM, VM],
        scratch_shapes=[
            fetched(skeleton.shape, jnp.int32),
            pltpu.SMEM(ranks.shape, jnp.int32),
            fetched((r, width), F32),
            fetched((r, r), F32),
            DMA((3,)),
        ],
        compiler_params=pltpu.CompilerParams(vmem_limit_bytes=32 * 1024 * 1024),
        name="top",
    )(basis, pk, pp, sp, *[pltpu.with_memory_space_constraint(x, pltpu.HBM) for x in (skeleton, ranks)])


def solution(mesh):
    placed = (
        P(None, ("leaf", "col")),
        P(("leaf", "col")),
        P(("leaf", "col")),
        P(),
        P(("leaf", "col"), None),
        P(),
        P(),
    )
    return jax.shard_map(
        local,
        mesh=mesh,
        in_specs=placed,
        out_specs=(P(("leaf", "col"), None), P("leaf", "col"), P("leaf", "col")),
        check_vma=False,
    )
```

```python
import jax
import jax.numpy as jnp
from jax import lax
from jax.experimental import pallas as pl
from jax.experimental.pallas import tpu as pltpu
from jax.sharding import PartitionSpec as P

MESH = pl.DeviceIdType.MESH
DMA = pltpu.SemaphoreType.DMA
F32 = jnp.float32
BF16 = jnp.bfloat16
VM = pl.BlockSpec(memory_space=pltpu.VMEM)
SM = pl.BlockSpec(memory_space=pltpu.SMEM)
ANY = pl.BlockSpec(memory_space=pl.ANY)
HBM = pl.BlockSpec(memory_space=pltpu.HBM)

NTOTAL = 1048576
KERNEL_SCALE = 1.0
RIDGE = 0.25
LOG2E = 1.4426950408889634
BITS = NTOTAL.bit_length() - 1
NBITS = 32
PANEL = 16
COLS = 16
ZS = COLS // 2
LANES = 128
LEVELS = 3


def bdot(a, b, ca, cb):
    return lax.dot_general(a, b, (((ca,), (cb,)), ((), ())), preferred_element_type=F32)


def split(x, count):
    pieces = []
    for _ in range(count - 1):
        piece = x.astype(BF16)
        pieces.append(piece)
        x = x - piece.astype(F32)
    return [*pieces, x.astype(BF16)]


def mm(a, b, ca, cb, terms=6):
    count = 3 if terms == 6 else 2
    pa, pb = split(a, count), split(b, count)
    pairs = [(i, j) for i in range(count) for j in range(count) if i + j < count]
    left = jnp.concatenate([pa[i] for i, _ in pairs], ca)
    right = jnp.concatenate([pb[j] for _, j in pairs], cb)
    return bdot(left, right, ca, cb)


def exact(a, b, ca, cb):
    pieces = split(a, 3)
    return bdot(jnp.concatenate(pieces, ca), jnp.concatenate([b] * 3, cb), ca, cb)


def iota(shape, axis):
    return lax.broadcasted_iota(jnp.int32, shape, axis)


def kern(squared_distance):
    return jnp.exp2(squared_distance * (-KERNEL_SCALE * LOG2E))


def spd_inverse(a_ref, scale, hook):
    n = a_ref.shape[0]
    lane = iota((PANEL, n), 1)
    sub = iota((PANEL, n), 0)
    ident = (lane == sub).astype(F32)
    lane_n = iota((n, n), 1)

    def step(b, carry):
        start = pl.multiple_of(b * PANEL, PANEL)
        panel = a_ref[pl.ds(start, PANEL), :]
        rolled = pltpu.roll(panel, lax.rem(n - start, n), 1)
        diag = [jnp.broadcast_to(rolled[:, k : k + 1], (PANEL, n)) for k in range(PANEL)]
        rows = jnp.where(lane < PANEL, ident, rolled)
        for k in range(0, PANEL, 2):
            one, two = diag[k], diag[k + 1]
            a, c = one[k : k + 1, :], two[k + 1 : k + 2, :]
            low, up = one[k + 1 : k + 2, :], two[k : k + 1, :]
            inv = 1.0 / (a * c - low * up)
            first, second = sub == k, sub == k + 1
            g0 = jnp.where(first, -c, jnp.where(second, low, one * c - two * low))
            g1 = jnp.where(first, up, jnp.where(second, -a, two * a - one * up))

            def sweep(x):
                base = jnp.where(first | second, 0.0, x)
                return base - (g0 * x[k : k + 1, :] + g1 * x[k + 1 : k + 2, :]) * inv

            for j in range(k + 2, PANEL):
                diag[j] = sweep(diag[j])
            rows = sweep(rows)
        rows = pltpu.roll(rows, start, 1)
        side = jnp.where(lane < start, -panel, panel)
        side = jnp.where((lane >= start) & (lane < start + PANEL), 0.0, side)
        change = mm(side, rows, 0, 0)
        cleared = jnp.where((lane_n >= start) & (lane_n < start + PANEL), 0.0, a_ref[...])
        a_ref[...] = cleared - change
        a_ref[pl.ds(start, PANEL), :] = rows
        hook(b)
        return carry

    lax.fori_loop(0, n // PANEL, step, 0)
    a_ref[...] = a_ref[...] * scale


def ridged(gram, rank):
    n = gram.shape[0]
    same = iota((n, n), 0) == iota((n, n), 1)
    trace = jnp.sum(jnp.where(same, gram, 0.0), keepdims=True)
    shift = RIDGE * trace / rank.astype(F32) + 1e-06
    scale = 1.0 / shift
    return gram * scale + jnp.where(same, 1.0, 0.0), scale


def unit8():
    return (iota((8, LANES), 0) == iota((8, LANES), 1)).astype(BF16)


def node_of(level, leaf, skel_ref, rank_ref):
    leaves = lax.axis_size("leaf")
    child_base = sum(leaves >> k for k in range(level - 1))
    base = child_base + (leaves >> (level - 1))
    node = leaf // (1 << level)
    ranks = (rank_ref[child_base + 2 * node], rank_ref[child_base + 2 * node + 1], rank_ref[base + node])
    return skel_ref[pl.ds(base + node, 1), :], ranks


def merge(row, ranks, pk, pp, sp):
    rank_l, rank_r, rank_p = ranks
    r = row.shape[1]
    sub = iota((r, 1), 0)
    spots_l = exact(sp[0], unit8(), 0, 0)
    row_r = sp[1]
    d2 = None
    for axis in range(3):
        off = spots_l[:, axis : axis + 1] - row_r[axis : axis + 1, :]
        d2 = off * off if d2 is None else d2 + off * off
    cross = kern(d2)
    upper = (pk[0] - mm(cross, pp[1], 1, 0, 3)) * jnp.where(sub < rank_l, 1.0, 0.0)
    lower = (pk[1] - mm(cross, pp[0], 0, 0, 3)) * jnp.where(sub < rank_r, 1.0, 0.0)
    cand = jnp.concatenate([upper, lower], 0)
    spots = jnp.concatenate([sp[0], row_r], 1)
    chooser = jnp.where(jnp.broadcast_to(row, (2 * r, r)) == iota((2 * r, r), 0), 1.0, 0.0).astype(BF16)
    chosen = bdot(jnp.concatenate([chooser] * 3, 0), jnp.concatenate(split(cand, 3), 0), 0, 0)
    return cand, spots, chooser, chosen * jnp.where(sub < rank_p, 1.0, 0.0)


def top_kernel(basis_ref, pk, pp, sp, meta, basis_out, top_s, top_o, pk3, ww3, sem):
    save = pltpu.make_async_copy(basis_ref, basis_out, sem)
    save.start()
    leaf = lax.axis_index("leaf")
    me = lax.axis_index("col")
    width = pk.shape[2]
    share, span = top_s.shape
    ranks = [meta[1 + i : 2 + i, 0:1] for i in range(3)]
    cand, _, _, picked = merge(meta[0:1, :], ranks, pk, pp, sp)
    pk3[...] = picked
    raw = mm(cand, picked, 1, 1, 3)
    back = mm(raw, jnp.concatenate([pp[0], pp[1]], 0), 0, 0)
    ww3[...], scale = ridged(mm(picked, picked, 1, 1, 3), ranks[2])
    spd_inverse(ww3, scale, lambda b: None)
    turn = lax.rem(width - me * span, width)
    rows = pl.ds(pl.multiple_of(lax.rem(leaf, 8) * share, share), share)
    top_s[...] = pltpu.roll(pk3[rows, :], turn, 1)[:, 0:span]
    top_o[...] = pltpu.roll(mm(ww3[rows, :], back, 1, 0), turn, 1)[:, 0:span]
    save.wait()


def hss_kernel(
    points_hbm, ids_hbm, signs_hbm, had_hbm, samp_hbm, skel_hbm, rank_hbm,
    basis_ref, pk_out, sp_out, pp, meta,
    points_ref, ids_ref, signs_ref, had_ref, skel_ref, rank_ref, samp, every, om_all, own_b, pick_b, res, raw_ref, part, half, mine, landed, spk, pk_low, sp_low, hh, ww,
    samp_sem, g_s, g_r, gp_s, gp_r, p_s, p_r, pp_s, pp_r,
    pair_s, pair_r, rs_s, rs_r, ag_s, ag_r, ap_s, ap_r, ax_s, ax_r, axp_s, axp_r,
    xs_s, xs_r, xk_s, xk_r, xkp_s, xkp_r, xh_s, xh_r, xhp_s, xhp_r, xw_s, xw_r, xwp_s, xwp_r,
):
    leaf = lax.axis_index("leaf")
    me = lax.axis_index("col")
    leaves = lax.axis_size("leaf")
    core = lax.rem(me, 2)
    z = me // 2
    partner = me + 1 - 2 * core
    rows = points_ref.shape[1]
    width = had_ref.shape[1]
    r = skel_ref.shape[1]
    count = r // COLS
    pk = [pk_low.at[0], pk_low.at[1], pk_out]
    sp = [sp_low.at[0], sp_low.at[1], sp_out]
    zhalf = lax.rem(z, 2)
    zmate = (z + 1 - 2 * zhalf) * 2 + core
    sides = [lax.rem(leaf // (1 << lvl), 2) for lvl in range(LEVELS)]
    siblings = [leaf + (1 << lvl) - (2 << lvl) * sides[lvl] for lvl in range(LEVELS)]
    sends = []

    def put(src, dst, send, recv, keep=True, **device):
        copy = pltpu.make_async_remote_copy(
            src_ref=src, dst_ref=dst, send_sem=send, recv_sem=recv, device_id=device, device_id_type=MESH
        )
        if keep:
            sends.append(copy)
        return copy

    def zpeer(off):
        return lax.rem(z + off, ZS)

    fetches = [
        pltpu.make_async_copy(source, target, samp_sem.at[i])
        for i, (source, target) in enumerate(
            (
                (points_hbm, points_ref),
                (ids_hbm, ids_ref),
                (signs_hbm, signs_ref),
                (skel_hbm, skel_ref),
                (rank_hbm, rank_ref),
                (had_hbm, had_ref),
                (samp_hbm, samp),
            )
        )
    ]
    for fetch in fetches:
        fetch.start()
    barrier = pltpu.get_barrier_semaphore()
    for off in range(1, ZS):
        pl.semaphore_signal(barrier, inc=1, device_id={"col": zpeer(off) * 2 + core}, device_id_type=MESH)
    pl.semaphore_signal(barrier, inc=1, device_id={"col": partner}, device_id_type=MESH)
    for sibling in siblings:
        pl.semaphore_signal(barrier, inc=1, device_id={"leaf": sibling}, device_id_type=MESH)
    for fetch in fetches:
        fetch.wait()
    every[me, 0:3, :] = points_ref[...]
    every[me, 3:4, :] = ids_ref[...].astype(F32)
    every[me, 4:5, :] = signs_ref[...].astype(F32)
    every[:, 5:8, :] = jnp.zeros((COLS, 3, rows), F32)

    my_rows = pl.ds(pl.multiple_of(me * count, count), count)
    entry = skel_ref[pl.ds(leaf, 1), :]

    def chooser_of(slot):
        return jnp.where(
            jnp.broadcast_to(entry - slot * rows, (rows, r)) == iota((rows, r), 0), 1.0, 0.0
        ).astype(BF16)

    part[...] = bdot(chooser_of(me), samp[...], 0, 0)
    spk[my_rows, :] = part[my_rows, :]

    ident = unit8()
    own_cols = exact(every[me], ident, 0, 0)
    for axis in range(3):
        own_b[axis] = jnp.broadcast_to(own_cols[:, axis : axis + 1], (rows, LANES))
    bit_row = iota((NBITS, width), 0)
    had = jnp.broadcast_to(had_ref[...], (NBITS, width))
    had_bits = ((had >> jnp.minimum(bit_row, BITS)) & 1).astype(F32) * 0.5
    had_bits = jnp.where(bit_row == BITS, 0.5, jnp.where(bit_row == BITS + 1, 0.25, had_bits))
    had_bits = jnp.where(bit_row > BITS + 1, 0.0, had_bits).astype(BF16)
    res[...] = samp[...].astype(F32)
    pl.semaphore_wait(barrier, ZS + LEVELS)

    def pick_rows(slot):
        return spk.at[pl.ds(pl.multiple_of(slot * count, count), count)]

    def block_of(slot):
        return every.at[slot, pl.ds(0, 5)]

    order = (1, 7, 2, 6, 3, 5, 4)
    for off in order:
        put(block_of(me), block_of(me), g_s.at[off], g_r.at[ZS - off], col=zpeer(off) * 2 + core).start()
    put(block_of(me), block_of(me), gp_s.at[0], gp_r.at[0], col=partner).start()
    for off in order:
        put(pick_rows(me), pick_rows(me), p_s.at[off], p_r.at[ZS - off], col=zpeer(off) * 2 + core).start()
    put(pick_rows(me), pick_rows(me), pp_s.at[0], pp_r.at[0], col=partner).start()

    def omega4(block):
        shift = iota((NBITS, rows), 0)
        ids = jnp.broadcast_to(block[3:4, :].astype(jnp.int32), (NBITS, rows))
        bits = ((ids >> jnp.minimum(shift, BITS)) & 1).astype(F32)
        bits = jnp.where(shift == BITS, 1.0 - block[4:5, :], bits)
        bits = jnp.where(shift == BITS + 1, 1.0, bits)
        bits = jnp.where(shift > BITS + 1, 0.0, bits).astype(BF16)
        halves = bdot(bits, had_bits, 0, 0)
        return (halves - jnp.round(halves)).astype(BF16)

    def zorder(t):
        return lax.rem(jnp.where(lax.rem(t, 2) == 1, (t + 1) // 2, ZS - t // 2), ZS)

    def tile_of(columns, block):
        tiles = []
        for c in range(rows // LANES):
            d2 = None
            for axis in range(3):
                off = columns[axis] - block[axis : axis + 1, c * LANES : (c + 1) * LANES]
                d2 = off * off if d2 is None else d2 + off * off
            tiles.append(kern(d2).astype(BF16))
        return jnp.concatenate(tiles, 1)

    def near_step(t, spots):
        off = zorder(t)
        there = zpeer(off)
        same = there * 2 + core
        other = there * 2 + 1 - core

        @pl.when(t > 0)
        def _():
            put(block_of(same), block_of(same), g_s.at[off], g_r.at[off], keep=False, col=partner).wait_recv()
            put(block_of(same), block_of(same), gp_s.at[t], gp_r.at[t], keep=False, col=partner).start()

        put(block_of(other), block_of(other), gp_s.at[t], gp_r.at[t], keep=False, col=partner).wait_recv()
        columns = [own_b[axis] for axis in range(3)]
        tiles, omegas = [], []
        for k in range(2):
            block = every[there * 2 + k]
            spots = spots + exact(block, chooser_of(there * 2 + k), 1, 0)
            om = omega4(block)
            om_all[there * 2 + k] = om
            omegas.append(om)
            tiles.append(tile_of(columns, block))
        res[...] -= 0.25 * bdot(jnp.concatenate(tiles, 1), jnp.concatenate(omegas, 0), 1, 0)

        return spots

    spots = lax.fori_loop(0, ZS, near_step, jnp.zeros((8, r), F32))
    sp[0][sides[0]] = spots
    put(sp[0].at[sides[0]], sp[0].at[sides[0]], xs_s.at[0], xs_r.at[0], leaf=siblings[0]).start()

    spot_cols = exact(spots, ident, 0, 0)
    for axis in range(3):
        pick_b[axis] = jnp.broadcast_to(spot_cols[:, axis : axis + 1], (r, LANES))
    part[...] = jnp.zeros((r, width), F32)

    def pick_relay(t, carry):
        off = zorder(t)
        same = zpeer(off) * 2 + core
        put(pick_rows(same), pick_rows(same), p_s.at[off], p_r.at[off], keep=False, col=partner).wait_recv()
        put(pick_rows(same), pick_rows(same), pp_s.at[t], pp_r.at[t], keep=False, col=partner).start()
        return carry

    lax.fori_loop(1, ZS, pick_relay, 0)

    def pick_step(t, carry):
        there = zpeer(zorder(t))
        columns = [pick_b[axis] for axis in range(3)]
        tile = jnp.concatenate([tile_of(columns, every[there * 2 + k]) for k in range(2)], 1)
        part[...] += bdot(tile, om_all[pl.ds(there * 2, 2)].reshape(2 * rows, width), 1, 0)
        return carry

    lax.fori_loop(0, ZS, pick_step, 0)

    def pick_settle(t, carry):
        other = zpeer(zorder(t)) * 2 + 1 - core
        put(pick_rows(other), pick_rows(other), pp_s.at[t], pp_r.at[t], keep=False, col=partner).wait_recv()
        return carry

    lax.fori_loop(0, ZS, pick_settle, 0)
    sub = iota((r, 1), 0)
    pk[0][sides[0]] = (spk[...] - 0.25 * part[...]) * jnp.where(sub < rank_ref[leaf], 1.0, 0.0)

    def pieces(buf, level, side, chunks, half_of):
        size = r // 2 // chunks
        return [buf.at[level, side, pl.ds(pl.multiple_of(half_of * (r // 2) + q * size, size), size)] for q in range(chunks)]

    def offer(buf, level, chunks, s, rv):
        for q, piece in enumerate(pieces(buf, level, sides[level], chunks, core)):
            put(piece, piece, s.at[level, q], rv.at[level, q], leaf=siblings[level]).start()

    def relay(buf, level, chunks, s, rv, s2, rv2):
        for q, piece in enumerate(pieces(buf, level, 1 - sides[level], chunks, core)):
            put(piece, piece, s.at[level, q], rv.at[level, q], keep=False, leaf=siblings[level]).wait_recv()
            put(piece, piece, s2.at[level, q], rv2.at[level, q], keep=False, col=partner).start()

    def settle(buf, level, chunks, s2, rv2):
        for q, piece in enumerate(pieces(buf, level, 1 - sides[level], chunks, 1 - core)):
            put(piece, piece, s2.at[level, q], rv2.at[level, q], keep=False, col=partner).wait_recv()

    def quarter(level, side, half_of, chip):
        size = r // 4
        return pk[level].at[side, pl.ds(pl.multiple_of((half_of * 2 + chip) * size, size), size)]

    def offer_picked(level):
        piece = quarter(level, sides[level], core, zhalf)
        put(piece, piece, xk_s.at[level, 0], xk_r.at[level, 0], leaf=siblings[level]).start()

    def relay_picked(level):
        got = quarter(level, 1 - sides[level], core, zhalf)
        put(got, got, xk_s.at[level, 0], xk_r.at[level, 0], keep=False, leaf=siblings[level]).wait_recv()
        put(got, got, xk_s.at[level, 1], xk_r.at[level, 1], keep=False, col=zmate).start()
        put(got, got, xkp_s.at[level, 0], xkp_r.at[level, 0], keep=False, col=partner).start()

    def relay_picked_mate(level):
        got = quarter(level, 1 - sides[level], core, 1 - zhalf)
        put(got, got, xk_s.at[level, 1], xk_r.at[level, 1], keep=False, col=zmate).wait_recv()
        put(got, got, xkp_s.at[level, 1], xkp_r.at[level, 1], keep=False, col=partner).start()

    def settle_picked(level):
        for q, chip in enumerate((zhalf, 1 - zhalf)):
            got = quarter(level, 1 - sides[level], 1 - core, chip)
            put(got, got, xkp_s.at[level, q], xkp_r.at[level, q], keep=False, col=partner).wait_recv()

    def drain_picked(level):
        got = quarter(level, 1 - sides[level], core, zhalf)
        put(got, got, xk_s.at[level, 1], xk_r.at[level, 1], keep=False, col=zmate).wait_send()
        for q in range(2):
            put(got, got, xkp_s.at[level, q], xkp_r.at[level, q], keep=False, col=partner).wait_send()

    def hear(level):
        got = sp[level].at[1 - sides[level]]
        put(got, got, xs_s.at[level], xs_r.at[level], keep=False, leaf=siblings[level]).wait_recv()

    def drain_relay(buf, level, chunks, s2, rv2):
        for q, piece in enumerate(pieces(buf, level, 1 - sides[level], chunks, core)):
            put(piece, piece, s2.at[level, q], rv2.at[level, q], keep=False, col=partner).wait_send()

    offer_picked(0)

    side0 = sides[0]
    picked = pk[0][side0]
    raw = mm(res[...], picked, 1, 1)
    raw_ref[...] = raw
    om_own = om_all[me]
    part[...] = 0.25 * exact(raw, om_own, 0, 0)
    r2 = r // 2
    own0 = pl.multiple_of(core * r2, r2)
    other0 = pl.multiple_of((1 - core) * r2, r2)
    pair = put(part.at[pl.ds(other0, r2)], half, pair_s, pair_r, col=partner)
    pair.start()
    ww[0, side0], scale = ridged(mm(picked, picked, 1, 1), rank_ref[leaf])
    scatter = []
    for off in range(1, ZS):
        piece = pl.ds(pl.multiple_of(zpeer(off) * count, count), count)
        scatter.append(put(mine.at[piece], landed.at[off - 1], rs_s.at[off], rs_r.at[off], col=zpeer(off) * 2 + core))

    def leaf_hook(b):
        @pl.when(b == 0)
        def _():
            pair.wait_recv()
            mine[...] = part[pl.ds(own0, r2)] + half[...]
            for copy in scatter:
                copy.start()

        @pl.when(b == 6)
        def _():
            relay_picked(0)

    spd_inverse(ww.at[0, side0], scale, leaf_hook)
    offer(ww, 0, 1, xw_s, xw_r)
    basis_ref[...] = mm(raw_ref[...], ww[0, side0], 1, 0).astype(BF16)

    def n_rows(side, half_of, chip):
        return hh.at[0, side, pl.ds(pl.multiple_of(half_of * r2 + chip * count, count), count)]

    total = mine[pl.ds(pl.multiple_of(z * count, count), count)]
    for off in range(1, ZS):
        scatter[off - 1].wait_recv()
        total = total + landed[off - 1]
    hh[0, side0, pl.ds(pl.multiple_of(own0 + z * count, count), count)] = total
    here = n_rows(side0, core, z)
    for off in (1, 7, 2, 6, 3, 5, 4):
        put(here, here, ag_s.at[off], ag_r.at[ZS - off], col=zpeer(off) * 2 + core).start()
    put(here, here, ap_s.at[0], ap_r.at[0], col=partner).start()
    put(here, here, ax_s.at[0], ax_r.at[0], leaf=siblings[0]).start()
    for off in (1, 7, 2, 6, 3, 5, 4):
        got = n_rows(side0, core, zpeer(off))
        put(got, got, ag_s.at[off], ag_r.at[off], keep=False, col=partner).wait_recv()
        put(got, got, ap_s.at[off], ap_r.at[off], col=partner).start()
        put(got, got, ax_s.at[off], ax_r.at[off], leaf=siblings[0]).start()
    relay_picked_mate(0)
    relay(ww, 0, 1, xw_s, xw_r, xwp_s, xwp_r)
    for off in (0, 1, 7, 2, 6, 3, 5, 4):
        got = n_rows(1 - side0, core, zpeer(off))
        put(got, got, ax_s.at[off], ax_r.at[off], keep=False, leaf=siblings[0]).wait_recv()
        put(got, got, axp_s.at[off], axp_r.at[off], col=partner).start()
    for off in range(ZS):
        got = n_rows(side0, 1 - core, zpeer(off))
        put(got, got, ap_s.at[off], ap_r.at[off], keep=False, col=partner).wait_recv()
    pp[side0] = mm(ww[0, side0], hh[0, side0], 1, 0)
    settle_picked(0)
    hear(0)
    settle(ww, 0, 1, xwp_s, xwp_r)
    for off in range(ZS):
        got = n_rows(1 - side0, 1 - core, zpeer(off))
        put(got, got, axp_s.at[off], axp_r.at[off], keep=False, col=partner).wait_recv()
    pp[1 - side0] = mm(ww[0, 1 - side0], hh[0, 1 - side0], 1, 0)

    row, ranks = node_of(LEVELS, leaf, skel_ref, rank_ref)
    meta[0:1, :] = row
    for i in range(3):
        meta[1 + i : 2 + i, :] = jnp.broadcast_to(ranks[i], (1, r)).astype(jnp.int32)

    for level in range(1, LEVELS):
        side = sides[level]
        row, ranks = node_of(level, leaf, skel_ref, rank_ref)
        cand, spots, chooser, picked = merge(row, ranks, pk[level - 1], pp, sp[level - 1])
        pk[level][side] = picked
        offer_picked(level)
        sp[level][side] = exact(spots, chooser, 1, 0)
        put(sp[level].at[side], sp[level].at[side], xs_s.at[level], xs_r.at[level], leaf=siblings[level]).start()
        raw = mm(cand, picked, 1, 1, 3)
        hh[level, side] = mm(raw, jnp.concatenate([pp[0], pp[1]], 0), 0, 0)
        offer(hh, level, 4, xh_s, xh_r)
        ww[level, side], scale = ridged(mm(picked, picked, 1, 1, 3), ranks[2])

        def hook(b, level=level):
            @pl.when(b == 5)
            def _():
                relay_picked(level)

        spd_inverse(ww.at[level, side], scale, hook)
        offer(ww, level, 1, xw_s, xw_r)
        pp[side] = mm(ww[level, side], hh[level, side], 1, 0)
        relay_picked_mate(level)
        relay(hh, level, 4, xh_s, xh_r, xhp_s, xhp_r)
        relay(ww, level, 1, xw_s, xw_r, xwp_s, xwp_r)
        settle_picked(level)
        hear(level)
        settle(hh, level, 4, xhp_s, xhp_r)
        settle(ww, level, 1, xwp_s, xwp_r)
        pp[1 - side] = mm(ww[level, 1 - side], hh[level, 1 - side], 1, 0)

    for copy in sends:
        copy.wait_send()
    for level in range(LEVELS):
        drain_picked(level)
        drain_relay(ww, level, 1, xwp_s, xwp_r)
        if level > 0:
            drain_relay(hh, level, 4, xhp_s, xhp_r)

    def drain(t, carry):
        same = zpeer(zorder(t)) * 2 + core
        put(block_of(same), block_of(same), gp_s.at[t], gp_r.at[t], keep=False, col=partner).wait_send()
        put(pick_rows(same), pick_rows(same), pp_s.at[t], pp_r.at[t], keep=False, col=partner).wait_send()
        return carry

    lax.fori_loop(1, ZS, drain, 0)


def local(points, point_ids, signs, hadamard_sample_rows, samples, skeleton, ranks):
    rows = points.shape[1]
    width = samples.shape[1]
    r = skeleton.shape[1]
    count = r // COLS
    shape = jax.ShapeDtypeStruct
    fetched = pltpu.VMEM
    inputs = [points, point_ids[None], signs[None], hadamard_sample_rows[None], samples, skeleton, ranks]
    pair_of = [DMA((LEVELS, 2))] * 4
    sems = [
        DMA((7,)), *[DMA((ZS,))] * 8, DMA(()), DMA(()), *[DMA((ZS,))] * 10, *[DMA((LEVELS,))] * 2,
        *pair_of, *[DMA((LEVELS, 4))] * 4, *pair_of,
    ]
    basis, pk, sp, pp, meta = pl.pallas_call(
        hss_kernel,
        out_shape=[
            shape((rows, r), BF16),
            shape((2, r, width), F32),
            shape((2, 8, r), F32),
            shape((2, r, width), F32),
            shape((8, r), jnp.int32),
        ],
        in_specs=[HBM] * 7,
        out_specs=[VM] * 5,
        scratch_shapes=[
            fetched((3, rows), F32),
            fetched((1, rows), jnp.int32),
            fetched((1, rows), jnp.int32),
            fetched((1, width), jnp.int32),
            fetched(skeleton.shape, jnp.int32),
            pltpu.SMEM(ranks.shape, jnp.int32),
            fetched((rows, width), BF16),
            fetched((COLS, 8, rows), F32),
            fetched((COLS, rows, width), BF16),
            fetched((3, rows, LANES), F32),
            fetched((3, r, LANES), F32),
            fetched((rows, width), F32),
            fetched((rows, r), F32),
            fetched((r, width), F32),
            fetched((r // 2, width), F32),
            fetched((r // 2, width), F32),
            fetched((ZS - 1, count, width), F32),
            fetched((r, width), F32),
            fetched((2, 2, r, width), F32),
            fetched((2, 2, 8, r), F32),
            fetched((LEVELS, 2, r, width), F32),
            fetched((LEVELS, 2, r, r), F32),
            *sems,
        ],
        compiler_params=pltpu.CompilerParams(
            collective_id=0, has_side_effects=True, vmem_limit_bytes=32 * 1024 * 1024
        ),
        name="hss",
    )(*[pltpu.with_memory_space_constraint(x, pltpu.HBM) for x in inputs])
    top = shape((r // 8, width // COLS), F32)
    return pl.pallas_call(
        top_kernel,
        out_shape=[shape((rows, r), BF16), top, top],
        in_specs=[VM] * 5,
        out_specs=[ANY, VM, VM],
        scratch_shapes=[
            fetched((r, width), F32),
            fetched((r, r), F32),
            DMA(()),
        ],
        compiler_params=pltpu.CompilerParams(vmem_limit_bytes=32 * 1024 * 1024),
        name="top",
    )(basis, pk, pp, sp, meta)


def solution(mesh):
    placed = (
        P(None, ("leaf", "col")),
        P(("leaf", "col")),
        P(("leaf", "col")),
        P(),
        P(("leaf", "col"), None),
        P(),
        P(),
    )
    return jax.shard_map(
        local,
        mesh=mesh,
        in_specs=placed,
        out_specs=(P(("leaf", "col"), None), P("leaf", "col"), P("leaf", "col")),
        check_vma=False,
    )
```

```python
import jax
import jax.numpy as jnp
from jax import lax
from jax.experimental import pallas as pl
from jax.experimental.pallas import tpu as pltpu
from jax.sharding import PartitionSpec as P

MESH = pl.DeviceIdType.MESH
DMA = pltpu.SemaphoreType.DMA
F32 = jnp.float32
BF16 = jnp.bfloat16
VM = pl.BlockSpec(memory_space=pltpu.VMEM)
SM = pl.BlockSpec(memory_space=pltpu.SMEM)
ANY = pl.BlockSpec(memory_space=pl.ANY)
HBM = pl.BlockSpec(memory_space=pltpu.HBM)

NTOTAL = 1048576
KERNEL_SCALE = 1.0
RIDGE = 0.25
LOG2E = 1.4426950408889634
BITS = NTOTAL.bit_length() - 1
NBITS = 32
PANEL = 16
COLS = 16
ZS = COLS // 2
LANES = 128
LEVELS = 3
FAR_FIRST = (4, 3, 5, 2, 6, 1, 7)


def bdot(a, b, ca, cb):
    return lax.dot_general(a, b, (((ca,), (cb,)), ((), ())), preferred_element_type=F32)


def split(x, count):
    pieces = []
    for _ in range(count - 1):
        piece = x.astype(BF16)
        pieces.append(piece)
        x = x - piece.astype(F32)
    return [*pieces, x.astype(BF16)]


def mm(a, b, ca, cb, terms=6):
    count = 3 if terms == 6 else 2
    pa, pb = split(a, count), split(b, count)
    pairs = [(i, j) for i in range(count) for j in range(count) if i + j < count]
    left = jnp.concatenate([pa[i] for i, _ in pairs], ca)
    right = jnp.concatenate([pb[j] for _, j in pairs], cb)
    return bdot(left, right, ca, cb)


def exact(a, b, ca, cb):
    pieces = split(a, 3)
    return bdot(jnp.concatenate(pieces, ca), jnp.concatenate([b] * 3, cb), ca, cb)


def iota(shape, axis):
    return lax.broadcasted_iota(jnp.int32, shape, axis)


def kern(squared_distance):
    return jnp.exp2(squared_distance * (-KERNEL_SCALE * LOG2E))


def spd_inverse(a_ref, scale, hook):
    n = a_ref.shape[0]
    lane = iota((PANEL, n), 1)
    sub = iota((PANEL, n), 0)
    ident = (lane == sub).astype(F32)
    lane_n = iota((n, n), 1)

    def step(b, carry):
        start = pl.multiple_of(b * PANEL, PANEL)
        panel = a_ref[pl.ds(start, PANEL), :]
        rolled = pltpu.roll(panel, lax.rem(n - start, n), 1)
        diag = [jnp.broadcast_to(rolled[:, k : k + 1], (PANEL, n)) for k in range(PANEL)]
        rows = jnp.where(lane < PANEL, ident, rolled)
        for k in range(0, PANEL, 2):
            one, two = diag[k], diag[k + 1]
            a, c = one[k : k + 1, :], two[k + 1 : k + 2, :]
            low, up = one[k + 1 : k + 2, :], two[k : k + 1, :]
            inv = 1.0 / (a * c - low * up)
            first, second = sub == k, sub == k + 1
            g0 = jnp.where(first, -c, jnp.where(second, low, one * c - two * low))
            g1 = jnp.where(first, up, jnp.where(second, -a, two * a - one * up))

            def sweep(x):
                base = jnp.where(first | second, 0.0, x)
                return base - (g0 * x[k : k + 1, :] + g1 * x[k + 1 : k + 2, :]) * inv

            for j in range(k + 2, PANEL):
                diag[j] = sweep(diag[j])
            rows = sweep(rows)
        rows = pltpu.roll(rows, start, 1)
        side = jnp.where(lane < start, -panel, panel)
        side = jnp.where((lane >= start) & (lane < start + PANEL), 0.0, side)
        change = mm(side, rows, 0, 0)
        cleared = jnp.where((lane_n >= start) & (lane_n < start + PANEL), 0.0, a_ref[...])
        a_ref[...] = cleared - change
        a_ref[pl.ds(start, PANEL), :] = rows
        hook(b)
        return carry

    lax.fori_loop(0, n // PANEL, step, 0)
    a_ref[...] = a_ref[...] * scale


def ridged(gram, rank):
    n = gram.shape[0]
    same = iota((n, n), 0) == iota((n, n), 1)
    trace = jnp.sum(jnp.where(same, gram, 0.0), keepdims=True)
    shift = RIDGE * trace / rank.astype(F32) + 1e-06
    scale = 1.0 / shift
    return gram * scale + jnp.where(same, 1.0, 0.0), scale


def unit8():
    return (iota((8, LANES), 0) == iota((8, LANES), 1)).astype(BF16)


def node_of(level, leaf, skel_ref, rank_ref):
    leaves = lax.axis_size("leaf")
    child_base = sum(leaves >> k for k in range(level - 1))
    base = child_base + (leaves >> (level - 1))
    node = leaf // (1 << level)
    ranks = (rank_ref[child_base + 2 * node], rank_ref[child_base + 2 * node + 1], rank_ref[base + node])
    return skel_ref[pl.ds(base + node, 1), :], ranks


def merge(row, ranks, pk, pp, sp):
    rank_l, rank_r, rank_p = ranks
    r = row.shape[1]
    sub = iota((r, 1), 0)
    spots_l = exact(sp[0], unit8(), 0, 0)
    row_r = sp[1]
    d2 = None
    for axis in range(3):
        off = spots_l[:, axis : axis + 1] - row_r[axis : axis + 1, :]
        d2 = off * off if d2 is None else d2 + off * off
    cross = kern(d2)
    upper = (pk[0] - mm(cross, pp[1], 1, 0, 3)) * jnp.where(sub < rank_l, 1.0, 0.0)
    lower = (pk[1] - mm(cross, pp[0], 0, 0, 3)) * jnp.where(sub < rank_r, 1.0, 0.0)
    cand = jnp.concatenate([upper, lower], 0)
    spots = jnp.concatenate([sp[0], row_r], 1)
    chooser = jnp.where(jnp.broadcast_to(row, (2 * r, r)) == iota((2 * r, r), 0), 1.0, 0.0).astype(BF16)
    chosen = bdot(jnp.concatenate([chooser] * 3, 0), jnp.concatenate(split(cand, 3), 0), 0, 0)
    return cand, spots, chooser, chosen * jnp.where(sub < rank_p, 1.0, 0.0)


def top_kernel(basis_ref, pk, pp, sp, meta, basis_out, top_s, top_o, pk3, ww3, sem):
    save = pltpu.make_async_copy(basis_ref, basis_out, sem)
    save.start()
    leaf = lax.axis_index("leaf")
    me = lax.axis_index("col")
    width = pk.shape[2]
    share, span = top_s.shape
    ranks = [meta[1 + i : 2 + i, 0:1] for i in range(3)]
    cand, _, _, picked = merge(meta[0:1, :], ranks, pk, pp, sp)
    pk3[...] = picked
    raw = mm(cand, picked, 1, 1, 3)
    back = mm(raw, jnp.concatenate([pp[0], pp[1]], 0), 0, 0)
    ww3[...], scale = ridged(mm(picked, picked, 1, 1, 3), ranks[2])
    spd_inverse(ww3, scale, lambda b: None)
    turn = lax.rem(width - me * span, width)
    rows = pl.ds(pl.multiple_of(lax.rem(leaf, 8) * share, share), share)
    top_s[...] = pltpu.roll(pk3[rows, :], turn, 1)[:, 0:span]
    top_o[...] = pltpu.roll(mm(ww3[rows, :], back, 1, 0), turn, 1)[:, 0:span]
    save.wait()


def hss_kernel(
    points_hbm, ids_hbm, signs_hbm, had_hbm, samp_hbm, skel_hbm, rank_hbm,
    basis_ref, pk_out, sp_out, pp, meta,
    points_ref, ids_ref, signs_ref, had_ref, skel_ref, rank_ref, samp, every, om_all, own_b, pick_b, res, raw_ref, part, half, mine, landed, spk, pk_low, sp_low, hh, ww,
    samp_sem, g_s, g_r, gp_s, gp_r, p_s, p_r, pp_s, pp_r,
    pair_s, pair_r, rs_s, rs_r, ag_s, ag_r, ap_s, ap_r, ax_s, ax_r, axp_s, axp_r,
    xs_s, xs_r, xk_s, xk_r, xkp_s, xkp_r, xh_s, xh_r, xhp_s, xhp_r, xw_s, xw_r, xwp_s, xwp_r,
):
    leaf = lax.axis_index("leaf")
    me = lax.axis_index("col")
    leaves = lax.axis_size("leaf")
    core = lax.rem(me, 2)
    z = me // 2
    partner = me + 1 - 2 * core
    rows = points_ref.shape[1]
    width = had_ref.shape[1]
    r = skel_ref.shape[1]
    count = r // COLS
    pk = [pk_low.at[0], pk_low.at[1], pk_out]
    sp = [sp_low.at[0], sp_low.at[1], sp_out]
    zhalf = lax.rem(z, 2)
    zmate = (z + 1 - 2 * zhalf) * 2 + core
    sides = [lax.rem(leaf // (1 << lvl), 2) for lvl in range(LEVELS)]
    siblings = [leaf + (1 << lvl) - (2 << lvl) * sides[lvl] for lvl in range(LEVELS)]
    sends = []

    def put(src, dst, send, recv, keep=True, **device):
        copy = pltpu.make_async_remote_copy(
            src_ref=src, dst_ref=dst, send_sem=send, recv_sem=recv, device_id=device, device_id_type=MESH
        )
        if keep:
            sends.append(copy)
        return copy

    def zpeer(off):
        return lax.rem(z + off, ZS)

    fetches = [
        pltpu.make_async_copy(source, target, samp_sem.at[i])
        for i, (source, target) in enumerate(
            (
                (points_hbm, points_ref),
                (ids_hbm, ids_ref),
                (signs_hbm, signs_ref),
                (skel_hbm, skel_ref),
                (rank_hbm, rank_ref),
                (had_hbm, had_ref),
                (samp_hbm, samp),
            )
        )
    ]
    for fetch in fetches:
        fetch.start()
    barrier = pltpu.get_barrier_semaphore()
    for off in range(1, ZS):
        pl.semaphore_signal(barrier, inc=1, device_id={"col": zpeer(off) * 2 + core}, device_id_type=MESH)
    pl.semaphore_signal(barrier, inc=1, device_id={"col": partner}, device_id_type=MESH)
    for sibling in siblings:
        pl.semaphore_signal(barrier, inc=1, device_id={"leaf": sibling}, device_id_type=MESH)
    for fetch in fetches:
        fetch.wait()
    every[me, 0:3, :] = points_ref[...]
    every[me, 3:4, :] = ids_ref[...].astype(F32)
    every[me, 4:5, :] = signs_ref[...].astype(F32)
    every[:, 5:8, :] = jnp.zeros((COLS, 3, rows), F32)

    my_rows = pl.ds(pl.multiple_of(me * count, count), count)
    entry = skel_ref[pl.ds(leaf, 1), :]

    def chooser_of(slot):
        return jnp.where(
            jnp.broadcast_to(entry - slot * rows, (rows, r)) == iota((rows, r), 0), 1.0, 0.0
        ).astype(BF16)

    part[...] = bdot(chooser_of(me), samp[...], 0, 0)
    spk[my_rows, :] = part[my_rows, :]

    ident = unit8()
    own_cols = exact(every[me], ident, 0, 0)
    for axis in range(3):
        own_b[axis] = jnp.broadcast_to(own_cols[:, axis : axis + 1], (rows, LANES))
    bit_row = iota((NBITS, width), 0)
    had = jnp.broadcast_to(had_ref[...], (NBITS, width))
    had_bits = ((had >> jnp.minimum(bit_row, BITS)) & 1).astype(F32) * 0.5
    had_bits = jnp.where(bit_row == BITS, 0.5, jnp.where(bit_row == BITS + 1, 0.25, had_bits))
    had_bits = jnp.where(bit_row > BITS + 1, 0.0, had_bits).astype(BF16)
    res[...] = samp[...].astype(F32)
    pl.semaphore_wait(barrier, ZS + LEVELS)

    def pick_rows(slot):
        return spk.at[pl.ds(pl.multiple_of(slot * count, count), count)]

    def block_of(slot):
        return every.at[slot, pl.ds(0, 5)]

    order = (1, 7, 2, 6, 3, 5, 4)
    for off in order:
        put(block_of(me), block_of(me), g_s.at[off], g_r.at[ZS - off], col=zpeer(off) * 2 + core).start()
    put(block_of(me), block_of(me), gp_s.at[0], gp_r.at[0], col=partner).start()
    for off in order:
        put(pick_rows(me), pick_rows(me), p_s.at[off], p_r.at[ZS - off], col=zpeer(off) * 2 + core).start()
    put(pick_rows(me), pick_rows(me), pp_s.at[0], pp_r.at[0], col=partner).start()

    def omega4(block):
        shift = iota((NBITS, rows), 0)
        ids = jnp.broadcast_to(block[3:4, :].astype(jnp.int32), (NBITS, rows))
        bits = ((ids >> jnp.minimum(shift, BITS)) & 1).astype(F32)
        bits = jnp.where(shift == BITS, 1.0 - block[4:5, :], bits)
        bits = jnp.where(shift == BITS + 1, 1.0, bits)
        bits = jnp.where(shift > BITS + 1, 0.0, bits).astype(BF16)
        halves = bdot(bits, had_bits, 0, 0)
        return (halves - jnp.round(halves)).astype(BF16)

    def zorder(t):
        return lax.rem(jnp.where(lax.rem(t, 2) == 1, (t + 1) // 2, ZS - t // 2), ZS)

    def tile_of(columns, block):
        tiles = []
        for c in range(rows // LANES):
            d2 = None
            for axis in range(3):
                off = columns[axis] - block[axis : axis + 1, c * LANES : (c + 1) * LANES]
                d2 = off * off if d2 is None else d2 + off * off
            tiles.append(kern(d2).astype(BF16))
        return jnp.concatenate(tiles, 1)

    def near_step(t, spots):
        off = zorder(t)
        there = zpeer(off)
        same = there * 2 + core
        other = there * 2 + 1 - core

        @pl.when(t > 0)
        def _():
            put(block_of(same), block_of(same), g_s.at[off], g_r.at[off], keep=False, col=partner).wait_recv()
            put(block_of(same), block_of(same), gp_s.at[t], gp_r.at[t], keep=False, col=partner).start()

        put(block_of(other), block_of(other), gp_s.at[t], gp_r.at[t], keep=False, col=partner).wait_recv()
        columns = [own_b[axis] for axis in range(3)]
        tiles, omegas = [], []
        for k in range(2):
            block = every[there * 2 + k]
            spots = spots + exact(block, chooser_of(there * 2 + k), 1, 0)
            om = omega4(block)
            om_all[there * 2 + k] = om
            omegas.append(om)
            tiles.append(tile_of(columns, block))
        res[...] -= 0.25 * bdot(jnp.concatenate(tiles, 1), jnp.concatenate(omegas, 0), 1, 0)

        return spots

    spots = lax.fori_loop(0, ZS, near_step, jnp.zeros((8, r), F32))
    sp[0][sides[0]] = spots
    put(sp[0].at[sides[0]], sp[0].at[sides[0]], xs_s.at[0], xs_r.at[0], leaf=siblings[0]).start()

    spot_cols = exact(spots, ident, 0, 0)
    for axis in range(3):
        pick_b[axis] = jnp.broadcast_to(spot_cols[:, axis : axis + 1], (r, LANES))
    part[...] = jnp.zeros((r, width), F32)

    def pick_relay(t, carry):
        off = zorder(t)
        same = zpeer(off) * 2 + core
        put(pick_rows(same), pick_rows(same), p_s.at[off], p_r.at[off], keep=False, col=partner).wait_recv()
        put(pick_rows(same), pick_rows(same), pp_s.at[t], pp_r.at[t], keep=False, col=partner).start()
        return carry

    lax.fori_loop(1, ZS, pick_relay, 0)

    def pick_step(t, carry):
        there = zpeer(zorder(t))
        columns = [pick_b[axis] for axis in range(3)]
        tile = jnp.concatenate([tile_of(columns, every[there * 2 + k]) for k in range(2)], 1)
        part[...] += bdot(tile, om_all[pl.ds(there * 2, 2)].reshape(2 * rows, width), 1, 0)
        return carry

    lax.fori_loop(0, ZS, pick_step, 0)

    def pick_settle(t, carry):
        other = zpeer(zorder(t)) * 2 + 1 - core
        put(pick_rows(other), pick_rows(other), pp_s.at[t], pp_r.at[t], keep=False, col=partner).wait_recv()
        return carry

    lax.fori_loop(0, ZS, pick_settle, 0)
    sub = iota((r, 1), 0)
    pk[0][sides[0]] = (spk[...] - 0.25 * part[...]) * jnp.where(sub < rank_ref[leaf], 1.0, 0.0)

    def pieces(buf, level, side, chunks, half_of):
        size = r // 2 // chunks
        return [buf.at[level, side, pl.ds(pl.multiple_of(half_of * (r // 2) + q * size, size), size)] for q in range(chunks)]

    def offer(buf, level, chunks, s, rv):
        for q, piece in enumerate(pieces(buf, level, sides[level], chunks, core)):
            put(piece, piece, s.at[level, q], rv.at[level, q], leaf=siblings[level]).start()

    def relay(buf, level, chunks, s, rv, s2, rv2):
        for q, piece in enumerate(pieces(buf, level, 1 - sides[level], chunks, core)):
            put(piece, piece, s.at[level, q], rv.at[level, q], keep=False, leaf=siblings[level]).wait_recv()
            put(piece, piece, s2.at[level, q], rv2.at[level, q], keep=False, col=partner).start()

    def settle(buf, level, chunks, s2, rv2):
        for q, piece in enumerate(pieces(buf, level, 1 - sides[level], chunks, 1 - core)):
            put(piece, piece, s2.at[level, q], rv2.at[level, q], keep=False, col=partner).wait_recv()

    def quarter(level, side, half_of, chip):
        size = r // 4
        return pk[level].at[side, pl.ds(pl.multiple_of((half_of * 2 + chip) * size, size), size)]

    def offer_picked(level):
        piece = quarter(level, sides[level], core, zhalf)
        put(piece, piece, xk_s.at[level, 0], xk_r.at[level, 0], leaf=siblings[level]).start()

    def relay_picked(level):
        got = quarter(level, 1 - sides[level], core, zhalf)
        put(got, got, xk_s.at[level, 0], xk_r.at[level, 0], keep=False, leaf=siblings[level]).wait_recv()
        put(got, got, xk_s.at[level, 1], xk_r.at[level, 1], keep=False, col=zmate).start()
        put(got, got, xkp_s.at[level, 0], xkp_r.at[level, 0], keep=False, col=partner).start()

    def relay_picked_mate(level):
        got = quarter(level, 1 - sides[level], core, 1 - zhalf)
        put(got, got, xk_s.at[level, 1], xk_r.at[level, 1], keep=False, col=zmate).wait_recv()
        put(got, got, xkp_s.at[level, 1], xkp_r.at[level, 1], keep=False, col=partner).start()

    def settle_picked(level):
        for q, chip in enumerate((zhalf, 1 - zhalf)):
            got = quarter(level, 1 - sides[level], 1 - core, chip)
            put(got, got, xkp_s.at[level, q], xkp_r.at[level, q], keep=False, col=partner).wait_recv()

    def drain_picked(level):
        got = quarter(level, 1 - sides[level], core, zhalf)
        put(got, got, xk_s.at[level, 1], xk_r.at[level, 1], keep=False, col=zmate).wait_send()
        for q in range(2):
            put(got, got, xkp_s.at[level, q], xkp_r.at[level, q], keep=False, col=partner).wait_send()

    def hear(level):
        got = sp[level].at[1 - sides[level]]
        put(got, got, xs_s.at[level], xs_r.at[level], keep=False, leaf=siblings[level]).wait_recv()

    def drain_relay(buf, level, chunks, s2, rv2):
        for q, piece in enumerate(pieces(buf, level, 1 - sides[level], chunks, core)):
            put(piece, piece, s2.at[level, q], rv2.at[level, q], keep=False, col=partner).wait_send()

    offer_picked(0)

    side0 = sides[0]
    picked = pk[0][side0]
    raw = mm(res[...], picked, 1, 1)
    raw_ref[...] = raw
    om_own = om_all[me]
    part[...] = 0.25 * exact(raw, om_own, 0, 0)
    r2 = r // 2
    own0 = pl.multiple_of(core * r2, r2)
    other0 = pl.multiple_of((1 - core) * r2, r2)
    pair = put(part.at[pl.ds(other0, r2)], half, pair_s, pair_r, col=partner)
    pair.start()
    ww[0, side0], scale = ridged(mm(picked, picked, 1, 1), rank_ref[leaf])
    scatter = []
    for off in range(1, ZS):
        piece = pl.ds(pl.multiple_of(zpeer(off) * count, count), count)
        scatter.append(put(mine.at[piece], landed.at[off - 1], rs_s.at[off], rs_r.at[off], col=zpeer(off) * 2 + core))

    def leaf_hook(b):
        @pl.when(b == 0)
        def _():
            pair.wait_recv()
            mine[...] = part[pl.ds(own0, r2)] + half[...]
            for off in FAR_FIRST:
                scatter[off - 1].start()

        @pl.when(b == 6)
        def _():
            relay_picked(0)

    spd_inverse(ww.at[0, side0], scale, leaf_hook)
    offer(ww, 0, 1, xw_s, xw_r)
    basis_ref[...] = mm(raw_ref[...], ww[0, side0], 1, 0).astype(BF16)

    def n_rows(side, half_of, chip):
        return hh.at[0, side, pl.ds(pl.multiple_of(half_of * r2 + chip * count, count), count)]

    total = mine[pl.ds(pl.multiple_of(z * count, count), count)]
    for off in range(1, ZS):
        scatter[off - 1].wait_recv()
        total = total + landed[off - 1]
    hh[0, side0, pl.ds(pl.multiple_of(own0 + z * count, count), count)] = total
    here = n_rows(side0, core, z)
    for off in FAR_FIRST:
        put(here, here, ag_s.at[off], ag_r.at[ZS - off], col=zpeer(off) * 2 + core).start()
    put(here, here, ap_s.at[0], ap_r.at[0], col=partner).start()
    put(here, here, ax_s.at[0], ax_r.at[0], leaf=siblings[0]).start()
    for off in (1, 7, 2, 6, 3, 5, 4):
        got = n_rows(side0, core, zpeer(off))
        put(got, got, ag_s.at[off], ag_r.at[off], keep=False, col=partner).wait_recv()
        put(got, got, ap_s.at[off], ap_r.at[off], col=partner).start()
        put(got, got, ax_s.at[off], ax_r.at[off], leaf=siblings[0]).start()
    relay_picked_mate(0)
    relay(ww, 0, 1, xw_s, xw_r, xwp_s, xwp_r)
    for off in (0, 1, 7, 2, 6, 3, 5, 4):
        got = n_rows(1 - side0, core, zpeer(off))
        put(got, got, ax_s.at[off], ax_r.at[off], keep=False, leaf=siblings[0]).wait_recv()
        put(got, got, axp_s.at[off], axp_r.at[off], col=partner).start()
    for off in range(ZS):
        got = n_rows(side0, 1 - core, zpeer(off))
        put(got, got, ap_s.at[off], ap_r.at[off], keep=False, col=partner).wait_recv()
    pp[side0] = mm(ww[0, side0], hh[0, side0], 1, 0)
    settle_picked(0)
    hear(0)
    settle(ww, 0, 1, xwp_s, xwp_r)
    for off in range(ZS):
        got = n_rows(1 - side0, 1 - core, zpeer(off))
        put(got, got, axp_s.at[off], axp_r.at[off], keep=False, col=partner).wait_recv()
    pp[1 - side0] = mm(ww[0, 1 - side0], hh[0, 1 - side0], 1, 0)

    row, ranks = node_of(LEVELS, leaf, skel_ref, rank_ref)
    meta[0:1, :] = row
    for i in range(3):
        meta[1 + i : 2 + i, :] = jnp.broadcast_to(ranks[i], (1, r)).astype(jnp.int32)

    for level in range(1, LEVELS):
        side = sides[level]
        row, ranks = node_of(level, leaf, skel_ref, rank_ref)
        cand, spots, chooser, picked = merge(row, ranks, pk[level - 1], pp, sp[level - 1])
        pk[level][side] = picked
        offer_picked(level)
        sp[level][side] = exact(spots, chooser, 1, 0)
        put(sp[level].at[side], sp[level].at[side], xs_s.at[level], xs_r.at[level], leaf=siblings[level]).start()
        raw = mm(cand, picked, 1, 1, 3)
        hh[level, side] = mm(raw, jnp.concatenate([pp[0], pp[1]], 0), 0, 0)
        offer(hh, level, 4, xh_s, xh_r)
        ww[level, side], scale = ridged(mm(picked, picked, 1, 1, 3), ranks[2])

        def hook(b, level=level):
            @pl.when(b == 5)
            def _():
                relay_picked(level)

        spd_inverse(ww.at[level, side], scale, hook)
        offer(ww, level, 1, xw_s, xw_r)
        pp[side] = mm(ww[level, side], hh[level, side], 1, 0)
        relay_picked_mate(level)
        relay(hh, level, 4, xh_s, xh_r, xhp_s, xhp_r)
        relay(ww, level, 1, xw_s, xw_r, xwp_s, xwp_r)
        settle_picked(level)
        hear(level)
        settle(hh, level, 4, xhp_s, xhp_r)
        settle(ww, level, 1, xwp_s, xwp_r)
        pp[1 - side] = mm(ww[level, 1 - side], hh[level, 1 - side], 1, 0)

    for copy in sends:
        copy.wait_send()
    for level in range(LEVELS):
        drain_picked(level)
        drain_relay(ww, level, 1, xwp_s, xwp_r)
        if level > 0:
            drain_relay(hh, level, 4, xhp_s, xhp_r)

    def drain(t, carry):
        same = zpeer(zorder(t)) * 2 + core
        put(block_of(same), block_of(same), gp_s.at[t], gp_r.at[t], keep=False, col=partner).wait_send()
        put(pick_rows(same), pick_rows(same), pp_s.at[t], pp_r.at[t], keep=False, col=partner).wait_send()
        return carry

    lax.fori_loop(1, ZS, drain, 0)


def local(points, point_ids, signs, hadamard_sample_rows, samples, skeleton, ranks):
    rows = points.shape[1]
    width = samples.shape[1]
    r = skeleton.shape[1]
    count = r // COLS
    shape = jax.ShapeDtypeStruct
    fetched = pltpu.VMEM
    inputs = [points, point_ids[None], signs[None], hadamard_sample_rows[None], samples, skeleton, ranks]
    pair_of = [DMA((LEVELS, 2))] * 4
    sems = [
        DMA((7,)), *[DMA((ZS,))] * 8, DMA(()), DMA(()), *[DMA((ZS,))] * 10, *[DMA((LEVELS,))] * 2,
        *pair_of, *[DMA((LEVELS, 4))] * 4, *pair_of,
    ]
    basis, pk, sp, pp, meta = pl.pallas_call(
        hss_kernel,
        out_shape=[
            shape((rows, r), BF16),
            shape((2, r, width), F32),
            shape((2, 8, r), F32),
            shape((2, r, width), F32),
            shape((8, r), jnp.int32),
        ],
        in_specs=[HBM] * 7,
        out_specs=[VM] * 5,
        scratch_shapes=[
            fetched((3, rows), F32),
            fetched((1, rows), jnp.int32),
            fetched((1, rows), jnp.int32),
            fetched((1, width), jnp.int32),
            fetched(skeleton.shape, jnp.int32),
            pltpu.SMEM(ranks.shape, jnp.int32),
            fetched((rows, width), BF16),
            fetched((COLS, 8, rows), F32),
            fetched((COLS, rows, width), BF16),
            fetched((3, rows, LANES), F32),
            fetched((3, r, LANES), F32),
            fetched((rows, width), F32),
            fetched((rows, r), F32),
            fetched((r, width), F32),
            fetched((r // 2, width), F32),
            fetched((r // 2, width), F32),
            fetched((ZS - 1, count, width), F32),
            fetched((r, width), F32),
            fetched((2, 2, r, width), F32),
            fetched((2, 2, 8, r), F32),
            fetched((LEVELS, 2, r, width), F32),
            fetched((LEVELS, 2, r, r), F32),
            *sems,
        ],
        compiler_params=pltpu.CompilerParams(
            collective_id=0, has_side_effects=True, vmem_limit_bytes=32 * 1024 * 1024
        ),
        name="hss",
    )(*[pltpu.with_memory_space_constraint(x, pltpu.HBM) for x in inputs])
    top = shape((r // 8, width // COLS), F32)
    return pl.pallas_call(
        top_kernel,
        out_shape=[shape((rows, r), BF16), top, top],
        in_specs=[VM] * 5,
        out_specs=[ANY, VM, VM],
        scratch_shapes=[
            fetched((r, width), F32),
            fetched((r, r), F32),
            DMA(()),
        ],
        compiler_params=pltpu.CompilerParams(vmem_limit_bytes=32 * 1024 * 1024),
        name="top",
    )(basis, pk, pp, sp, meta)


def solution(mesh):
    placed = (
        P(None, ("leaf", "col")),
        P(("leaf", "col")),
        P(("leaf", "col")),
        P(),
        P(("leaf", "col"), None),
        P(),
        P(),
    )
    return jax.shard_map(
        local,
        mesh=mesh,
        in_specs=placed,
        out_specs=(P(("leaf", "col"), None), P("leaf", "col"), P("leaf", "col")),
        check_vma=False,
    )
```
